128 devices in a mesh: group: 4 (over x), shard: 32 (over z, y, core).
Axes of the slice: x: 4, y: 4, z: 4, core: 2. Of those that a mesh axis runs over, the one named last changes fastest.
Arguments:
- samples: bfloat16 [16384, 1, 4096], P(('group', 'shard')), may hold values from -6 to 6
- fan_taps: float32 [33, 2048], replicated, may hold values from -1 to 1
- pair_blocks: int32 [512, 2], replicated, may hold values from 0 to 127
- pair_valid: int32 [512], P(('group', 'shard')), may hold values 0 or 1
- coil_offsets: int32 [128], replicated, may hold values from 0 to 63
Outputs:
- correlations: float32 [512, 128, 512], P(('group', 'shard'))
The draws below stay inside these ranges and needn't reach their ends.
Inputs may be any that keep to these rules, and one draw needn't show every extreme that they name: `pair_blocks`: block indices.
All inputs are finite; a program needn't handle non-finite values. No bound on the sum of `pair_valid` on one device may be relied on, other than what follows from the above.
Results may differ from the reference program's by a relative error of at most 0.0076.
Values may be sent and summed in bfloat16 or wider, within the bound.
A program may use at most 192 MiB of HBM per device.

```python
import math
import jax
import jax.numpy as jnp
import numpy as np
from jax import lax

NB = 2048
NT = 4096
BLK = 128
HALF = 16
SMOOTH = 64
NLAG = 512
NSEG = 1
NBLK = 128
NCH = 16384
PAIRS = 512
N_GROUP = 4
N_SHARD = 32


def set_ends(entries, rng, least, largest):
    longest = entries.shape.index(max(entries.shape))
    spots = []
    for shift in (0, 1):
        where = [jax.random.randint(jax.random.fold_in(rng, axis), (), 0, length) for axis, length in enumerate(entries.shape)]
        where[longest] = (where[longest] + shift) % entries.shape[longest]
        spots.append(tuple(where))
    return entries.at[spots[0]].set(least).at[spots[1]].set(largest)


def block_levels(stream_key, dims, shards, smallest, high):
    level, own = 1.0, jax.random.fold_in(stream_key, 6)
    for axis_at, blocks in shards:
        steps = jnp.exp(jax.random.uniform(jax.random.fold_in(own, axis_at), (blocks,), jnp.float32, smallest / len(shards), high / len(shards)))
        level = level * jnp.repeat(steps, dims[axis_at] // blocks).reshape([-1 if axis == axis_at else 1 for axis in range(len(dims))])
    return level


def rank_bounds(count, slope):
    loads = [(1 << 20) // math.isqrt(grade ** slope) + 1 for grade in range(1, count + 1)]
    scale = 1 + sum(loads) // (1 << 30)
    return np.cumsum(np.array([max(1, weight // scale) for weight in loads]))


def ranked_ids(stream_key, extent, number_of, slope):
    listing = rank_bounds(number_of, slope)
    pick = jax.random.randint(jax.random.fold_in(stream_key, 1), extent, 0, int(listing[number_of - 1]))
    standing = jnp.searchsorted(jnp.asarray(listing, jnp.int32), pick, side="right")
    return jax.random.permutation(jax.random.fold_in(stream_key, 2), number_of)[standing].astype(jnp.int32)


def centred(key, dims, deviation, limit, cuts=(), kind=jnp.bfloat16):
    entries = jax.random.normal(key, dims, jnp.float32) * deviation
    if len(cuts) > 0:
        entries = block_levels(key, dims, cuts, -0.22, 0.18) * entries
    return jnp.clip(entries, min=-limit, max=limit).astype(kind)


def setup_inputs(seed: int = 0) -> dict:
    seeds = jax.random.split(jax.random.key(seed), 6)
    return {
        "samples": centred(seeds[0], (NCH, NSEG, NT), 1.0, 6.0, ((0, 128),)),
        "fan_taps": centred(seeds[1], (2 * HALF + 1, NB), (2 * HALF + 1) ** -0.5, 1.0, (), jnp.float32),
        "pair_blocks": set_ends(ranked_ids(seeds[2], (PAIRS, 2), NBLK, 2), jax.random.fold_in(seeds[2], 3), 0, NBLK - 1).astype(jnp.int32),
        "pair_valid": set_ends((jax.random.randint(seeds[3], (PAIRS,), 0, 4) < 3).astype(jnp.int32), jax.random.fold_in(seeds[3], 1), 0, 1),
        "coil_offsets": set_ends(jax.random.randint(seeds[4], (NBLK,), 0, 64), jax.random.fold_in(seeds[4], 1), 0, 63).astype(jnp.int32),
    }


EPSILON = 1e-05

def forward_tables(length, bin_count):
    split = 1 << length.bit_length() // 2
    coarse_n = (jnp.arange(length // split, dtype=jnp.int32) * split)[:, None]
    fine_n = jnp.arange(split, dtype=jnp.int32)[:, None]
    cols_k = jnp.arange(bin_count, dtype=jnp.int32)[None, :]
    coarse_ph = jnp.mod(coarse_n * cols_k, length).astype(jnp.float32) * (2.0 * jnp.pi / length)
    fine_ph = jnp.mod(fine_n * cols_k, length).astype(jnp.float32) * (2.0 * jnp.pi / length)
    cos_a = jnp.cos(coarse_ph)[:, None, :]
    sin_a = jnp.sin(coarse_ph)[:, None, :]
    cos_b = jnp.cos(fine_ph)[None, :, :]
    sin_b = jnp.sin(fine_ph)[None, :, :]
    cosine = (cos_a * cos_b - sin_a * sin_b).reshape(length, bin_count)
    sine_vals = (sin_a * cos_b + cos_a * sin_b).reshape(length, bin_count)
    scaled = 1.0 / jnp.sqrt(jnp.float32(length))
    return (jnp.concatenate([cosine, -sine_vals], axis=1) * scaled).astype(jnp.bfloat16)

def inverse_tables(length, bin_count, lag_count):
    freq_index = jnp.arange(bin_count, dtype=jnp.int32)[:, None]
    lagged = jnp.arange(lag_count, dtype=jnp.int32)[None, :] - lag_count // 2
    phases = jnp.mod(freq_index * lagged, length).astype(jnp.float32) * (2.0 * jnp.pi / length)
    return jnp.stack([jnp.cos(phases), -jnp.sin(phases)]).astype(jnp.bfloat16)

def box_mean(power_sum):
    bin_count = power_sum.shape[1]
    zero_row = jnp.zeros_like(power_sum[:, :1])
    prefix = jnp.concatenate([zero_row, jnp.cumsum(power_sum, axis=1)], axis=1)
    last_row = prefix[:, bin_count:bin_count + 1]
    first_row = prefix[:, 0:1]
    upper_vals = jnp.concatenate([prefix[:, SMOOTH + 1:], jnp.broadcast_to(last_row, (prefix.shape[0], SMOOTH) + prefix.shape[2:])], axis=1)
    lower_vals = jnp.concatenate([jnp.broadcast_to(first_row, (prefix.shape[0], SMOOTH + 1) + prefix.shape[2:]), prefix[:, 1:bin_count - SMOOTH]], axis=1)
    bins_k = jnp.arange(bin_count, dtype=jnp.int32)
    counts = (jnp.minimum(bins_k + SMOOTH, bin_count - 1) - jnp.maximum(bins_k - SMOOTH, 0) + 1).astype(jnp.float32)
    return (upper_vals - lower_vals) / counts[None, :, None]

def whiten(padded, fan_taps):
    width = padded.shape[3] - 2 * HALF
    filtered = jnp.zeros(padded.shape[:3] + (width,), jnp.float32)
    for offset in range(2 * HALF + 1):
        filtered = filtered + fan_taps[offset][None, None, :, None] * padded[:, :, :, offset:offset + width].astype(jnp.float32)
    power_sum = filtered[:, 0] * filtered[:, 0] + filtered[:, 1] * filtered[:, 1]
    mean_power = box_mean(power_sum)
    return (filtered * lax.rsqrt(mean_power + EPSILON)[:, None]).astype(jnp.bfloat16)

def reference(samples, fan_taps, pair_blocks, pair_valid, coil_offsets):
    nblocks = N_GROUP * N_SHARD
    forward = forward_tables(NT, NB).astype(jnp.float32)

    def block_spectra(channel_rows):
        spectra = jnp.einsum('cst,tk->skc', channel_rows.astype(jnp.float32), forward)
        return spectra.astype(jnp.bfloat16).reshape(NSEG, 2, NB, BLK)
    per_block = lax.map(block_spectra, samples.reshape(nblocks, BLK, NSEG, NT))
    whole_line = jnp.moveaxis(per_block, 0, 3).reshape(NSEG, 2, NB, nblocks * BLK)
    padded = jnp.pad(whole_line, ((0, 0), (0, 0), (0, 0), (HALF, HALF)))

    def block_white(index_block):
        window = lax.dynamic_slice_in_dim(padded, index_block * BLK, BLK + 2 * HALF, axis=3)
        return whiten(window, fan_taps)
    whitened = lax.map(block_white, jnp.arange(nblocks, dtype=jnp.int32))
    inverse = inverse_tables(NT, NB, NLAG).astype(jnp.float32)
    bin_index = jnp.arange(NB, dtype=jnp.int32)

    def one_pair(pair_slot):
        first_block = pair_blocks[pair_slot, 0]
        second_block = pair_blocks[pair_slot, 1]
        left_side = whitened[first_block].astype(jnp.float32)
        right_side = jnp.roll(whitened[second_block], -(BLK // 2), axis=3).astype(jnp.float32)
        real_part = lax.optimization_barrier(jnp.sum(left_side[:, 0] * right_side[:, 0] + left_side[:, 1] * right_side[:, 1], axis=0))
        imag_part = lax.optimization_barrier(jnp.sum(left_side[:, 1] * right_side[:, 0] - left_side[:, 0] * right_side[:, 1], axis=0))
        shift_samples = coil_offsets[first_block] - coil_offsets[second_block]
        phases = jnp.mod(bin_index * shift_samples, NT).astype(jnp.float32) * (2.0 * jnp.pi / NT)
        cosine = jnp.cos(phases)[:, None]
        sine_values = jnp.sin(phases)[:, None]
        cross_spec = jnp.stack([real_part * cosine + imag_part * sine_values, imag_part * cosine - real_part * sine_values]).astype(jnp.bfloat16)
        correlation = jnp.einsum('rkc,rkl->cl', cross_spec.astype(jnp.float32), inverse)
        return correlation * (pair_valid[pair_slot].astype(jnp.float32) / jnp.sqrt(jnp.float32(NB * NSEG)))
    return lax.map(one_pair, jnp.arange(PAIRS, dtype=jnp.int32))
```

```python
import functools
import math

import jax
import jax.numpy as jnp
import ml_dtypes
import numpy as np
from jax import lax
from jax.experimental import pallas as pl
from jax.experimental.pallas import tpu as pltpu
from jax.sharding import PartitionSpec as P

HALF = 16
NLAG = 512
NT = 4096
NB = 2048
BLK = 128
WIDE = BLK + 2 * HALF
EPSILON = 1e-05
AXES = ("group", "shard")
NDEV = 128
TAPS = 2 * HALF + 1
QT = 16


def residues():
    low = np.arange(QT)
    high = np.where(low == 0, 16, 32 - low)
    return low, high


def tile_bins():
    low, high = residues()
    k2 = np.arange(64)
    return np.concatenate([low[:, None] + 32 * k2, high[:, None] + 32 * k2], axis=1)


def second_stage_table():
    bins = tile_bins()
    b = np.arange(128)
    phase = 2 * np.pi * ((b[None, :, None] * bins[:, None, :]) % NT) / NT
    cos, sin = np.cos(phase), np.sin(phase)
    table = np.zeros((QT, 2, 128, 2, 128))
    conj = np.concatenate([np.ones(64), -np.ones(64)])
    table[:, 0, :, 0] = cos
    table[:, 1, :, 0] = sin * conj
    table[:, 0, :, 1] = -sin
    table[:, 1, :, 1] = cos * conj
    table[0] = 0.0
    table[0, 0, :, 0, :64] = cos[0, :, :64]
    table[0, 0, :, 1, :64] = -sin[0, :, :64]
    table[0, 1, :, 0, 64:] = cos[0, :, 64:]
    table[0, 1, :, 1, 64:] = -sin[0, :, 64:]
    return (table.reshape(QT, 256, 256) / math.sqrt(NT)).astype(ml_dtypes.bfloat16)


def inverse_table():
    bins = tile_bins().reshape(NDEV, 16)
    lags = np.arange(NLAG) - NLAG // 2
    phase = 2 * np.pi * ((bins[:, :, None] * lags) % NT) / NT
    return np.stack([np.cos(phase), -np.sin(phase)], axis=1).astype(ml_dtypes.bfloat16)


def real_fft(rows):
    count = len(rows)
    if count == 2:
        return [(rows[0] + rows[1], None), (rows[0] - rows[1], None)]
    even = real_fft(rows[0::2])
    odd = real_fft(rows[1::2])
    half, quarter = count // 2, count // 4
    out = [None] * (half + 1)
    out[0] = (even[0][0] + odd[0][0], None)
    out[half] = (even[0][0] - odd[0][0], None)
    out[quarter] = (even[quarter][0], -odd[quarter][0])
    for k in range(1, quarter):
        wr, wi = math.cos(2 * math.pi * k / count), -math.sin(2 * math.pi * k / count)
        o_re, o_im = odd[k]
        e_re, e_im = even[k]
        t_re = o_re * wr - o_im * wi
        t_im = o_re * wi + o_im * wr
        out[k] = (e_re + t_re, e_im + t_im)
        out[half - k] = (e_re - t_re, t_im - e_im)
    return out


def white_kernel(x_ref, table_ref, taps_ref, offsets_ref, out_ref, y_ref, spec_ref, filt_ref, run_ref, rows_ref):
    me = lax.axis_index("group") * lax.axis_size("shard") + lax.axis_index("shard")

    lane = lax.broadcasted_iota(jnp.int32, (QT, 128), 1)
    tile = lax.broadcasted_iota(jnp.int32, (QT, 128), 0)
    residue = jnp.where(lane < 64, tile, jnp.where(tile == 0, 16, 32 - tile))
    bins = residue + 32 * (lane & 63)
    theta = ((bins * offsets_ref[me]) & (NT - 1)).astype(jnp.float32) * (2.0 * math.pi / NT)
    rows_ref[0] = jnp.cos(theta)
    rows_ref[1] = jnp.sin(theta)
    count = jnp.minimum(bins + 64, NB - 1) - jnp.maximum(bins - 64, 0) + 1
    rows_ref[2] = 1.0 / count.astype(jnp.float32)

    @pl.loop(0, WIDE // 16)
    def _(chunk):
        at = pl.ds(pl.multiple_of(chunk * 16, 16), 16)
        rows = [x_ref[at, a * 128 : (a + 1) * 128].astype(jnp.float32) for a in range(32)]
        freq = real_fft(rows)
        for q in range(QT):
            first = freq[q][0]
            second = freq[16][0] if q == 0 else freq[q][1]
            y_ref[q, at, 0:128] = first.astype(jnp.bfloat16)
            y_ref[q, at, 128:256] = second.astype(jnp.bfloat16)

    @pl.loop(0, QT)
    def _(q):
        both = jnp.dot(y_ref[q], table_ref[q], preferred_element_type=jnp.float32)
        spec_ref[q, 0] = both[:, :128]
        spec_ref[q, 1] = both[:, 128:]

    run_ref[...] = jnp.zeros_like(run_ref)

    @pl.loop(0, QT)
    def _(q):
        def tap_step(t, sums):
            re, im = sums
            tap = taps_ref[q, pl.ds(t, 1), :]
            re = re + tap * spec_ref[q, 0, pl.ds(t, BLK), :]
            im = im + tap * spec_ref[q, 1, pl.ds(t, BLK), :]
            return re, im

        zero = jnp.zeros((BLK, 128), jnp.float32)
        re, im = lax.fori_loop(0, TAPS, tap_step, (zero, zero), unroll=3)
        filt_ref[q, 0] = re
        filt_ref[q, 1] = im
        run_ref[0] += re * re + im * im

    lanes = lax.broadcasted_iota(jnp.int32, (BLK, 128), 1)
    low = lanes < 64
    k2 = lanes & 63
    sums = run_ref[0]
    swapped = pltpu.roll(sums, 64, 1)
    total = sums + swapped
    run_ref[1] = total
    run_ref[2] = (
        total
        + jnp.where(k2 >= 1, pltpu.roll(total, 1, 1), 0.0)
        + jnp.where(k2 <= 62, pltpu.roll(total, 127, 1), 0.0)
    )

    def finish(q, re, im, prefix, suffix):
        window = (
            run_ref[2]
            + jnp.where(k2 >= 2, pltpu.roll(suffix, 2, 1), 0.0)
            + jnp.where(k2 <= 61, pltpu.roll(prefix, 126, 1), 0.0)
        )
        scale = lax.rsqrt(window * rows_ref[2, pl.ds(q, 1), :] + EPSILON)
        cos = rows_ref[0, pl.ds(q, 1), :]
        sin = rows_ref[1, pl.ds(q, 1), :]
        white_re = ((re * cos + im * sin) * scale).astype(jnp.bfloat16).T
        white_im = ((im * cos - re * sin) * scale).astype(jnp.bfloat16).T
        bands = pl.ds(q * 8, 8)
        out_ref[bands, 0] = white_re.reshape(8, 16, 128)
        out_ref[bands, 1] = white_im.reshape(8, 16, 128)

    re, im = filt_ref[0, 0], filt_ref[0, 1]
    power = re * re + im * im
    finish(0, re, im, jnp.where(low, power, swapped + power), jnp.where(low, total, sums))
    run_ref[0] = jnp.where(low, power, 0.0)

    @pl.loop(1, QT)
    def _(q):
        re, im = filt_ref[q, 0], filt_ref[q, 1]
        before = run_ref[0]
        upto = before + (re * re + im * im)
        rest = jnp.maximum(run_ref[1] - before, 0.0)
        run_ref[0] = upto
        finish(q, re, im, jnp.where(low, upto, rest), jnp.where(low, rest, upto))


def whiten_block(wide, table, taps, offsets):
    return pl.pallas_call(
        white_kernel,
        out_shape=jax.ShapeDtypeStruct((NDEV, 2, 16, BLK), jnp.bfloat16),
        in_specs=[
            pl.BlockSpec(memory_space=pltpu.VMEM),
            pl.BlockSpec(memory_space=pltpu.VMEM),
            pl.BlockSpec(memory_space=pltpu.VMEM),
            pl.BlockSpec(memory_space=pltpu.SMEM),
        ],
        out_specs=pl.BlockSpec(memory_space=pltpu.VMEM),
        scratch_shapes=[
            pltpu.VMEM((QT, WIDE, 256), jnp.bfloat16),
            pltpu.VMEM((QT, 2, WIDE, 128), jnp.float32),
            pltpu.VMEM((QT, 2, BLK, 128), jnp.float32),
            pltpu.VMEM((3, BLK, 128), jnp.float32),
            pltpu.VMEM((3, QT, 128), jnp.float32),
        ],
        compiler_params=pltpu.CompilerParams(vmem_limit_bytes=40 << 20),
        name="whiten_block",
    )(wide, table, taps, offsets)


def cross_kernel(step, pairs_ref, bands_ref, out_ref, rolled_ref):
    i = pl.program_id(0)

    @pl.when(i == 0)
    def _():
        @pl.loop(0, NDEV)
        def _(block):
            both = bands_ref[block].astype(jnp.float32).reshape(32, 128)
            rolled_ref[block] = pltpu.roll(both, 64, 1).astype(jnp.bfloat16).reshape(2, 16, 128)

    @pl.loop(0, step, unroll=4)
    def _(p):
        a = pairs_ref[2 * (i * step + p)]
        b = pairs_ref[2 * (i * step + p) + 1]
        left = bands_ref[a].astype(jnp.float32)
        right = rolled_ref[b].astype(jnp.float32)
        out_ref[p, 0] = (left[0] * right[0] + left[1] * right[1]).astype(jnp.bfloat16)
        out_ref[p, 1] = (left[1] * right[0] - left[0] * right[1]).astype(jnp.bfloat16)


def cross_products(pairs, bands):
    count = pairs.shape[0] // 2
    step = count // 8
    return pl.pallas_call(
        functools.partial(cross_kernel, step),
        out_shape=jax.ShapeDtypeStruct((count, 2, 16, BLK), jnp.bfloat16),
        grid_spec=pltpu.PrefetchScalarGridSpec(
            num_scalar_prefetch=1,
            grid=(8,),
            in_specs=[pl.BlockSpec((NDEV, 2, 16, BLK), lambda i, *_: (0, 0, 0, 0))],
            out_specs=pl.BlockSpec((step, 2, 16, BLK), lambda i, *_: (i, 0, 0, 0)),
            scratch_shapes=[pltpu.VMEM((NDEV, 2, 16, BLK), jnp.bfloat16)],
        ),
        compiler_params=pltpu.CompilerParams(vmem_limit_bytes=24 << 20),
        name="cross_products",
    )(pairs, bands)


def lag_kernel(valid_ref, cross_ref, table_ref, out_ref):
    i = pl.program_id(0)
    table = table_ref[...].reshape(256, NLAG)
    for p in range(4):
        piece = cross_ref[:, p].reshape(256, BLK)
        part = lax.dot_general(piece, table, (((0,), (0,)), ((), ())), preferred_element_type=jnp.float32)

        @pl.when(i == 0)
        def _():
            out_ref[p] = part

        @pl.when(i > 0)
        def _():
            out_ref[p] += part

    @pl.when(i == pl.num_programs(0) - 1)
    def _():
        for p in range(4):
            out_ref[p] = out_ref[p] * (valid_ref[p].astype(jnp.float32) * (1.0 / math.sqrt(NB)))


def lag_sums(valid, owned, table):
    return pl.pallas_call(
        lag_kernel,
        out_shape=jax.ShapeDtypeStruct((4, BLK, NLAG), jnp.float32),
        grid_spec=pltpu.PrefetchScalarGridSpec(
            num_scalar_prefetch=1,
            grid=(16,),
            in_specs=[
                pl.BlockSpec((8, 4, 2, 16, BLK), lambda i, *_: (i, 0, 0, 0, 0)),
                pl.BlockSpec((8, 2, 16, NLAG), lambda i, *_: (i, 0, 0, 0)),
            ],
            out_specs=pl.BlockSpec((4, BLK, NLAG), lambda i, *_: (0, 0, 0)),
        ),
        compiler_params=pltpu.CompilerParams(vmem_limit_bytes=24 << 20),
        name="lag_sums",
    )(valid, owned, table)


def body(samples, fan_taps, pair_blocks, pair_valid, coil_offsets):
    x = samples.reshape(BLK, NT)
    before = lax.ppermute(x[BLK - HALF :], AXES, [(i, i + 1) for i in range(NDEV - 1)])
    after = lax.ppermute(x[:HALF], AXES, [(i + 1, i) for i in range(NDEV - 1)])
    wide = jnp.concatenate([before, x, after], axis=0)
    by_residue = fan_taps.reshape(TAPS, 64, 32).transpose(2, 0, 1)
    low, high = by_residue[:QT], jnp.concatenate([by_residue[QT : QT + 1], by_residue[:QT:-1]], axis=0)
    taps = jnp.concatenate([low, high], axis=2)
    white = whiten_block(wide, jnp.asarray(second_stage_table()), taps, coil_offsets)
    bands = lax.all_to_all(white, AXES, split_axis=0, concat_axis=0, tiled=True)
    cross = cross_products(pair_blocks.reshape(-1), bands)
    owned = lax.all_to_all(cross.reshape(NDEV, 4, 2, 16, BLK), AXES, split_axis=0, concat_axis=0, tiled=True)
    return lag_sums(pair_valid, owned, jnp.asarray(inverse_table()))


def solution(mesh):
    return jax.shard_map(
        body,
        mesh=mesh,
        in_specs=(P(AXES, None, None), P(), P(), P(AXES), P()),
        out_specs=P(AXES, None, None),
        check_vma=False,
    )
```

```python
import math

import jax
import jax.numpy as jnp
import ml_dtypes
import numpy as np
from jax import lax
from jax.experimental import pallas as pl
from jax.experimental.pallas import tpu as pltpu
from jax.sharding import PartitionSpec as P

HALF = 16
NLAG = 512
NT = 4096
NB = 2048
BLK = 128
WIDE = BLK + 2 * HALF
EPSILON = 1e-05
AXES = ("group", "shard")
NDEV = 128
MESH = pl.DeviceIdType.MESH
TAPS = 2 * HALF + 1
QT = 16


def residues():
    low = np.arange(QT)
    high = np.where(low == 0, 16, 32 - low)
    return low, high


def tile_bins():
    low, high = residues()
    k2 = np.arange(64)
    return np.concatenate([low[:, None] + 32 * k2, high[:, None] + 32 * k2], axis=1)


def second_stage_table():
    bins = tile_bins()
    b = np.arange(128)
    phase = 2 * np.pi * ((b[None, :, None] * bins[:, None, :]) % NT) / NT
    cos, sin = np.cos(phase), np.sin(phase)
    table = np.zeros((QT, 2, 128, 2, 128))
    conj = np.concatenate([np.ones(64), -np.ones(64)])
    table[:, 0, :, 0] = cos
    table[:, 1, :, 0] = sin * conj
    table[:, 0, :, 1] = -sin
    table[:, 1, :, 1] = cos * conj
    table[0] = 0.0
    table[0, 0, :, 0, :64] = cos[0, :, :64]
    table[0, 0, :, 1, :64] = -sin[0, :, :64]
    table[0, 1, :, 0, 64:] = cos[0, :, 64:]
    table[0, 1, :, 1, 64:] = -sin[0, :, 64:]
    return (table.reshape(QT, 256, 256) / math.sqrt(NT)).astype(ml_dtypes.bfloat16)


def real_fft(rows):
    count = len(rows)
    if count == 2:
        return [(rows[0] + rows[1], None), (rows[0] - rows[1], None)]
    even = real_fft(rows[0::2])
    odd = real_fft(rows[1::2])
    half, quarter = count // 2, count // 4
    out = [None] * (half + 1)
    out[0] = (even[0][0] + odd[0][0], None)
    out[half] = (even[0][0] - odd[0][0], None)
    out[quarter] = (even[quarter][0], -odd[quarter][0])
    for k in range(1, quarter):
        wr, wi = math.cos(2 * math.pi * k / count), -math.sin(2 * math.pi * k / count)
        o_re, o_im = odd[k]
        e_re, e_im = even[k]
        t_re = o_re * wr - o_im * wi
        t_im = o_re * wi + o_im * wr
        out[k] = (e_re + t_re, e_im + t_im)
        out[half - k] = (e_re - t_re, t_im - e_im)
    return out


def white_kernel(x_ref, table_ref, taps_ref, offsets_ref, out_ref, y_ref, spec_ref, filt_ref, run_ref, rows_ref):
    me = lax.axis_index("group") * lax.axis_size("shard") + lax.axis_index("shard")

    lane = lax.broadcasted_iota(jnp.int32, (QT, 128), 1)
    tile = lax.broadcasted_iota(jnp.int32, (QT, 128), 0)
    residue = jnp.where(lane < 64, tile, jnp.where(tile == 0, 16, 32 - tile))
    bins = residue + 32 * (lane & 63)
    theta = ((bins * offsets_ref[me]) & (NT - 1)).astype(jnp.float32) * (2.0 * math.pi / NT)
    rows_ref[0] = jnp.cos(theta)
    rows_ref[1] = jnp.sin(theta)
    count = jnp.minimum(bins + 64, NB - 1) - jnp.maximum(bins - 64, 0) + 1
    rows_ref[2] = 1.0 / count.astype(jnp.float32)

    @pl.loop(0, WIDE // 16)
    def _(chunk):
        at = pl.ds(pl.multiple_of(chunk * 16, 16), 16)
        rows = [x_ref[at, a * 128 : (a + 1) * 128].astype(jnp.float32) for a in range(32)]
        freq = real_fft(rows)
        for q in range(QT):
            first = freq[q][0]
            second = freq[16][0] if q == 0 else freq[q][1]
            y_ref[q, at, 0:128] = first.astype(jnp.bfloat16)
            y_ref[q, at, 128:256] = second.astype(jnp.bfloat16)

    @pl.loop(0, QT)
    def _(q):
        both = jnp.dot(y_ref[q], table_ref[q], preferred_element_type=jnp.float32)
        spec_ref[q, 0] = both[:, :128]
        spec_ref[q, 1] = both[:, 128:]

    run_ref[...] = jnp.zeros_like(run_ref)

    @pl.loop(0, QT)
    def _(q):
        def tap_step(t, sums):
            re, im = sums
            tap = taps_ref[q, pl.ds(t, 1), :]
            re = re + tap * spec_ref[q, 0, pl.ds(t, BLK), :]
            im = im + tap * spec_ref[q, 1, pl.ds(t, BLK), :]
            return re, im

        zero = jnp.zeros((BLK, 128), jnp.float32)
        re, im = lax.fori_loop(0, TAPS, tap_step, (zero, zero), unroll=3)
        filt_ref[q, 0] = re
        filt_ref[q, 1] = im
        run_ref[0] += re * re + im * im

    lanes = lax.broadcasted_iota(jnp.int32, (BLK, 128), 1)
    low = lanes < 64
    k2 = lanes & 63
    sums = run_ref[0]
    swapped = pltpu.roll(sums, 64, 1)
    total = sums + swapped
    run_ref[1] = total
    run_ref[2] = (
        total
        + jnp.where(k2 >= 1, pltpu.roll(total, 1, 1), 0.0)
        + jnp.where(k2 <= 62, pltpu.roll(total, 127, 1), 0.0)
    )

    def finish(q, re, im, prefix, suffix):
        window = (
            run_ref[2]
            + jnp.where(k2 >= 2, pltpu.roll(suffix, 2, 1), 0.0)
            + jnp.where(k2 <= 61, pltpu.roll(prefix, 126, 1), 0.0)
        )
        scale = lax.rsqrt(window * rows_ref[2, pl.ds(q, 1), :] + EPSILON)
        cos = rows_ref[0, pl.ds(q, 1), :]
        sin = rows_ref[1, pl.ds(q, 1), :]
        white_re = ((re * cos + im * sin) * scale).astype(jnp.bfloat16).T
        white_im = ((im * cos - re * sin) * scale).astype(jnp.bfloat16).T
        bands = pl.ds(q * 8, 8)
        out_ref[bands, 0] = white_re.reshape(8, 16, 128)
        out_ref[bands, 1] = white_im.reshape(8, 16, 128)

    re, im = filt_ref[0, 0], filt_ref[0, 1]
    power = re * re + im * im
    finish(0, re, im, jnp.where(low, power, swapped + power), jnp.where(low, total, sums))
    run_ref[0] = jnp.where(low, power, 0.0)

    @pl.loop(1, QT)
    def _(q):
        re, im = filt_ref[q, 0], filt_ref[q, 1]
        before = run_ref[0]
        upto = before + (re * re + im * im)
        rest = jnp.maximum(run_ref[1] - before, 0.0)
        run_ref[0] = upto
        finish(q, re, im, jnp.where(low, upto, rest), jnp.where(low, rest, upto))


def whiten_block(wide, table, taps, offsets):
    return pl.pallas_call(
        white_kernel,
        out_shape=jax.ShapeDtypeStruct((NDEV, 2, 16, BLK), jnp.bfloat16),
        in_specs=[
            pl.BlockSpec(memory_space=pltpu.VMEM),
            pl.BlockSpec(memory_space=pltpu.VMEM),
            pl.BlockSpec(memory_space=pltpu.VMEM),
            pl.BlockSpec(memory_space=pltpu.SMEM),
        ],
        out_specs=pl.BlockSpec(memory_space=pltpu.VMEM),
        scratch_shapes=[
            pltpu.VMEM((QT, WIDE, 256), jnp.bfloat16),
            pltpu.VMEM((QT, 2, WIDE, 128), jnp.float32),
            pltpu.VMEM((QT, 2, BLK, 128), jnp.float32),
            pltpu.VMEM((3, BLK, 128), jnp.float32),
            pltpu.VMEM((3, QT, 128), jnp.float32),
        ],
        compiler_params=pltpu.CompilerParams(vmem_limit_bytes=40 << 20),
        name="whiten_block",
    )(wide, table, taps, offsets)


def offsets_of(i):
    return i % 4, (i // 4 + 2 * i) % 4, (i // 16 + 3 * i) % 4, i // 64


def place():
    shard = lax.axis_index("shard")
    return lax.axis_index("group"), shard // 8, (shard // 2) % 4, shard % 2


def partner(i, back):
    x, z, y, core = place()
    dx, dz, dy, dc = offsets_of(i)
    other = (core + dc) % 2
    sign = 2 * other - 1 if back else 1 - 2 * core
    return (x + 4 + sign * dx) % 4, ((z + 4 + sign * dz) % 4 * 4 + (y + 4 + sign * dy) % 4) * 2 + other


def signal_everyone(barrier):
    x, z, y, core = place()

    @pl.loop(0, 16)
    def _(i):
        there = (x + i // 4) % 4
        row = (z + i % 4) % 4 * 8
        for dy in range(4):
            for dc in range(2):
                shard = row + (y + dy) % 4 * 2 + (core + dc) % 2

                def signal():
                    pl.semaphore_signal(barrier, inc=1, device_id=(there, shard), device_id_type=MESH)

                if dy == 0 and dc == 0:
                    pl.when(i > 0)(signal)
                else:
                    signal()


def lag_rows(i, coarse_ref, fine_ref, table_ref):
    group, shard = partner(i, True)
    band = group * 32 + shard
    tile, part = band // 8, band % 8
    residue = jnp.where(part < 4, tile, jnp.where(tile == 0, 16, 32 - tile))
    cos_a, sin_a = coarse_ref[0, pl.ds(residue, 1), :], coarse_ref[1, pl.ds(residue, 1), :]
    rows = pl.ds(pl.multiple_of(part % 4 * 16, 16), 16)
    cos_b, sin_b = fine_ref[0, rows, :], fine_ref[1, rows, :]
    table_ref[i, 0] = (cos_a * cos_b - sin_a * sin_b).astype(jnp.bfloat16)
    table_ref[i, 1] = (-(sin_a * cos_b + cos_a * sin_b)).astype(jnp.bfloat16)


def pair_kernel(
    pairs_ref, white_ref, out_ref, bands_ref, rolled_ref, send_ref, recv_ref, table_ref,
    coarse_ref, fine_ref, band_send, band_recv, cross_send, cross_recv,
):
    me = lax.axis_index("group") * 32 + lax.axis_index("shard")
    barrier = pltpu.get_barrier_semaphore()
    signal_everyone(barrier)
    pl.semaphore_wait(barrier, NDEV - 1)

    @pl.loop(1, NDEV)
    def _(i):
        group, shard = partner(i, False)
        pltpu.make_async_remote_copy(
            src_ref=white_ref.at[group * 32 + shard],
            dst_ref=bands_ref.at[me],
            send_sem=band_send,
            recv_sem=band_recv,
            device_id=(group, shard),
            device_id_type=MESH,
        ).start()

    bands_ref[me] = white_ref[me]
    lag = lax.broadcasted_iota(jnp.int32, (64, NLAG), 1) - NLAG // 2
    row = lax.broadcasted_iota(jnp.int32, (64, NLAG), 0)
    fine = ((32 * row * lag) & (NT - 1)).astype(jnp.float32) * (2.0 * math.pi / NT)
    coarse = ((row * lag) & (NT - 1)).astype(jnp.float32) * (2.0 * math.pi / NT)
    fine_ref[0] = jnp.cos(fine)
    fine_ref[1] = jnp.sin(fine)
    coarse_ref[0] = jnp.cos(coarse[:32])
    coarse_ref[1] = jnp.sin(coarse[:32])

    @pl.loop(0, NDEV)
    def _(i):
        lag_rows(i, coarse_ref, fine_ref, table_ref)

    out_ref[...] = jnp.zeros_like(out_ref)
    everyone = pl.ds(0, NDEV - 1)
    arrivals = pltpu.make_async_remote_copy(
        src_ref=white_ref.at[everyone],
        dst_ref=bands_ref.at[everyone],
        send_sem=band_send,
        recv_sem=band_recv,
        device_id=partner(1, False),
        device_id_type=MESH,
    )
    arrivals.wait()

    @pl.loop(0, NDEV)
    def _(block):
        both = bands_ref[block].astype(jnp.float32).reshape(32, 128)
        rolled_ref[block] = pltpu.roll(both, 64, 1).astype(jnp.bfloat16).reshape(2, 16, 128)

    def products(owner, to_ref, slot):
        for p in range(4):
            a = pairs_ref[8 * owner + 2 * p]
            b = pairs_ref[8 * owner + 2 * p + 1]
            left = bands_ref[a].astype(jnp.float32)
            right = rolled_ref[b].astype(jnp.float32)
            to_ref[slot, p, 0] = (left[0] * right[0] + left[1] * right[1]).astype(jnp.bfloat16)
            to_ref[slot, p, 1] = (left[1] * right[0] - left[0] * right[1]).astype(jnp.bfloat16)

    @pl.loop(1, NDEV)
    def _(i):
        group, shard = partner(i, False)
        products(group * 32 + shard, send_ref, i)
        pltpu.make_async_remote_copy(
            src_ref=send_ref.at[i],
            dst_ref=recv_ref.at[i],
            send_sem=cross_send,
            recv_sem=cross_recv.at[i // 8],
            device_id=(group, shard),
            device_id_type=MESH,
        ).start()

    products(me, recv_ref, 0)

    def accumulate(first, count, piece_of):
        pltpu.make_async_remote_copy(
            src_ref=send_ref.at[pl.ds(first, count)],
            dst_ref=recv_ref.at[pl.ds(first, count)],
            send_sem=cross_send,
            recv_sem=cross_recv.at[piece_of],
            device_id=partner(1, False),
            device_id_type=MESH,
        ).wait_recv()
        slots = pl.ds(piece_of * 8, 8)
        table = table_ref[slots].reshape(256, NLAG)
        for p in range(4):
            piece = recv_ref[slots, p].reshape(256, BLK)
            out_ref[p] += lax.dot_general(
                piece, table, (((0,), (0,)), ((), ())), preferred_element_type=jnp.float32
            )

    accumulate(1, 7, 0)

    @pl.loop(1, 16)
    def _(g):
        accumulate(g * 8, 8, g)

    pltpu.make_async_remote_copy(
        src_ref=send_ref.at[pl.ds(1, NDEV - 1)],
        dst_ref=recv_ref.at[pl.ds(1, NDEV - 1)],
        send_sem=cross_send,
        recv_sem=cross_recv.at[0],
        device_id=partner(1, False),
        device_id_type=MESH,
    ).wait_send()


def correlate(pairs, white):
    return pl.pallas_call(
        pair_kernel,
        out_shape=jax.ShapeDtypeStruct((4, BLK, NLAG), jnp.float32),
        in_specs=[pl.BlockSpec(memory_space=pltpu.SMEM), pl.BlockSpec(memory_space=pltpu.VMEM)],
        out_specs=pl.BlockSpec(memory_space=pltpu.VMEM),
        scratch_shapes=[
            pltpu.VMEM((NDEV, 2, 16, BLK), jnp.bfloat16),
            pltpu.VMEM((NDEV, 2, 16, BLK), jnp.bfloat16),
            pltpu.VMEM((NDEV, 4, 2, 16, BLK), jnp.bfloat16),
            pltpu.VMEM((NDEV, 4, 2, 16, BLK), jnp.bfloat16),
            pltpu.VMEM((NDEV, 2, 16, NLAG), jnp.bfloat16),
            pltpu.VMEM((2, 32, NLAG), jnp.float32),
            pltpu.VMEM((2, 64, NLAG), jnp.float32),
            pltpu.SemaphoreType.DMA,
            pltpu.SemaphoreType.DMA,
            pltpu.SemaphoreType.DMA,
            pltpu.SemaphoreType.DMA((16,)),
        ],
        compiler_params=pltpu.CompilerParams(collective_id=0, has_side_effects=True, vmem_limit_bytes=40 << 20),
        name="correlate",
    )(pairs, white)


def body(samples, fan_taps, pair_blocks, pair_valid, coil_offsets):
    x = samples.reshape(BLK, NT)
    before = lax.ppermute(x[BLK - HALF :], AXES, [(i, i + 1) for i in range(NDEV - 1)])
    after = lax.ppermute(x[:HALF], AXES, [(i + 1, i) for i in range(NDEV - 1)])
    wide = jnp.concatenate([before, x, after], axis=0)
    by_residue = fan_taps.reshape(TAPS, 64, 32).transpose(2, 0, 1)
    low, high = by_residue[:QT], jnp.concatenate([by_residue[QT : QT + 1], by_residue[:QT:-1]], axis=0)
    taps = jnp.concatenate([low, high], axis=2)
    white = whiten_block(wide, jnp.asarray(second_stage_table()), taps, coil_offsets)
    sums = correlate(pair_blocks.reshape(-1), white)
    weights = pair_valid.astype(jnp.float32) * (1.0 / math.sqrt(NB))
    return sums * weights[:, None, None]


def solution(mesh):
    return jax.shard_map(
        body,
        mesh=mesh,
        in_specs=(P(AXES, None, None), P(), P(), P(AXES), P()),
        out_specs=P(AXES, None, None),
        check_vma=False,
    )
```

```python
import math

import jax
import jax.numpy as jnp
import ml_dtypes
import numpy as np
from jax import lax
from jax.experimental import pallas as pl
from jax.experimental.pallas import tpu as pltpu
from jax.sharding import PartitionSpec as P

HALF = 16
NLAG = 512
NT = 4096
NB = 2048
BLK = 128
WIDE = BLK + 2 * HALF
EPSILON = 1e-05
AXES = ("group", "shard")
NDEV = 128
MESH = pl.DeviceIdType.MESH
TAPS = 2 * HALF + 1
QT = 16


def residues():
    low = np.arange(QT)
    high = np.where(low == 0, 16, 32 - low)
    return low, high


def tile_bins():
    low, high = residues()
    k2 = np.arange(64)
    return np.concatenate([low[:, None] + 32 * k2, high[:, None] + 32 * k2], axis=1)


def second_stage_table():
    bins = tile_bins()
    b = np.arange(128)
    phase = 2 * np.pi * ((b[None, :, None] * bins[:, None, :]) % NT) / NT
    cos, sin = np.cos(phase), np.sin(phase)
    table = np.zeros((QT, 2, 128, 2, 128))
    conj = np.concatenate([np.ones(64), -np.ones(64)])
    table[:, 0, :, 0] = cos
    table[:, 1, :, 0] = sin * conj
    table[:, 0, :, 1] = -sin
    table[:, 1, :, 1] = cos * conj
    table[0] = 0.0
    table[0, 0, :, 0, :64] = cos[0, :, :64]
    table[0, 0, :, 1, :64] = -sin[0, :, :64]
    table[0, 1, :, 0, 64:] = cos[0, :, 64:]
    table[0, 1, :, 1, 64:] = -sin[0, :, 64:]
    return (table.reshape(QT, 256, 256) / math.sqrt(NT)).astype(ml_dtypes.bfloat16)


def real_fft(rows):
    count = len(rows)
    if count == 2:
        return [(rows[0] + rows[1], None), (rows[0] - rows[1], None)]
    even = real_fft(rows[0::2])
    odd = real_fft(rows[1::2])
    half, quarter = count // 2, count // 4
    out = [None] * (half + 1)
    out[0] = (even[0][0] + odd[0][0], None)
    out[half] = (even[0][0] - odd[0][0], None)
    out[quarter] = (even[quarter][0], -odd[quarter][0])
    for k in range(1, quarter):
        wr, wi = math.cos(2 * math.pi * k / count), -math.sin(2 * math.pi * k / count)
        o_re, o_im = odd[k]
        e_re, e_im = even[k]
        t_re = o_re * wr - o_im * wi
        t_im = o_re * wi + o_im * wr
        out[k] = (e_re + t_re, e_im + t_im)
        out[half - k] = (e_re - t_re, t_im - e_im)
    return out


def offsets_of(i):
    return i % 4, (i // 4 + 2 * i) % 4, (i // 16 + 3 * i) % 4, i // 64


def place():
    shard = lax.axis_index("shard")
    return lax.axis_index("group"), shard // 8, (shard // 2) % 4, shard % 2


def partner(i, back):
    x, z, y, core = place()
    dx, dz, dy, dc = offsets_of(i)
    other = (core + dc) % 2
    sign = 2 * other - 1 if back else 1 - 2 * core
    return (x + 4 + sign * dx) % 4, ((z + 4 + sign * dz) % 4 * 4 + (y + 4 + sign * dy) % 4) * 2 + other


def signal_some(barrier, i):
    x, z, y, core = place()
    there = (x + i // 4) % 4
    row = (z + i % 4) % 4 * 8
    for dy in range(4):
        for dc in range(2):
            shard = row + (y + dy) % 4 * 2 + (core + dc) % 2

            def signal():
                pl.semaphore_signal(barrier, inc=1, device_id=(there, shard), device_id_type=MESH)

            if dy == 0 and dc == 0:
                pl.when(i > 0)(signal)
            else:
                signal()


def first_stage(rows, y_ref, at):
    freq = real_fft(rows)
    for q in range(QT):
        second = freq[16][0] if q == 0 else freq[q][1]
        y_ref[q, at, 0:128] = freq[q][0].astype(jnp.bfloat16)
        y_ref[q, at, 128:256] = second.astype(jnp.bfloat16)


def sort_taps(fan_ref, turned_ref, taps_ref):
    blank = jnp.zeros((128 - TAPS, 128), jnp.float32)

    @pl.loop(0, QT)
    def _(j):
        at = pl.ds(pl.multiple_of(j * 128, 128), 128)
        turned_ref[at, :] = jnp.concatenate([fan_ref[:, at], blank], axis=0).T

    @pl.loop(0, QT)
    def _(q):
        high = jnp.where(q == 0, 16, 32 - q)
        both = jnp.concatenate(
            [turned_ref[pl.ds(q, 64, stride=32), :], turned_ref[pl.ds(high, 64, stride=32), :]], axis=0
        )
        taps_ref[q] = both.T[:40]


def lag_tables(coarse_ref, fine_ref):
    lag = lax.broadcasted_iota(jnp.int32, (64, NLAG), 1) - NLAG // 2
    row = lax.broadcasted_iota(jnp.int32, (64, NLAG), 0)
    fine = ((32 * row * lag) & (NT - 1)).astype(jnp.float32) * (2.0 * math.pi / NT)
    coarse = ((row * lag) & (NT - 1)).astype(jnp.float32) * (2.0 * math.pi / NT)
    fine_ref[0] = jnp.cos(fine)
    fine_ref[1] = jnp.sin(fine)
    coarse_ref[0] = jnp.cos(coarse[:32])
    coarse_ref[1] = jnp.sin(coarse[:32])


def lag_rows(i, coarse_ref, fine_ref, lags_ref):
    group, shard = partner(i, True)
    band = group * 32 + shard
    tile, part = band // 8, band % 8
    residue = jnp.where(part < 4, tile, jnp.where(tile == 0, 16, 32 - tile))
    cos_a, sin_a = coarse_ref[0, pl.ds(residue, 1), :], coarse_ref[1, pl.ds(residue, 1), :]
    rows = pl.ds(pl.multiple_of(part % 4 * 16, 16), 16)
    cos_b, sin_b = fine_ref[0, rows, :], fine_ref[1, rows, :]
    lags_ref[i, 0] = (cos_a * cos_b - sin_a * sin_b).astype(jnp.bfloat16)
    lags_ref[i, 1] = (-(sin_a * cos_b + cos_a * sin_b)).astype(jnp.bfloat16)


def bin_rows(offset, rows_ref):
    lane = lax.broadcasted_iota(jnp.int32, (QT, 128), 1)
    tile = lax.broadcasted_iota(jnp.int32, (QT, 128), 0)
    residue = jnp.where(lane < 64, tile, jnp.where(tile == 0, 16, 32 - tile))
    bins = residue + 32 * (lane & 63)
    theta = ((bins * offset) & (NT - 1)).astype(jnp.float32) * (2.0 * math.pi / NT)
    rows_ref[0] = jnp.cos(theta)
    rows_ref[1] = jnp.sin(theta)
    count = jnp.minimum(bins + 64, NB - 1) - jnp.maximum(bins - 64, 0) + 1
    rows_ref[2] = 1.0 / count.astype(jnp.float32)


def copy_to(src, dst, send_sem, recv_sem, device):
    return pltpu.make_async_remote_copy(
        src_ref=src, dst_ref=dst, send_sem=send_sem, recv_sem=recv_sem, device_id=device, device_id_type=MESH
    )


def kernel(
    pairs_ref, offsets_ref, x_ref, fan_ref, table_hbm, out_ref,
    table_ref, halo_ref, y_ref, even_ref, odd_ref, turned_ref, taps_ref, filt_ref, upto_ref, run_ref, rows_ref,
    white_ref, bands_ref, send_ref, recv_ref, lags_ref, coarse_ref, fine_ref,
    table_sem, halo_send, halo_recv, band_send, band_recv, cross_send, cross_recv,
):
    x, z, y, core = place()
    me = lax.axis_index("group") * 32 + lax.axis_index("shard")
    barrier = pltpu.get_barrier_semaphore()
    fetch = pltpu.make_async_copy(table_hbm, table_ref, table_sem)
    fetch.start()

    @pl.loop(0, 8)
    def _(chunk):
        signal_some(barrier, 2 * chunk)
        signal_some(barrier, 2 * chunk + 1)
        at = pl.ds(pl.multiple_of(chunk * 16, 16), 16)
        to = pl.ds(pl.multiple_of(chunk * 16 + 16, 16), 16)
        first_stage([x_ref[at, a * 128 : (a + 1) * 128].astype(jnp.float32) for a in range(32)], y_ref, to)

    pl.semaphore_wait(barrier, NDEV - 1)
    after, before = (me + 1) % NDEV, (me + NDEV - 1) % NDEV
    to_after = copy_to(
        x_ref.at[pl.ds(BLK - HALF, HALF)], halo_ref.at[0], halo_send.at[0], halo_recv.at[0],
        (after // 32, after % 32),
    )
    to_before = copy_to(
        x_ref.at[pl.ds(0, HALF)], halo_ref.at[1], halo_send.at[1], halo_recv.at[1],
        (before // 32, before % 32),
    )
    to_after.start()
    to_before.start()

    sort_taps(fan_ref, turned_ref, taps_ref)
    bin_rows(offsets_ref[me], rows_ref)
    lag_tables(coarse_ref, fine_ref)

    @pl.loop(0, NDEV)
    def _(i):
        lag_rows(i, coarse_ref, fine_ref, lags_ref)

    to_after.wait()
    to_before.wait()

    @pl.loop(0, 2)
    def _(side):
        edge = jnp.where(side == 0, me > 0, me < NDEV - 1).astype(jnp.float32)
        to = pl.ds(pl.multiple_of(side * (BLK + HALF), 16), 16)
        first_stage(
            [halo_ref[side, :, a * 128 : (a + 1) * 128].astype(jnp.float32) * edge for a in range(32)], y_ref, to
        )

    fetch.wait()
    lanes = lax.broadcasted_iota(jnp.int32, (BLK, 128), 1)
    low = lanes < 64
    k2 = lanes & 63

    def second_stage(q, to_ref):
        both = jnp.dot(y_ref[q], table_ref[q], preferred_element_type=jnp.float32)
        to_ref[0] = both[:, :128]
        to_ref[1] = both[:, 128:]

    def fan(q, spec_ref):
        for h in (0, 64):
            re = jnp.zeros((64, 128), jnp.float32)
            im = re
            for t in range(TAPS):
                tap = taps_ref[q, t : t + 1, :]
                re = re + tap * spec_ref[0, t + h : t + h + 64, :]
                im = im + tap * spec_ref[1, t + h : t + h + 64, :]
            rows = slice(h, h + 64)
            filt_ref[q, 0, rows] = re
            filt_ref[q, 1, rows] = im
            run = run_ref[0, rows] + jnp.where(low[:64] | (q > 0), re * re + im * im, 0.0)
            run_ref[0, rows] = run
            upto_ref[q, rows] = run

    run_ref[0] = jnp.zeros((BLK, 128), jnp.float32)
    second_stage(0, even_ref)

    @pl.loop(0, QT // 2)
    def _(h):
        second_stage(2 * h + 1, odd_ref)
        fan(2 * h, even_ref)
        second_stage(jnp.minimum(2 * h + 2, QT - 1), even_ref)
        fan(2 * h + 1, odd_ref)

    power = filt_ref[0, 0] * filt_ref[0, 0] + filt_ref[0, 1] * filt_ref[0, 1]
    run_ref[0] = run_ref[0] + jnp.where(low, 0.0, power)
    sums = run_ref[0]
    swapped = pltpu.roll(sums, 64, 1)
    total = sums + swapped
    run_ref[1] = total
    run_ref[2] = (
        total
        + jnp.where(k2 >= 1, pltpu.roll(total, 1, 1), 0.0)
        + jnp.where(k2 <= 62, pltpu.roll(total, 127, 1), 0.0)
    )
    run_ref[3] = jnp.where(low, power, sums)
    run_ref[4] = jnp.where(low, total, swapped + power)
    sign = 1 - 2 * core

    @pl.loop(0, QT)
    def _(step):
        to_x = (x + 4 + sign * (step % 4)) % 4
        to_z = (z + 4 + sign * ((step // 4 + 2 * step) % 4)) % 4
        q = to_x * 4 + to_z
        re, im = filt_ref[q, 0], filt_ref[q, 1]
        upto = jnp.where(q == 0, run_ref[3], upto_ref[q])
        rest = jnp.where(q == 0, run_ref[4], jnp.maximum(run_ref[1] - upto_ref[jnp.maximum(q - 1, 0)], 0.0))
        prefix = jnp.where(low, upto, rest)
        suffix = jnp.where(low, rest, upto)
        window = (
            run_ref[2]
            + jnp.where(k2 >= 2, pltpu.roll(suffix, 2, 1), 0.0)
            + jnp.where(k2 <= 61, pltpu.roll(prefix, 126, 1), 0.0)
        )
        scale = lax.rsqrt(window * rows_ref[2, pl.ds(q, 1), :] + EPSILON)
        cos = rows_ref[0, pl.ds(q, 1), :]
        sin = rows_ref[1, pl.ds(q, 1), :]
        white_re = ((re * cos + im * sin) * scale).astype(jnp.bfloat16).T
        white_im = ((im * cos - re * sin) * scale).astype(jnp.bfloat16).T
        tile = pl.ds(q * 8, 8)
        white_ref[tile, 0] = white_re.reshape(8, 16, 128)
        white_ref[tile, 1] = white_im.reshape(8, 16, 128)
        for dy in range(4):
            for dc in range(2):
                shard = (to_z * 4 + (y + 4 + sign * dy) % 4) * 2 + (core + dc) % 2

                def push():
                    copy_to(
                        white_ref.at[to_x * 32 + shard], bands_ref.at[me], band_send, band_recv, (to_x, shard)
                    ).start()

                if dy == 0 and dc == 0:
                    pl.when(step > 0)(push)
                else:
                    push()

    bands_ref[me] = white_ref[me]
    out_ref[...] = jnp.zeros_like(out_ref)
    somewhere = partner(1, False)
    others = pl.ds(0, NDEV - 1)
    copy_to(white_ref.at[others], bands_ref.at[others], band_send, band_recv, somewhere).wait()

    def products(owner, to_ref, slot):
        for p in range(4):
            a = pairs_ref[0, 4 * owner + p]
            b = pairs_ref[1, 4 * owner + p]
            left = bands_ref[a].astype(jnp.float32)
            right = pltpu.roll(bands_ref[b].astype(jnp.float32).reshape(32, 128), 64, 1).reshape(2, 16, 128)
            to_ref[slot, p, 0] = (left[0] * right[0] + left[1] * right[1]).astype(jnp.bfloat16)
            to_ref[slot, p, 1] = (left[1] * right[0] - left[0] * right[1]).astype(jnp.bfloat16)

    @pl.loop(1, NDEV)
    def _(i):
        group, shard = partner(i, False)
        products(group * 32 + shard, send_ref, i)
        copy_to(send_ref.at[i], recv_ref.at[i], cross_send, cross_recv.at[i // 8], (group, shard)).start()

    products(me, recv_ref, 0)

    def accumulate(first, count, g):
        some = pl.ds(first, count)
        copy_to(send_ref.at[some], recv_ref.at[some], cross_send, cross_recv.at[g], somewhere).wait_recv()
        slots = pl.ds(g * 8, 8)
        lags = lags_ref[slots].reshape(256, NLAG)
        for p in range(4):
            piece = recv_ref[slots, p].reshape(256, BLK)
            out_ref[p] += lax.dot_general(
                piece, lags, (((0,), (0,)), ((), ())), preferred_element_type=jnp.float32
            )

    accumulate(1, 7, 0)

    @pl.loop(1, 16)
    def _(g):
        accumulate(g * 8, 8, g)

    rest_of = pl.ds(1, NDEV - 1)
    copy_to(send_ref.at[rest_of], recv_ref.at[rest_of], cross_send, cross_recv.at[0], somewhere).wait_send()


def correlate(pairs, offsets, x, fan_taps, table):
    f32, bf16 = jnp.float32, jnp.bfloat16
    vmem = pl.BlockSpec(memory_space=pltpu.VMEM)
    smem = pl.BlockSpec(memory_space=pltpu.SMEM)
    return pl.pallas_call(
        kernel,
        out_shape=jax.ShapeDtypeStruct((4, BLK, NLAG), f32),
        in_specs=[smem, smem, vmem, vmem, pl.BlockSpec(memory_space=pl.ANY)],
        out_specs=vmem,
        scratch_shapes=[
            pltpu.VMEM((QT, 256, 256), bf16),
            pltpu.VMEM((2, HALF, NT), bf16),
            pltpu.VMEM((QT, WIDE, 256), bf16),
            pltpu.VMEM((2, WIDE, 128), f32),
            pltpu.VMEM((2, WIDE, 128), f32),
            pltpu.VMEM((NB, 128), f32),
            pltpu.VMEM((QT, 40, 128), f32),
            pltpu.VMEM((QT, 2, BLK, 128), f32),
            pltpu.VMEM((QT, BLK, 128), f32),
            pltpu.VMEM((5, BLK, 128), f32),
            pltpu.VMEM((3, QT, 128), f32),
            pltpu.VMEM((NDEV, 2, 16, BLK), bf16),
            pltpu.VMEM((NDEV, 2, 16, BLK), bf16),
            pltpu.VMEM((NDEV, 4, 2, 16, BLK), bf16),
            pltpu.VMEM((NDEV, 4, 2, 16, BLK), bf16),
            pltpu.VMEM((NDEV, 2, 16, NLAG), bf16),
            pltpu.VMEM((2, 32, NLAG), f32),
            pltpu.VMEM((2, 64, NLAG), f32),
            pltpu.SemaphoreType.DMA,
            pltpu.SemaphoreType.DMA((2,)),
            pltpu.SemaphoreType.DMA((2,)),
            pltpu.SemaphoreType.DMA,
            pltpu.SemaphoreType.DMA,
            pltpu.SemaphoreType.DMA,
            pltpu.SemaphoreType.DMA((16,)),
        ],
        compiler_params=pltpu.CompilerParams(collective_id=0, has_side_effects=True, vmem_limit_bytes=48 << 20),
        name="correlate",
    )(pairs, offsets, x, fan_taps, table)


def body(samples, fan_taps, pair_blocks, pair_valid, coil_offsets):
    table = jnp.asarray(second_stage_table())
    sums = correlate(pair_blocks.T, coil_offsets, samples.reshape(BLK, NT), fan_taps, table)
    weights = pair_valid.astype(jnp.float32) * (1.0 / math.sqrt(NB))
    return sums * weights[:, None, None]


def solution(mesh):
    return jax.shard_map(
        body,
        mesh=mesh,
        in_specs=(P(AXES, None, None), P(), P(), P(AXES), P()),
        out_specs=P(AXES, None, None),
        check_vma=False,
    )
```

```python
import math

import jax
import jax.numpy as jnp
import ml_dtypes
import numpy as np
from jax import lax
from jax.experimental import pallas as pl
from jax.experimental.pallas import tpu as pltpu
from jax.sharding import PartitionSpec as P

HALF = 16
NLAG = 512
NT = 4096
NB = 2048
BLK = 128
WIDE = BLK + 2 * HALF
EPSILON = 1e-05
AXES = ("group", "shard")
NDEV = 128
PAIRS = 512
MESH = pl.DeviceIdType.MESH
TAPS = 2 * HALF + 1
QT = 16


def residues():
    low = np.arange(QT)
    high = np.where(low == 0, 16, 32 - low)
    return low, high


def tile_bins():
    low, high = residues()
    k2 = np.arange(64)
    return np.concatenate([low[:, None] + 32 * k2, high[:, None] + 32 * k2], axis=1)


def second_stage_table():
    bins = tile_bins()
    b = np.arange(128)
    phase = 2 * np.pi * ((b[None, :, None] * bins[:, None, :]) % NT) / NT
    cos, sin = np.cos(phase), np.sin(phase)
    table = np.zeros((QT, 2, 128, 2, 128))
    conj = np.concatenate([np.ones(64), -np.ones(64)])
    table[:, 0, :, 0] = cos
    table[:, 1, :, 0] = sin * conj
    table[:, 0, :, 1] = -sin
    table[:, 1, :, 1] = cos * conj
    table[0] = 0.0
    table[0, 0, :, 0, :64] = cos[0, :, :64]
    table[0, 0, :, 1, :64] = -sin[0, :, :64]
    table[0, 1, :, 0, 64:] = cos[0, :, 64:]
    table[0, 1, :, 1, 64:] = -sin[0, :, 64:]
    return (table.reshape(QT, 256, 256) / math.sqrt(NT)).astype(ml_dtypes.bfloat16)


def real_fft(rows):
    count = len(rows)
    if count == 2:
        return [(rows[0] + rows[1], None), (rows[0] - rows[1], None)]
    even = real_fft(rows[0::2])
    odd = real_fft(rows[1::2])
    half, quarter = count // 2, count // 4
    out = [None] * (half + 1)
    out[0] = (even[0][0] + odd[0][0], None)
    out[half] = (even[0][0] - odd[0][0], None)
    out[quarter] = (even[quarter][0], -odd[quarter][0])
    for k in range(1, quarter):
        wr, wi = math.cos(2 * math.pi * k / count), -math.sin(2 * math.pi * k / count)
        o_re, o_im = odd[k]
        e_re, e_im = even[k]
        t_re = o_re * wr - o_im * wi
        t_im = o_re * wi + o_im * wr
        out[k] = (e_re + t_re, e_im + t_im)
        out[half - k] = (e_re - t_re, t_im - e_im)
    return out


def offsets_of(i):
    return i % 4, (i // 4 + 2 * i) % 4, (i // 16 + 3 * i) % 4, i // 64


def place():
    shard = lax.axis_index("shard")
    return lax.axis_index("group"), shard // 8, (shard // 2) % 4, shard % 2


def partner(i, back):
    x, z, y, core = place()
    dx, dz, dy, dc = offsets_of(i)
    other = (core + dc) % 2
    sign = 2 * other - 1 if back else 1 - 2 * core
    return (x + 4 + sign * dx) % 4, ((z + 4 + sign * dz) % 4 * 4 + (y + 4 + sign * dy) % 4) * 2 + other


def signal_some(barrier, i):
    x, z, y, core = place()
    there = (x + i // 4) % 4
    row = (z + i % 4) % 4 * 8
    for dy in range(4):
        for dc in range(2):
            shard = row + (y + dy) % 4 * 2 + (core + dc) % 2

            def signal():
                pl.semaphore_signal(barrier, inc=1, device_id=(there, shard), device_id_type=MESH)

            if dy == 0 and dc == 0:
                pl.when(i > 0)(signal)
            else:
                signal()


def first_stage(rows, y_ref, at):
    freq = real_fft(rows)
    for q in range(QT):
        second = freq[16][0] if q == 0 else freq[q][1]
        y_ref[q, at, 0:128] = freq[q][0].astype(jnp.bfloat16)
        y_ref[q, at, 128:256] = second.astype(jnp.bfloat16)


def sort_taps(fan_ref, turned_ref, taps_ref):
    blank = jnp.zeros((128 - TAPS, 128), jnp.float32)

    @pl.loop(0, QT)
    def _(j):
        at = pl.ds(pl.multiple_of(j * 128, 128), 128)
        turned_ref[at, :] = jnp.concatenate([fan_ref[:, at], blank], axis=0).T

    @pl.loop(0, QT)
    def _(q):
        high = jnp.where(q == 0, 16, 32 - q)
        both = jnp.concatenate(
            [turned_ref[pl.ds(q, 64, stride=32), :], turned_ref[pl.ds(high, 64, stride=32), :]], axis=0
        )
        taps_ref[q] = both.T[:40]


def lag_tables(coarse_ref, fine_ref):
    lag = lax.broadcasted_iota(jnp.int32, (64, NLAG), 1) - NLAG // 2
    row = lax.broadcasted_iota(jnp.int32, (64, NLAG), 0)
    fine = ((32 * row * lag) & (NT - 1)).astype(jnp.float32) * (2.0 * math.pi / NT)
    coarse = ((row * lag) & (NT - 1)).astype(jnp.float32) * (2.0 * math.pi / NT)
    fine_ref[0] = jnp.cos(fine)
    fine_ref[1] = jnp.sin(fine)
    coarse_ref[0] = jnp.cos(coarse[:32])
    coarse_ref[1] = jnp.sin(coarse[:32])


def lag_rows(q, coarse_ref, fine_ref, lags_ref):
    cos_b, sin_b = fine_ref[0], fine_ref[1]
    for half, residue in ((0, q), (64, jnp.where(q == 0, 16, 32 - q))):
        cos_a, sin_a = coarse_ref[0, pl.ds(residue, 1), :], coarse_ref[1, pl.ds(residue, 1), :]
        lags_ref[q, half : half + 64] = (cos_a * cos_b - sin_a * sin_b).astype(jnp.bfloat16)
        lags_ref[q, 128 + half : 192 + half] = (-(sin_a * cos_b + cos_a * sin_b)).astype(jnp.bfloat16)


def pick_rows(pairs_ref, pick_ref):
    block = lax.broadcasted_iota(jnp.int32, (128, 128), 0)
    for side in range(2):
        for at in range(0, PAIRS, 128):
            chosen = block == pairs_ref[side : side + 1, at : at + 128]
            pick_ref[side, at : at + 128, :] = jnp.where(chosen, 1.0, 0.0).T.astype(jnp.bfloat16)


def bin_rows(offset, rows_ref):
    lane = lax.broadcasted_iota(jnp.int32, (QT, 128), 1)
    tile = lax.broadcasted_iota(jnp.int32, (QT, 128), 0)
    residue = jnp.where(lane < 64, tile, jnp.where(tile == 0, 16, 32 - tile))
    bins = residue + 32 * (lane & 63)
    theta = ((bins * offset) & (NT - 1)).astype(jnp.float32) * (2.0 * math.pi / NT)
    rows_ref[0] = jnp.cos(theta)
    rows_ref[1] = jnp.sin(theta)
    count = jnp.minimum(bins + 64, NB - 1) - jnp.maximum(bins - 64, 0) + 1
    rows_ref[2] = 1.0 / count.astype(jnp.float32)


def copy_to(src, dst, send_sem, recv_sem, device):
    return pltpu.make_async_remote_copy(
        src_ref=src, dst_ref=dst, send_sem=send_sem, recv_sem=recv_sem, device_id=device, device_id_type=MESH
    )


def channel_of(device):
    return device // 2 + 64 * (device % 2)


def kernel(
    pairs_hbm, offsets_hbm, valid_hbm, x_hbm, fan_hbm, table_hbm, out_ref,
    pairs_ref, offsets_ref, valid_ref, x_ref, fan_ref, table_ref,
    halo_ref, y_ref, even_ref, odd_ref, turned_ref, taps_ref, filt_ref, upto_ref, run_ref, rows_ref,
    rows32_ref, white_ref, blocks_ref, own_ref, other_ref, pick_ref, cross_ref, sums_ref,
    parts_ref, recv_ref, lags_ref, coarse_ref, fine_ref,
    fetch_sem, halo_send, halo_recv, block_send, block_recv, swap_send, swap_recv, part_send, part_recv,
):
    x, z, y, core = place()
    me = lax.axis_index("group") * 32 + lax.axis_index("shard")
    barrier = pltpu.get_barrier_semaphore()
    moves = (
        (x_hbm, x_ref), (offsets_hbm, offsets_ref), (fan_hbm, fan_ref),
        (pairs_hbm, pairs_ref), (valid_hbm, valid_ref), (table_hbm, table_ref),
    )
    fetches = [pltpu.make_async_copy(src, dst, fetch_sem.at[n]) for n, (src, dst) in enumerate(moves)]
    for fetch in fetches:
        fetch.start()
    fetches[0].wait()

    @pl.loop(0, 8)
    def _(chunk):
        signal_some(barrier, 2 * chunk)
        signal_some(barrier, 2 * chunk + 1)
        at = pl.ds(pl.multiple_of(chunk * 16, 16), 16)
        to = pl.ds(pl.multiple_of(chunk * 16 + 16, 16), 16)
        first_stage([x_ref[at, a * 128 : (a + 1) * 128].astype(jnp.float32) for a in range(32)], y_ref, to)

    pl.semaphore_wait(barrier, NDEV - 1)
    after, before = (me + 1) % NDEV, (me + NDEV - 1) % NDEV
    to_after = copy_to(
        x_ref.at[pl.ds(BLK - HALF, HALF)], halo_ref.at[0], halo_send.at[0], halo_recv.at[0],
        (after // 32, after % 32),
    )
    to_before = copy_to(
        x_ref.at[pl.ds(0, HALF)], halo_ref.at[1], halo_send.at[1], halo_recv.at[1],
        (before // 32, before % 32),
    )
    to_after.start()
    to_before.start()

    for fetch in fetches[1:5]:
        fetch.wait()
    sort_taps(fan_ref, turned_ref, taps_ref)
    bin_rows(offsets_ref[me], rows_ref)
    lag_tables(coarse_ref, fine_ref)
    pick_rows(pairs_ref, pick_ref)

    @pl.loop(0, QT)
    def _(q):
        lag_rows(q, coarse_ref, fine_ref, lags_ref)

    to_after.wait()
    to_before.wait()

    @pl.loop(0, 2)
    def _(side):
        edge = jnp.where(side == 0, me > 0, me < NDEV - 1).astype(jnp.float32)
        to = pl.ds(pl.multiple_of(side * (BLK + HALF), 16), 16)
        first_stage(
            [halo_ref[side, :, a * 128 : (a + 1) * 128].astype(jnp.float32) * edge for a in range(32)], y_ref, to
        )

    fetches[5].wait()
    lanes = lax.broadcasted_iota(jnp.int32, (BLK, 128), 1)
    low = lanes < 64
    k2 = lanes & 63

    def second_stage(q, to_ref):
        both = jnp.dot(y_ref[q], table_ref[q], preferred_element_type=jnp.float32)
        to_ref[0] = both[:, :128]
        to_ref[1] = both[:, 128:]

    def fan(q, spec_ref):
        for h in (0, 64):
            re = jnp.zeros((64, 128), jnp.float32)
            im = re
            for t in range(TAPS):
                tap = taps_ref[q, t : t + 1, :]
                re = re + tap * spec_ref[0, t + h : t + h + 64, :]
                im = im + tap * spec_ref[1, t + h : t + h + 64, :]
            rows = slice(h, h + 64)
            filt_ref[q, 0, rows] = re
            filt_ref[q, 1, rows] = im
            run = run_ref[0, rows] + jnp.where(low[:64] | (q > 0), re * re + im * im, 0.0)
            run_ref[0, rows] = run
            upto_ref[q, rows] = run

    run_ref[0] = jnp.zeros((BLK, 128), jnp.float32)
    second_stage(0, even_ref)

    @pl.loop(0, QT // 2)
    def _(h):
        second_stage(2 * h + 1, odd_ref)
        fan(2 * h, even_ref)
        second_stage(jnp.minimum(2 * h + 2, QT - 1), even_ref)
        fan(2 * h + 1, odd_ref)

    power = filt_ref[0, 0] * filt_ref[0, 0] + filt_ref[0, 1] * filt_ref[0, 1]
    run_ref[0] = run_ref[0] + jnp.where(low, 0.0, power)
    sums = run_ref[0]
    swapped = pltpu.roll(sums, 64, 1)
    total = sums + swapped
    run_ref[1] = total
    run_ref[2] = (
        total
        + jnp.where(k2 >= 1, pltpu.roll(total, 1, 1), 0.0)
        + jnp.where(k2 <= 62, pltpu.roll(total, 127, 1), 0.0)
    )
    run_ref[3] = jnp.where(low, power, sums)
    run_ref[4] = jnp.where(low, total, swapped + power)

    @pl.loop(0, QT)
    def _(q):
        re, im = filt_ref[q, 0], filt_ref[q, 1]
        upto = jnp.where(q == 0, run_ref[3], upto_ref[q])
        rest = jnp.where(q == 0, run_ref[4], jnp.maximum(run_ref[1] - upto_ref[jnp.maximum(q - 1, 0)], 0.0))
        prefix = jnp.where(low, upto, rest)
        suffix = jnp.where(low, rest, upto)
        window = (
            run_ref[2]
            + jnp.where(k2 >= 2, pltpu.roll(suffix, 2, 1), 0.0)
            + jnp.where(k2 <= 61, pltpu.roll(prefix, 126, 1), 0.0)
        )
        scale = lax.rsqrt(window * rows_ref[2, pl.ds(q, 1), :] + EPSILON)
        cos = rows_ref[0, pl.ds(q, 1), :]
        sin = rows_ref[1, pl.ds(q, 1), :]
        rows32_ref[pl.ds(q, BLK, stride=32), :] = (re * cos + im * sin) * scale
        rows32_ref[pl.ds(16 + q, BLK, stride=32), :] = (im * cos - re * sin) * scale

    def packed(channel):
        return rows32_ref[pl.ds(pl.multiple_of(channel * 32, 32), 32), :].astype(jnp.bfloat16)

    @pl.loop(1, NDEV)
    def _(i):
        group, shard = partner(i, False)
        channel = channel_of(group * 32 + shard)
        white_ref[channel] = packed(channel)
        copy_to(white_ref.at[channel], blocks_ref.at[me], block_send, block_recv, (group, shard)).start()

    mine = channel_of(me)
    blocks_ref[me] = packed(mine)
    somewhere = partner(1, False)
    others = pl.ds(0, NDEV - 1)
    copy_to(white_ref.at[others], blocks_ref.at[others], block_send, block_recv, somewhere).wait()

    sibling = (lax.axis_index("group"), lax.axis_index("shard") + 1 - 2 * core)

    @pl.loop(0, NDEV // 8)
    def _(d):
        eight = pl.ds(pl.multiple_of(d * 8, 8), 8)
        to = pl.ds(pl.multiple_of(d * 256, 256), 256)
        rows32_ref[to, :] = blocks_ref[eight].reshape(256, 128).astype(jnp.float32)

    def swap(part):
        some = pl.ds(part * 4, 4)
        return copy_to(own_ref.at[some], other_ref.at[some], swap_send.at[part], swap_recv.at[part], sibling)

    @pl.loop(0, 4)
    def _(part):
        for n in range(4):
            q = part * 4 + n
            own_ref[q, :, 0:128] = rows32_ref[pl.ds(q, BLK, stride=32), :].astype(jnp.bfloat16)
            own_ref[q, :, 128:256] = rows32_ref[pl.ds(16 + q, BLK, stride=32), :].astype(jnp.bfloat16)
        swap(part).start()

    def add_part(part, half):
        rows = pl.ds(pl.multiple_of(half * 256, 256), 256)
        for n in range(4):
            q = part * 4 + n
            left = jnp.dot(pick_ref[0, rows, :], own_ref[q], preferred_element_type=jnp.float32)
            right = jnp.dot(pick_ref[1, rows, :], other_ref[q], preferred_element_type=jnp.float32)
            l_re, l_im, r_re, r_im = left[:, :128], left[:, 128:], right[:, :128], right[:, 128:]
            cross_ref[:, n * 256 : n * 256 + 128] = (l_re * r_re + l_im * r_im).astype(jnp.bfloat16)
            cross_ref[:, n * 256 + 128 : n * 256 + 256] = (l_im * r_re - l_re * r_im).astype(jnp.bfloat16)
        lags = lags_ref[pl.ds(part * 4, 4)].reshape(1024, NLAG)
        return jnp.dot(cross_ref[...], lags, preferred_element_type=jnp.float32)

    @pl.loop(0, 3)
    def _(part):
        swap(part).wait()
        for half in range(2):
            rows = slice(half * 256, half * 256 + 256)
            added = add_part(part, half)
            sums_ref[rows, :] = jnp.where(part == 0, added, sums_ref[rows, :] + added)

    swap(3).wait()

    @pl.loop(0, 2)
    def _(turn):
        half = (turn + y) % 2
        rows = pl.ds(pl.multiple_of(half * 256, 256), 256)
        done = sums_ref[rows, :] + add_part(3, half)
        for n in range(4):
            rows32_ref[pl.ds(half * 1024 + n, 256, stride=4), :] = done[:, n * 128 : n * 128 + 128]

        @pl.loop(0, 64)
        def _(i):
            to_x = 2 * half + (x + i) % 2
            to_y = (y + i // 2 + i) % 4
            to_z = (z + i // 8 + i) % 4
            shard = (to_z * 4 + to_y) * 2 + (core + i // 32) % 2
            owner = to_x * 32 + shard
            part = rows32_ref[pl.ds(pl.multiple_of(owner * 16, 16), 16), :].astype(jnp.bfloat16)
            parts_ref[owner] = part

            @pl.when(owner != me)
            def _():
                copy_to(parts_ref.at[owner], recv_ref.at[mine], part_send, part_recv, (to_x, shard)).start()

    recv_ref[mine] = parts_ref[me]
    copy_to(parts_ref.at[others], recv_ref.at[others], part_send, part_recv, somewhere).wait()

    @pl.loop(0, NDEV // 16)
    def _(d):
        some = pl.ds(pl.multiple_of(d * 16, 16), 16)
        to = pl.ds(pl.multiple_of(d * 256, 256), 256)
        rows32_ref[to, :] = recv_ref[some].reshape(256, 128).astype(jnp.float32)

    for p in range(4):
        weight = valid_ref[p].astype(jnp.float32) * (1.0 / math.sqrt(NB))
        for n in range(4):
            out_ref[p, :, n * 128 : n * 128 + 128] = rows32_ref[pl.ds(p * 4 + n, BLK, stride=16), :] * weight


def correlate(*operands):
    f32, bf16, i32 = jnp.float32, jnp.bfloat16, jnp.int32
    return pl.pallas_call(
        kernel,
        out_shape=jax.ShapeDtypeStruct((4, BLK, NLAG), f32),
        in_specs=[pl.BlockSpec(memory_space=pltpu.HBM)] * 6,
        out_specs=pl.BlockSpec(memory_space=pltpu.VMEM),
        scratch_shapes=[
            pltpu.VMEM((2, PAIRS), i32),
            pltpu.SMEM((NDEV,), i32),
            pltpu.SMEM((4,), i32),
            pltpu.VMEM((BLK, NT), bf16),
            pltpu.VMEM((TAPS, NB), f32),
            pltpu.VMEM((QT, 256, 256), bf16),
            pltpu.VMEM((2, HALF, NT), bf16),
            pltpu.VMEM((QT, WIDE, 256), bf16),
            pltpu.VMEM((2, WIDE, 128), f32),
            pltpu.VMEM((2, WIDE, 128), f32),
            pltpu.VMEM((NB, 128), f32),
            pltpu.VMEM((QT, 40, 128), f32),
            pltpu.VMEM((QT, 2, BLK, 128), f32),
            pltpu.VMEM((QT, BLK, 128), f32),
            pltpu.VMEM((5, BLK, 128), f32),
            pltpu.VMEM((3, QT, 128), f32),
            pltpu.VMEM((32 * BLK, 128), f32),
            pltpu.VMEM((NDEV, 32, 128), bf16),
            pltpu.VMEM((NDEV, 32, 128), bf16),
            pltpu.VMEM((QT, NDEV, 256), bf16),
            pltpu.VMEM((QT, NDEV, 256), bf16),
            pltpu.VMEM((2, PAIRS, NDEV), bf16),
            pltpu.VMEM((256, 1024), bf16),
            pltpu.VMEM((PAIRS, NLAG), f32),
            pltpu.VMEM((NDEV, 16, 128), bf16),
            pltpu.VMEM((NDEV, 16, 128), bf16),
            pltpu.VMEM((QT, 256, NLAG), bf16),
            pltpu.VMEM((2, 32, NLAG), f32),
            pltpu.VMEM((2, 64, NLAG), f32),
            pltpu.SemaphoreType.DMA((6,)),
            pltpu.SemaphoreType.DMA((2,)),
            pltpu.SemaphoreType.DMA((2,)),
            pltpu.SemaphoreType.DMA,
            pltpu.SemaphoreType.DMA,
            pltpu.SemaphoreType.DMA((4,)),
            pltpu.SemaphoreType.DMA((4,)),
            pltpu.SemaphoreType.DMA,
            pltpu.SemaphoreType.DMA,
        ],
        compiler_params=pltpu.CompilerParams(collective_id=0, has_side_effects=True, vmem_limit_bytes=48 << 20),
        name="correlate",
    )(*operands)


def body(samples, fan_taps, pair_blocks, pair_valid, coil_offsets):
    table = jnp.asarray(second_stage_table())
    return correlate(pair_blocks.T, coil_offsets, pair_valid, samples.reshape(BLK, NT), fan_taps, table)


def solution(mesh):
    return jax.shard_map(
        body,
        mesh=mesh,
        in_specs=(P(AXES, None, None), P(), P(), P(AXES), P()),
        out_specs=P(AXES, None, None),
        check_vma=False,
    )
```

```python
import math

import jax
import jax.numpy as jnp
import ml_dtypes
import numpy as np
from jax import lax
from jax.experimental import pallas as pl
from jax.experimental.pallas import tpu as pltpu
from jax.sharding import PartitionSpec as P

HALF = 16
NLAG = 512
NT = 4096
NB = 2048
BLK = 128
WIDE = BLK + 2 * HALF
EPSILON = 1e-05
AXES = ("group", "shard")
NDEV = 128
PAIRS = 512
CHUNK = 32
MESH = pl.DeviceIdType.MESH
TAPS = 2 * HALF + 1
QT = 16


def residues():
    low = np.arange(QT)
    high = np.where(low == 0, 16, 32 - low)
    return low, high


def tile_bins():
    low, high = residues()
    k2 = np.arange(64)
    return np.concatenate([low[:, None] + 32 * k2, high[:, None] + 32 * k2], axis=1)


def second_stage_table():
    bins = tile_bins()
    b = np.arange(128)
    phase = 2 * np.pi * ((b[None, :, None] * bins[:, None, :]) % NT) / NT
    cos, sin = np.cos(phase), np.sin(phase)
    table = np.zeros((QT, 2, 128, 2, 128))
    conj = np.concatenate([np.ones(64), -np.ones(64)])
    table[:, 0, :, 0] = cos
    table[:, 1, :, 0] = sin * conj
    table[:, 0, :, 1] = -sin
    table[:, 1, :, 1] = cos * conj
    table[0] = 0.0
    table[0, 0, :, 0, :64] = cos[0, :, :64]
    table[0, 0, :, 1, :64] = -sin[0, :, :64]
    table[0, 1, :, 0, 64:] = cos[0, :, 64:]
    table[0, 1, :, 1, 64:] = -sin[0, :, 64:]
    return (table.reshape(QT, 256, 256) / math.sqrt(NT)).astype(ml_dtypes.bfloat16)


def real_fft(rows):
    count = len(rows)
    if count == 2:
        return [(rows[0] + rows[1], None), (rows[0] - rows[1], None)]
    even = real_fft(rows[0::2])
    odd = real_fft(rows[1::2])
    half, quarter = count // 2, count // 4
    out = [None] * (half + 1)
    out[0] = (even[0][0] + odd[0][0], None)
    out[half] = (even[0][0] - odd[0][0], None)
    out[quarter] = (even[quarter][0], -odd[quarter][0])
    for k in range(1, quarter):
        wr, wi = math.cos(2 * math.pi * k / count), -math.sin(2 * math.pi * k / count)
        o_re, o_im = odd[k]
        e_re, e_im = even[k]
        t_re = o_re * wr - o_im * wi
        t_im = o_re * wi + o_im * wr
        out[k] = (e_re + t_re, e_im + t_im)
        out[half - k] = (e_re - t_re, t_im - e_im)
    return out


def place():
    shard = lax.axis_index("shard")
    return lax.axis_index("group"), shard // 8, (shard // 2) % 4, shard % 2


def wrap(value, size):
    return lax.rem(value, size)


def signal_some(barrier, i):
    x, z, y, core = place()
    there = (x + i // 4) % 4
    row = (z + i % 4) % 4 * 8
    for dy in range(4):
        for dc in range(2):
            shard = row + (y + dy) % 4 * 2 + (core + dc) % 2

            def signal():
                pl.semaphore_signal(barrier, inc=1, device_id=(there, shard), device_id_type=MESH)

            if dy == 0 and dc == 0:
                pl.when(i > 0)(signal)
            else:
                signal()


def first_stage(rows, y_ref, at):
    freq = real_fft(rows)
    for q in range(QT):
        second = freq[16][0] if q == 0 else freq[q][1]
        y_ref[q, at, 0:128] = freq[q][0].astype(jnp.bfloat16)
        y_ref[q, at, 128:256] = second.astype(jnp.bfloat16)


def sort_taps(fan_ref, turned_ref, taps_ref):
    blank = jnp.zeros((128 - TAPS, 128), jnp.float32)

    @pl.loop(0, QT)
    def _(j):
        at = pl.ds(pl.multiple_of(j * 128, 128), 128)
        turned_ref[at, :] = jnp.concatenate([fan_ref[:, at], blank], axis=0).T

    @pl.loop(0, QT)
    def _(q):
        high = jnp.where(q == 0, 16, 32 - q)
        both = jnp.concatenate(
            [turned_ref[pl.ds(q, 64, stride=32), :], turned_ref[pl.ds(high, 64, stride=32), :]], axis=0
        )
        taps_ref[q] = both.T[:40]


def lag_tables(coarse_ref, fine_ref):
    lag = lax.broadcasted_iota(jnp.int32, (64, NLAG), 1) - NLAG // 2
    row = lax.broadcasted_iota(jnp.int32, (64, NLAG), 0)
    fine = ((32 * row * lag) & (NT - 1)).astype(jnp.float32) * (2.0 * math.pi / NT)
    coarse = ((row * lag) & (NT - 1)).astype(jnp.float32) * (2.0 * math.pi / NT)
    fine_ref[0] = jnp.cos(fine)
    fine_ref[1] = jnp.sin(fine)
    coarse_ref[0] = jnp.cos(coarse[:32])
    coarse_ref[1] = jnp.sin(coarse[:32])


def lag_rows(q, coarse_ref, fine_ref, lags_ref):
    cos_b, sin_b = fine_ref[0], fine_ref[1]
    for half, residue in ((0, q), (64, jnp.where(q == 0, 16, 32 - q))):
        cos_a, sin_a = coarse_ref[0, pl.ds(residue, 1), :], coarse_ref[1, pl.ds(residue, 1), :]
        lags_ref[q, half : half + 64] = (cos_a * cos_b - sin_a * sin_b).astype(jnp.bfloat16)
        lags_ref[q, 128 + half : 192 + half] = (-(sin_a * cos_b + cos_a * sin_b)).astype(jnp.bfloat16)


def pick_rows(pairs_ref, pick_ref):
    block = lax.broadcasted_iota(jnp.int32, (128, 128), 0)
    for side in range(2):
        for at in range(0, PAIRS, 128):
            chosen = block == pairs_ref[side : side + 1, at : at + 128]
            pick_ref[side, at : at + 128, :] = jnp.where(chosen, 1.0, 0.0).T.astype(jnp.bfloat16)


def bin_rows(offset, rows_ref):
    lane = lax.broadcasted_iota(jnp.int32, (QT, 128), 1)
    tile = lax.broadcasted_iota(jnp.int32, (QT, 128), 0)
    residue = jnp.where(lane < 64, tile, jnp.where(tile == 0, 16, 32 - tile))
    bins = residue + 32 * (lane & 63)
    theta = ((bins * offset) & (NT - 1)).astype(jnp.float32) * (2.0 * math.pi / NT)
    rows_ref[0] = jnp.cos(theta)
    rows_ref[1] = jnp.sin(theta)
    count = jnp.minimum(bins + 64, NB - 1) - jnp.maximum(bins - 64, 0) + 1
    rows_ref[2] = 1.0 / count.astype(jnp.float32)


def copy_to(src, dst, send_sem, recv_sem, device):
    return pltpu.make_async_remote_copy(
        src_ref=src, dst_ref=dst, send_sem=send_sem, recv_sem=recv_sem, device_id=device, device_id_type=MESH
    )


def channel_of(x, z, y, core):
    return wrap(x + z + y, 2) * 32 + (x * 16 + z * 4 + y) // 2 + 64 * core


def kernel(
    pairs_hbm, offsets_hbm, valid_hbm, x_hbm, fan_hbm, table_hbm, out_ref,
    pairs_ref, offsets_ref, valid_ref, x_ref, fan_ref, table_ref,
    halo_ref, y_ref, spec_ref, turned_ref, taps_ref, filt_ref, upto_ref, run_ref, rows_ref,
    rows32_ref, white_ref, blocks_ref, own_ref, other_ref, pick_ref, cross_ref, sums_ref,
    parts_ref, recv_ref, lags_ref, coarse_ref, fine_ref,
    fetch_sem, halo_send, halo_recv, block_send, block_recv, swap_send, swap_recv, part_send, part_recv,
):
    x, z, y, core = place()
    me = lax.axis_index("group") * 32 + lax.axis_index("shard")
    barrier = pltpu.get_barrier_semaphore()
    moves = (
        (x_hbm, x_ref), (offsets_hbm, offsets_ref), (fan_hbm, fan_ref),
        (pairs_hbm, pairs_ref), (valid_hbm, valid_ref), (table_hbm, table_ref),
    )
    fetches = [pltpu.make_async_copy(src, dst, fetch_sem.at[n]) for n, (src, dst) in enumerate(moves)]
    for fetch in fetches:
        fetch.start()
    fetches[0].wait()

    @pl.loop(0, 8)
    def _(chunk):
        signal_some(barrier, 2 * chunk)
        signal_some(barrier, 2 * chunk + 1)
        at = pl.ds(pl.multiple_of(chunk * 16, 16), 16)
        to = pl.ds(pl.multiple_of(chunk * 16 + 16, 16), 16)
        first_stage([x_ref[at, a * 128 : (a + 1) * 128].astype(jnp.float32) for a in range(32)], y_ref, to)

    for fetch in fetches[1:]:
        fetch.wait()
    sort_taps(fan_ref, turned_ref, taps_ref)
    bin_rows(offsets_ref[me], rows_ref)

    def second_stage(rows):
        @pl.loop(0, QT)
        def _(q):
            both = jnp.dot(y_ref[q, rows], table_ref[q], preferred_element_type=jnp.float32)
            spec_ref[q, 0, rows] = both[:, :128]
            spec_ref[q, 1, rows] = both[:, 128:]

    second_stage(pl.ds(HALF, BLK))

    pl.semaphore_wait(barrier, NDEV - 1)
    after, before = wrap(me + 1, NDEV), wrap(me + NDEV - 1, NDEV)
    to_after = copy_to(
        x_ref.at[pl.ds(BLK - HALF, HALF)], halo_ref.at[0], halo_send.at[0], halo_recv.at[0],
        (after // 32, wrap(after, 32)),
    )
    to_before = copy_to(
        x_ref.at[pl.ds(0, HALF)], halo_ref.at[1], halo_send.at[1], halo_recv.at[1],
        (before // 32, wrap(before, 32)),
    )
    to_after.start()
    to_before.start()

    def take_halo():
        to_after.wait()
        to_before.wait()

        @pl.loop(0, 2)
        def _(side):
            edge = jnp.where(side == 0, me > 0, me < NDEV - 1).astype(jnp.float32)
            to = pl.ds(pl.multiple_of(side * (BLK + HALF), 16), 16)
            first_stage(
                [halo_ref[side, :, a * 128 : (a + 1) * 128].astype(jnp.float32) * edge for a in range(32)],
                y_ref,
                to,
            )

        second_stage(pl.ds(0, HALF))
        second_stage(pl.ds(BLK + HALF, HALF))

    lanes = lax.broadcasted_iota(jnp.int32, (CHUNK, 128), 1)
    low = lanes < 64
    k2 = lanes & 63
    sign = 1 - 2 * core
    mine = channel_of(x, z, y, core)
    somewhere = (x, lax.axis_index("shard") + 1 - 2 * core)
    others = pl.ds(0, NDEV - 1)

    @pl.loop(0, 4)
    def _(turn):
        pl.when(turn == 2)(take_halo)
        ahead = jnp.where(turn < 2, 1 + turn, 3 * turn - 6)
        chunk = jnp.where(core == 0, ahead, 3 - ahead)
        first = pl.multiple_of(chunk * CHUNK, CHUNK)

        def fan(q, run):
            re = jnp.zeros((CHUNK, 128), jnp.float32)
            im = re
            for t in range(TAPS):
                tap = taps_ref[q, t : t + 1, :]
                re = re + tap * spec_ref[q, 0, pl.ds(first + t, CHUNK), :]
                im = im + tap * spec_ref[q, 1, pl.ds(first + t, CHUNK), :]
            filt_ref[q, 0] = re
            filt_ref[q, 1] = im
            run = run + jnp.where(low | (q > 0), re * re + im * im, 0.0)
            upto_ref[q] = run
            return run

        run = lax.fori_loop(0, QT, fan, jnp.zeros((CHUNK, 128), jnp.float32))

        power = filt_ref[0, 0] * filt_ref[0, 0] + filt_ref[0, 1] * filt_ref[0, 1]
        sums = run + jnp.where(low, 0.0, power)
        swapped = pltpu.roll(sums, 64, 1)
        total = sums + swapped
        run_ref[1] = total
        run_ref[2] = (
            total
            + jnp.where(k2 >= 1, pltpu.roll(total, 1, 1), 0.0)
            + jnp.where(k2 <= 62, pltpu.roll(total, 127, 1), 0.0)
        )
        run_ref[3] = jnp.where(low, power, sums)
        run_ref[4] = jnp.where(low, total, swapped + power)

        @pl.loop(0, QT, unroll=2)
        def _(q):
            re, im = filt_ref[q, 0], filt_ref[q, 1]
            upto = jnp.where(q == 0, run_ref[3], upto_ref[q])
            rest = jnp.where(q == 0, run_ref[4], jnp.maximum(run_ref[1] - upto_ref[jnp.maximum(q - 1, 0)], 0.0))
            prefix = jnp.where(low, upto, rest)
            suffix = jnp.where(low, rest, upto)
            window = (
                run_ref[2]
                + jnp.where(k2 >= 2, pltpu.roll(suffix, 2, 1), 0.0)
                + jnp.where(k2 <= 61, pltpu.roll(prefix, 126, 1), 0.0)
            )
            scale = lax.rsqrt(window * rows_ref[2, pl.ds(q, 1), :] + EPSILON)
            cos = rows_ref[0, pl.ds(q, 1), :]
            sin = rows_ref[1, pl.ds(q, 1), :]
            rows32_ref[pl.ds(q, CHUNK, stride=32), :] = (re * cos + im * sin) * scale
            rows32_ref[pl.ds(16 + q, CHUNK, stride=32), :] = (im * cos - re * sin) * scale

        to_core, parity = chunk // 2, wrap(chunk, 2)

        @pl.loop(0, 8)
        def _(i):
            to_y2 = wrap(y // 2 + i // 4, 2)
            for dx in range(4):
                to_x = wrap(x + 4 + sign * dx, 4)
                to_z = wrap(z + 4 + sign * wrap(i + dx, 4), 4)
                to_y = 2 * to_y2 + wrap(parity + to_x + to_z, 2)
                shard = (to_z * 4 + to_y) * 2 + to_core
                channel = channel_of(to_x, to_z, to_y, to_core)
                at = pl.multiple_of((channel - first) * 32, 32)
                white_ref[channel] = rows32_ref[pl.ds(at, 32), :].astype(jnp.bfloat16)

                @pl.when(channel != mine)
                def _():
                    copy_to(
                        white_ref.at[channel], blocks_ref.at[me], block_send, block_recv, (to_x, shard)
                    ).start()

    blocks_ref[me] = white_ref[mine]

    lag_tables(coarse_ref, fine_ref)
    pick_rows(pairs_ref, pick_ref)

    @pl.loop(0, QT)
    def _(q):
        lag_rows(q, coarse_ref, fine_ref, lags_ref)

    copy_to(white_ref.at[others], blocks_ref.at[others], block_send, block_recv, somewhere).wait()

    @pl.loop(0, NDEV // 8)
    def _(d):
        eight = pl.ds(pl.multiple_of(d * 8, 8), 8)
        to = pl.ds(pl.multiple_of(d * 256, 256), 256)
        rows32_ref[to, :] = blocks_ref[eight].reshape(256, 128).astype(jnp.float32)

    def swap(part):
        some = pl.ds(part * 4, 4)
        return copy_to(own_ref.at[some], other_ref.at[some], swap_send.at[part], swap_recv.at[part], somewhere)

    @pl.loop(0, 4)
    def _(part):
        for n in range(4):
            q = part * 4 + n
            own_ref[q, :, 0:128] = rows32_ref[pl.ds(q, BLK, stride=32), :].astype(jnp.bfloat16)
            own_ref[q, :, 128:256] = rows32_ref[pl.ds(16 + q, BLK, stride=32), :].astype(jnp.bfloat16)
        swap(part).start()

    def add_part(part, half):
        rows = pl.ds(pl.multiple_of(half * 256, 256), 256)
        for n in range(4):
            q = part * 4 + n
            left = jnp.dot(pick_ref[0, rows, :], own_ref[q], preferred_element_type=jnp.float32)
            right = jnp.dot(pick_ref[1, rows, :], other_ref[q], preferred_element_type=jnp.float32)
            l_re, l_im, r_re, r_im = left[:, :128], left[:, 128:], right[:, :128], right[:, 128:]
            cross_ref[:, n * 256 : n * 256 + 128] = (l_re * r_re + l_im * r_im).astype(jnp.bfloat16)
            cross_ref[:, n * 256 + 128 : n * 256 + 256] = (l_im * r_re - l_re * r_im).astype(jnp.bfloat16)
        lags = lags_ref[pl.ds(part * 4, 4)].reshape(1024, NLAG)
        return jnp.dot(cross_ref[...], lags, preferred_element_type=jnp.float32)

    @pl.loop(0, 2)
    def _(turn):
        half = wrap(turn + y, 2)

        @pl.loop(0, 4)
        def _(part):
            pl.when(turn == 0)(lambda: swap(part).wait())
            added = add_part(part, half)
            sums_ref[...] = jnp.where(part == 0, added, sums_ref[...] + added)

        for n in range(4):
            rows32_ref[pl.ds(n, 256, stride=4), :] = sums_ref[:, n * 128 : n * 128 + 128]

        @pl.loop(0, 16)
        def _(i):
            for n in range(4):
                to_x = 2 * half + wrap(x + n, 2)
                to_y = wrap(y + i + 2 * (n // 2), 4)
                to_z = wrap(z + i // 4 + i + n, 4)
                shard = (to_z * 4 + to_y) * 2 + wrap(core + n // 2, 2)
                owner = to_x * 32 + shard
                at = pl.multiple_of((owner - 64 * half) * 16, 16)
                parts_ref[owner] = rows32_ref[pl.ds(at, 16), :].astype(jnp.bfloat16)

                @pl.when(owner != me)
                def _():
                    copy_to(parts_ref.at[owner], recv_ref.at[mine], part_send, part_recv, (to_x, shard)).start()

    recv_ref[mine] = parts_ref[me]
    copy_to(parts_ref.at[others], recv_ref.at[others], part_send, part_recv, somewhere).wait()

    @pl.loop(0, NDEV // 16)
    def _(d):
        some = pl.ds(pl.multiple_of(d * 16, 16), 16)
        to = pl.ds(pl.multiple_of(d * 256, 256), 256)
        rows32_ref[to, :] = recv_ref[some].reshape(256, 128).astype(jnp.float32)

    for p in range(4):
        weight = valid_ref[p].astype(jnp.float32) * (1.0 / math.sqrt(NB))
        for n in range(4):
            out_ref[p, :, n * 128 : n * 128 + 128] = rows32_ref[pl.ds(p * 4 + n, BLK, stride=16), :] * weight


def correlate(*operands):
    f32, bf16, i32 = jnp.float32, jnp.bfloat16, jnp.int32
    return pl.pallas_call(
        kernel,
        out_shape=jax.ShapeDtypeStruct((4, BLK, NLAG), f32),
        in_specs=[pl.BlockSpec(memory_space=pltpu.HBM)] * 6,
        out_specs=pl.BlockSpec(memory_space=pltpu.VMEM),
        scratch_shapes=[
            pltpu.VMEM((2, PAIRS), i32),
            pltpu.SMEM((NDEV,), i32),
            pltpu.SMEM((4,), i32),
            pltpu.VMEM((BLK, NT), bf16),
            pltpu.VMEM((TAPS, NB), f32),
            pltpu.VMEM((QT, 256, 256), bf16),
            pltpu.VMEM((2, HALF, NT), bf16),
            pltpu.VMEM((QT, WIDE, 256), bf16),
            pltpu.VMEM((QT, 2, WIDE, 128), f32),
            pltpu.VMEM((NB, 128), f32),
            pltpu.VMEM((QT, 40, 128), f32),
            pltpu.VMEM((QT, 2, CHUNK, 128), f32),
            pltpu.VMEM((QT, CHUNK, 128), f32),
            pltpu.VMEM((5, CHUNK, 128), f32),
            pltpu.VMEM((3, QT, 128), f32),
            pltpu.VMEM((32 * BLK, 128), f32),
            pltpu.VMEM((NDEV, 32, 128), bf16),
            pltpu.VMEM((NDEV, 32, 128), bf16),
            pltpu.VMEM((QT, NDEV, 256), bf16),
            pltpu.VMEM((QT, NDEV, 256), bf16),
            pltpu.VMEM((2, PAIRS, NDEV), bf16),
            pltpu.VMEM((256, 1024), bf16),
            pltpu.VMEM((PAIRS // 2, NLAG), f32),
            pltpu.VMEM((NDEV, 16, 128), bf16),
            pltpu.VMEM((NDEV, 16, 128), bf16),
            pltpu.VMEM((QT, 256, NLAG), bf16),
            pltpu.VMEM((2, 32, NLAG), f32),
            pltpu.VMEM((2, 64, NLAG), f32),
            pltpu.SemaphoreType.DMA((6,)),
            pltpu.SemaphoreType.DMA((2,)),
            pltpu.SemaphoreType.DMA((2,)),
            pltpu.SemaphoreType.DMA,
            pltpu.SemaphoreType.DMA,
            pltpu.SemaphoreType.DMA((4,)),
            pltpu.SemaphoreType.DMA((4,)),
            pltpu.SemaphoreType.DMA,
            pltpu.SemaphoreType.DMA,
        ],
        compiler_params=pltpu.CompilerParams(collective_id=0, has_side_effects=True, vmem_limit_bytes=48 << 20),
        name="correlate",
    )(*operands)


def body(samples, fan_taps, pair_blocks, pair_valid, coil_offsets):
    table = jnp.asarray(second_stage_table())
    operands = (pair_blocks.T, coil_offsets, pair_valid, samples.reshape(BLK, NT), fan_taps, table)
    return correlate(*(pltpu.with_memory_space_constraint(operand, pltpu.HBM) for operand in operands))


def solution(mesh):
    return jax.shard_map(
        body,
        mesh=mesh,
        in_specs=(P(AXES, None, None), P(), P(), P(AXES), P()),
        out_specs=P(AXES, None, None),
        check_vma=False,
    )
```

```python
import math

import jax
import jax.numpy as jnp
import ml_dtypes
import numpy as np
from jax import lax
from jax.experimental import pallas as pl
from jax.experimental.pallas import tpu as pltpu
from jax.sharding import PartitionSpec as P

HALF = 16
NLAG = 512
NT = 4096
NB = 2048
BLK = 128
WIDE = BLK + 2 * HALF
EPSILON = 1e-05
AXES = ("group", "shard")
NDEV = 128
PAIRS = 512
CHUNK = 32
MESH = pl.DeviceIdType.MESH
TAPS = 2 * HALF + 1
QT = 16


def residues():
    low = np.arange(QT)
    high = np.where(low == 0, 16, 32 - low)
    return low, high


def tile_bins():
    low, high = residues()
    k2 = np.arange(64)
    return np.concatenate([low[:, None] + 32 * k2, high[:, None] + 32 * k2], axis=1)


def second_stage_table():
    bins = tile_bins()
    b = np.arange(128)
    phase = 2 * np.pi * ((b[None, :, None] * bins[:, None, :]) % NT) / NT
    cos, sin = np.cos(phase), np.sin(phase)
    table = np.zeros((QT, 2, 128, 2, 128))
    conj = np.concatenate([np.ones(64), -np.ones(64)])
    table[:, 0, :, 0] = cos
    table[:, 1, :, 0] = sin * conj
    table[:, 0, :, 1] = -sin
    table[:, 1, :, 1] = cos * conj
    table[0] = 0.0
    table[0, 0, :, 0, :64] = cos[0, :, :64]
    table[0, 0, :, 1, :64] = -sin[0, :, :64]
    table[0, 1, :, 0, 64:] = cos[0, :, 64:]
    table[0, 1, :, 1, 64:] = -sin[0, :, 64:]
    return (table.reshape(QT, 256, 256) / math.sqrt(NT)).astype(ml_dtypes.bfloat16)


def real_fft(rows):
    count = len(rows)
    if count == 2:
        return [(rows[0] + rows[1], None), (rows[0] - rows[1], None)]
    even = real_fft(rows[0::2])
    odd = real_fft(rows[1::2])
    half, quarter = count // 2, count // 4
    out = [None] * (half + 1)
    out[0] = (even[0][0] + odd[0][0], None)
    out[half] = (even[0][0] - odd[0][0], None)
    out[quarter] = (even[quarter][0], -odd[quarter][0])
    for k in range(1, quarter):
        wr, wi = math.cos(2 * math.pi * k / count), -math.sin(2 * math.pi * k / count)
        o_re, o_im = odd[k]
        e_re, e_im = even[k]
        t_re = o_re * wr - o_im * wi
        t_im = o_re * wi + o_im * wr
        out[k] = (e_re + t_re, e_im + t_im)
        out[half - k] = (e_re - t_re, t_im - e_im)
    return out


def place():
    shard = lax.axis_index("shard")
    return lax.axis_index("group"), shard // 8, (shard // 2) % 4, shard % 2


def wrap(value, size):
    return lax.rem(value, size)


def signal_some(barrier, i, guard=True):
    x, z, y, core = place()
    there = (x + i // 4) % 4
    row = (z + i % 4) % 4 * 8
    for dy in range(4):
        for dc in range(2):
            shard = row + (y + dy) % 4 * 2 + (core + dc) % 2

            def signal():
                pl.semaphore_signal(barrier, inc=1, device_id=(there, shard), device_id_type=MESH)

            if guard and dy == 0 and dc == 0:
                pl.when(i > 0)(signal)
            else:
                signal()


def first_stage(rows, y_ref, at):
    freq = real_fft(rows)
    for q in range(QT):
        second = freq[16][0] if q == 0 else freq[q][1]
        y_ref[q, at, 0:128] = freq[q][0].astype(jnp.bfloat16)
        y_ref[q, at, 128:256] = second.astype(jnp.bfloat16)


def sort_taps(fan_ref, turned_ref, taps_ref):
    blank = jnp.zeros((128 - TAPS, 128), jnp.float32)

    @pl.loop(0, QT)
    def _(j):
        at = pl.ds(pl.multiple_of(j * 128, 128), 128)
        turned_ref[at, :] = jnp.concatenate([fan_ref[:, at], blank], axis=0).T

    @pl.loop(0, QT)
    def _(q):
        high = jnp.where(q == 0, 16, 32 - q)
        both = jnp.concatenate(
            [turned_ref[pl.ds(q, 64, stride=32), :], turned_ref[pl.ds(high, 64, stride=32), :]], axis=0
        )
        taps_ref[q] = both.T[:40]


def lag_tables(coarse_ref, fine_ref):
    lag = lax.broadcasted_iota(jnp.int32, (64, NLAG), 1) - NLAG // 2
    row = lax.broadcasted_iota(jnp.int32, (64, NLAG), 0)
    fine = ((32 * row * lag) & (NT - 1)).astype(jnp.float32) * (2.0 * math.pi / NT)
    coarse = ((row * lag) & (NT - 1)).astype(jnp.float32) * (2.0 * math.pi / NT)
    fine_ref[0] = jnp.cos(fine)
    fine_ref[1] = jnp.sin(fine)
    coarse_ref[0] = jnp.cos(coarse[:32])
    coarse_ref[1] = jnp.sin(coarse[:32])


def lag_rows(q, coarse_ref, fine_ref, lags_ref):
    cos_b, sin_b = fine_ref[0], fine_ref[1]
    for half, residue in ((0, q), (64, jnp.where(q == 0, 16, 32 - q))):
        cos_a, sin_a = coarse_ref[0, pl.ds(residue, 1), :], coarse_ref[1, pl.ds(residue, 1), :]
        lags_ref[q, half : half + 64] = (cos_a * cos_b - sin_a * sin_b).astype(jnp.bfloat16)
        lags_ref[q, 128 + half : 192 + half] = (-(sin_a * cos_b + cos_a * sin_b)).astype(jnp.bfloat16)


def pick_rows(planes, pairs_ref, pick_ref):
    block = lax.broadcasted_iota(jnp.int32, (128, 128), 0)
    for side in range(2):
        for n, plane in enumerate(planes):
            at = pl.ds(pl.multiple_of(plane * 128, 128), 128)
            chosen = block == pairs_ref[side : side + 1, at]
            pick_ref[side, n * 128 : n * 128 + 128, :] = jnp.where(chosen, 1.0, 0.0).T.astype(jnp.bfloat16)


def bin_rows(offset, rows_ref):
    lane = lax.broadcasted_iota(jnp.int32, (QT, 128), 1)
    tile = lax.broadcasted_iota(jnp.int32, (QT, 128), 0)
    residue = jnp.where(lane < 64, tile, jnp.where(tile == 0, 16, 32 - tile))
    bins = residue + 32 * (lane & 63)
    theta = ((bins * offset) & (NT - 1)).astype(jnp.float32) * (2.0 * math.pi / NT)
    rows_ref[0] = jnp.cos(theta)
    rows_ref[1] = jnp.sin(theta)
    count = jnp.minimum(bins + 64, NB - 1) - jnp.maximum(bins - 64, 0) + 1
    rows_ref[2] = 1.0 / count.astype(jnp.float32)


def copy_to(src, dst, send_sem, recv_sem, device):
    return pltpu.make_async_remote_copy(
        src_ref=src, dst_ref=dst, send_sem=send_sem, recv_sem=recv_sem, device_id=device, device_id_type=MESH
    )


def channel_of(x, z, y, core):
    return wrap(x + z + y, 2) * 32 + (x * 16 + z * 4 + y) // 2 + 64 * core


def kernel(
    pairs_hbm, offsets_hbm, valid_hbm, x_hbm, fan_hbm, table_hbm, out_ref,
    pairs_ref, offsets_ref, valid_ref, x_ref, fan_ref, table_ref,
    halo_ref, y_ref, y_halo_ref, spec_ref, turned_ref, taps_ref, filt_ref, upto_ref, run_ref, rows_ref,
    rows32_ref, white_ref, blocks_ref, own_ref, other_ref, pick_ref, cross_ref, sums_ref,
    parts_ref, recv_ref, lags_ref, coarse_ref, fine_ref,
    fetch_sem, halo_send, halo_recv, block_send, block_recv, swap_send, swap_recv, part_send, part_recv,
):
    x, z, y, core = place()
    me = lax.axis_index("group") * 32 + lax.axis_index("shard")
    barrier = pltpu.get_barrier_semaphore()
    moves = (
        (x_hbm, x_ref), (offsets_hbm, offsets_ref), (fan_hbm, fan_ref),
        (pairs_hbm, pairs_ref), (valid_hbm, valid_ref), (table_hbm, table_ref),
    )
    fetches = [pltpu.make_async_copy(src, dst, fetch_sem.at[n]) for n, (src, dst) in enumerate(moves)]
    for fetch in fetches:
        fetch.start()

    @pl.loop(0, 8)
    def _(column):
        signal_some(barrier, column)

    fetches[0].wait()

    @pl.loop(0, 8)
    def _(chunk):
        signal_some(barrier, chunk + 8, False)
        at = pl.ds(pl.multiple_of(chunk * 16, 16), 16)
        first_stage([x_ref[at, a * 128 : (a + 1) * 128].astype(jnp.float32) for a in range(32)], y_ref, at)

    for fetch in fetches[1:]:
        fetch.wait()
    sort_taps(fan_ref, turned_ref, taps_ref)
    bin_rows(offsets_ref[me], rows_ref)

    @pl.loop(0, QT // 4)
    def _(group):
        for n in range(4):
            q = group * 4 + n
            both = jnp.dot(y_ref[q], table_ref[q], preferred_element_type=jnp.float32)
            spec_ref[q, 0, HALF : HALF + BLK] = both[:, :128]
            spec_ref[q, 1, HALF : HALF + BLK] = both[:, 128:]

    pl.semaphore_wait(barrier, NDEV - 1)
    after, before = wrap(me + 1, NDEV), wrap(me + NDEV - 1, NDEV)
    to_after = copy_to(
        x_ref.at[pl.ds(BLK - HALF, HALF)], halo_ref.at[0], halo_send.at[0], halo_recv.at[0],
        (after // 32, wrap(after, 32)),
    )
    to_before = copy_to(
        x_ref.at[pl.ds(0, HALF)], halo_ref.at[1], halo_send.at[1], halo_recv.at[1],
        (before // 32, wrap(before, 32)),
    )
    to_after.start()
    to_before.start()

    def take_halo():
        to_after.wait()
        to_before.wait()

        @pl.loop(0, 2)
        def _(side):
            edge = jnp.where(side == 0, me > 0, me < NDEV - 1).astype(jnp.float32)
            to = pl.ds(pl.multiple_of(side * HALF, HALF), HALF)
            first_stage(
                [halo_ref[side, :, a * 128 : (a + 1) * 128].astype(jnp.float32) * edge for a in range(32)],
                y_halo_ref,
                to,
            )

        @pl.loop(0, QT // 4)
        def _(group):
            for n in range(4):
                q = group * 4 + n
                both = jnp.dot(y_halo_ref[q], table_ref[q], preferred_element_type=jnp.float32)
                for r in range(2):
                    spec_ref[q, r, 0:HALF] = both[:HALF, r * 128 : r * 128 + 128]
                    spec_ref[q, r, HALF + BLK : WIDE] = both[HALF:, r * 128 : r * 128 + 128]

    lanes = lax.broadcasted_iota(jnp.int32, (CHUNK, 128), 1)
    low = lanes < 64
    k2 = lanes & 63
    sign = 1 - 2 * core
    mine = channel_of(x, z, y, core)
    somewhere = (x, lax.axis_index("shard") + 1 - 2 * core)
    others = pl.ds(0, NDEV - 1)
    xs = [wrap(x + 4 + sign * n, 4) for n in range(4)]
    zs = [wrap(z + 4 + sign * n, 4) for n in range(4)]
    ys = [wrap(y // 2 + n, 2) for n in range(2)]

    @pl.loop(0, 4)
    def _(turn):
        pl.when(turn == 2)(take_halo)
        ahead = jnp.where(turn < 2, 1 + turn, 3 * turn - 6)
        chunk = jnp.where(core == 0, ahead, 3 - ahead)
        first = pl.multiple_of(chunk * CHUNK, CHUNK)

        def fan(q, run):
            re = jnp.zeros((CHUNK, 128), jnp.float32)
            im = re
            for t in range(TAPS):
                tap = taps_ref[q, t : t + 1, :]
                re = re + tap * spec_ref[q, 0, pl.ds(first + t, CHUNK), :]
                im = im + tap * spec_ref[q, 1, pl.ds(first + t, CHUNK), :]
            filt_ref[q, 0] = re
            filt_ref[q, 1] = im
            run = run + jnp.where(low | (q > 0), re * re + im * im, 0.0)
            upto_ref[q] = run
            return run

        run = lax.fori_loop(0, QT, fan, jnp.zeros((CHUNK, 128), jnp.float32))

        power = filt_ref[0, 0] * filt_ref[0, 0] + filt_ref[0, 1] * filt_ref[0, 1]
        sums = run + jnp.where(low, 0.0, power)
        swapped = pltpu.roll(sums, 64, 1)
        total = sums + swapped
        run_ref[1] = total
        run_ref[2] = (
            total
            + jnp.where(k2 >= 1, pltpu.roll(total, 1, 1), 0.0)
            + jnp.where(k2 <= 62, pltpu.roll(total, 127, 1), 0.0)
        )
        run_ref[3] = jnp.where(low, power, sums)
        run_ref[4] = jnp.where(low, total, swapped + power)

        @pl.loop(0, QT, unroll=2)
        def _(q):
            re, im = filt_ref[q, 0], filt_ref[q, 1]
            upto = jnp.where(q == 0, run_ref[3], upto_ref[q])
            rest = jnp.where(q == 0, run_ref[4], jnp.maximum(run_ref[1] - upto_ref[jnp.maximum(q - 1, 0)], 0.0))
            prefix = jnp.where(low, upto, rest)
            suffix = jnp.where(low, rest, upto)
            window = (
                run_ref[2]
                + jnp.where(k2 >= 2, pltpu.roll(suffix, 2, 1), 0.0)
                + jnp.where(k2 <= 61, pltpu.roll(prefix, 126, 1), 0.0)
            )
            scale = lax.rsqrt(window * rows_ref[2, pl.ds(q, 1), :] + EPSILON)
            cos = rows_ref[0, pl.ds(q, 1), :]
            sin = rows_ref[1, pl.ds(q, 1), :]
            rows32_ref[pl.ds(q, CHUNK, stride=32), :] = (re * cos + im * sin) * scale
            rows32_ref[pl.ds(16 + q, CHUNK, stride=32), :] = (im * cos - re * sin) * scale

        to_core, parity = chunk // 2, wrap(chunk, 2)
        for n in range(32):
            to_x, to_z, to_y2 = xs[n % 4], zs[(n // 4 + n) % 4], ys[n // 16]
            shard = to_z * 8 + to_y2 * 4 + 2 * wrap(parity + to_x + to_z, 2) + to_core
            row = to_x * 8 + to_z * 2 + to_y2
            white_ref[first + row] = rows32_ref[pl.ds(pl.multiple_of(row * 32, 32), 32), :].astype(jnp.bfloat16)
            push = copy_to(
                white_ref.at[first + row], blocks_ref.at[me], block_send, block_recv, (to_x, shard)
            ).start
            if n == 0:
                pl.when(first + row != mine)(push)
            else:
                push()

    blocks_ref[me] = white_ref[mine]

    lag_tables(coarse_ref, fine_ref)
    pick_rows(xs, pairs_ref, pick_ref)

    @pl.loop(0, QT)
    def _(q):
        lag_rows(q, coarse_ref, fine_ref, lags_ref)

    copy_to(white_ref.at[others], blocks_ref.at[others], block_send, block_recv, somewhere).wait()

    @pl.loop(0, NDEV // 8)
    def _(d):
        eight = pl.ds(pl.multiple_of(d * 8, 8), 8)
        to = pl.ds(pl.multiple_of(d * 256, 256), 256)
        rows32_ref[to, :] = blocks_ref[eight].reshape(256, 128).astype(jnp.float32)

    def swap(part):
        some = pl.ds(part * 4, 4)
        return copy_to(own_ref.at[some], other_ref.at[some], swap_send.at[part], swap_recv.at[part], somewhere)

    @pl.loop(0, 4)
    def _(part):
        for n in range(4):
            q = part * 4 + n
            own_ref[q, :, 0:128] = rows32_ref[pl.ds(q, BLK, stride=32), :].astype(jnp.bfloat16)
            own_ref[q, :, 128:256] = rows32_ref[pl.ds(16 + q, BLK, stride=32), :].astype(jnp.bfloat16)
        swap(part).start()

    def add_part(part, half):
        rows = pl.ds(pl.multiple_of(half * 256, 256), 256)
        for n in range(4):
            q = part * 4 + n
            left = jnp.dot(pick_ref[0, rows, :], own_ref[q], preferred_element_type=jnp.float32)
            right = jnp.dot(pick_ref[1, rows, :], other_ref[q], preferred_element_type=jnp.float32)
            l_re, l_im, r_re, r_im = left[:, :128], left[:, 128:], right[:, :128], right[:, 128:]
            cross_ref[:, n * 256 : n * 256 + 128] = (l_re * r_re + l_im * r_im).astype(jnp.bfloat16)
            cross_ref[:, n * 256 + 128 : n * 256 + 256] = (l_im * r_re - l_re * r_im).astype(jnp.bfloat16)
        lags = lags_ref[pl.ds(part * 4, 4)].reshape(1024, NLAG)
        return jnp.dot(cross_ref[...], lags, preferred_element_type=jnp.float32)

    @pl.loop(0, 2)
    def _(turn):
        @pl.loop(0, 4)
        def _(part):
            pl.when(turn == 0)(lambda: swap(part).wait())
            added = add_part(part, turn)
            sums_ref[...] = jnp.where(part == 0, added, sums_ref[...] + added)

        for n in range(4):
            rows32_ref[pl.ds(n, 256, stride=4), :] = sums_ref[:, n * 128 : n * 128 + 128]

        planes = [wrap(x + 4 + sign * (2 * turn + n), 4) for n in range(2)]

        @pl.loop(0, 4)
        def _(i):
            for n in range(16):
                to_core = core if n < 8 else 1 - core
                shard = zs[n // 2 % 4] * 8 + wrap(y + i + n, 4) * 2 + to_core
                row = n % 2 * 32 + shard
                slot = turn * 64 + row
                parts_ref[slot] = rows32_ref[pl.ds(pl.multiple_of(row * 16, 16), 16), :].astype(jnp.bfloat16)
                push = copy_to(
                    parts_ref.at[slot], recv_ref.at[mine], part_send, part_recv, (planes[n % 2], shard)
                ).start
                if n == 0:
                    pl.when(turn + i > 0)(push)
                else:
                    push()

    recv_ref[mine] = parts_ref[lax.axis_index("shard")]
    copy_to(parts_ref.at[others], recv_ref.at[others], part_send, part_recv, somewhere).wait()

    @pl.loop(0, NDEV // 16)
    def _(d):
        some = pl.ds(pl.multiple_of(d * 16, 16), 16)
        to = pl.ds(pl.multiple_of(d * 256, 256), 256)
        rows32_ref[to, :] = recv_ref[some].reshape(256, 128).astype(jnp.float32)

    for p in range(4):
        weight = valid_ref[p].astype(jnp.float32) * (1.0 / math.sqrt(NB))
        for n in range(4):
            out_ref[p, :, n * 128 : n * 128 + 128] = rows32_ref[pl.ds(p * 4 + n, BLK, stride=16), :] * weight


def correlate(*operands):
    f32, bf16, i32 = jnp.float32, jnp.bfloat16, jnp.int32
    return pl.pallas_call(
        kernel,
        out_shape=jax.ShapeDtypeStruct((4, BLK, NLAG), f32),
        in_specs=[pl.BlockSpec(memory_space=pltpu.HBM)] * 6,
        out_specs=pl.BlockSpec(memory_space=pltpu.VMEM),
        scratch_shapes=[
            pltpu.VMEM((2, PAIRS), i32),
            pltpu.SMEM((NDEV,), i32),
            pltpu.SMEM((4,), i32),
            pltpu.VMEM((BLK, NT), bf16),
            pltpu.VMEM((TAPS, NB), f32),
            pltpu.VMEM((QT, 256, 256), bf16),
            pltpu.VMEM((2, HALF, NT), bf16),
            pltpu.VMEM((QT, BLK, 256), bf16),
            pltpu.VMEM((QT, 2 * HALF, 256), bf16),
            pltpu.VMEM((QT, 2, WIDE, 128), f32),
            pltpu.VMEM((NB, 128), f32),
            pltpu.VMEM((QT, 40, 128), f32),
            pltpu.VMEM((QT, 2, CHUNK, 128), f32),
            pltpu.VMEM((QT, CHUNK, 128), f32),
            pltpu.VMEM((5, CHUNK, 128), f32),
            pltpu.VMEM((3, QT, 128), f32),
            pltpu.VMEM((32 * BLK, 128), f32),
            pltpu.VMEM((NDEV, 32, 128), bf16),
            pltpu.VMEM((NDEV, 32, 128), bf16),
            pltpu.VMEM((QT, NDEV, 256), bf16),
            pltpu.VMEM((QT, NDEV, 256), bf16),
            pltpu.VMEM((2, PAIRS, NDEV), bf16),
            pltpu.VMEM((256, 1024), bf16),
            pltpu.VMEM((PAIRS // 2, NLAG), f32),
            pltpu.VMEM((NDEV, 16, 128), bf16),
            pltpu.VMEM((NDEV, 16, 128), bf16),
            pltpu.VMEM((QT, 256, NLAG), bf16),
            pltpu.VMEM((2, 32, NLAG), f32),
            pltpu.VMEM((2, 64, NLAG), f32),
            pltpu.SemaphoreType.DMA((6,)),
            pltpu.SemaphoreType.DMA((2,)),
            pltpu.SemaphoreType.DMA((2,)),
            pltpu.SemaphoreType.DMA,
            pltpu.SemaphoreType.DMA,
            pltpu.SemaphoreType.DMA((4,)),
            pltpu.SemaphoreType.DMA((4,)),
            pltpu.SemaphoreType.DMA,
            pltpu.SemaphoreType.DMA,
        ],
        compiler_params=pltpu.CompilerParams(collective_id=0, has_side_effects=True, vmem_limit_bytes=48 << 20),
        name="correlate",
    )(*operands)


def body(samples, fan_taps, pair_blocks, pair_valid, coil_offsets):
    table = jnp.asarray(second_stage_table())
    operands = (pair_blocks.T, coil_offsets, pair_valid, samples.reshape(BLK, NT), fan_taps, table)
    return correlate(*(pltpu.with_memory_space_constraint(operand, pltpu.HBM) for operand in operands))


def solution(mesh):
    return jax.shard_map(
        body,
        mesh=mesh,
        in_specs=(P(AXES, None, None), P(), P(), P(AXES), P()),
        out_specs=P(AXES, None, None),
        check_vma=False,
    )
```

```python
import math

import jax
import jax.numpy as jnp
import ml_dtypes
import numpy as np
from jax import lax
from jax.experimental import pallas as pl
from jax.experimental.pallas import tpu as pltpu
from jax.sharding import PartitionSpec as P

HALF = 16
NLAG = 512
NT = 4096
NB = 2048
BLK = 128
WIDE = BLK + 2 * HALF
EPSILON = 1e-05
AXES = ("group", "shard")
NDEV = 128
PAIRS = 512
CHUNK = 32
MESH = pl.DeviceIdType.MESH
TAPS = 2 * HALF + 1
QT = 16


def residues():
    low = np.arange(QT)
    high = np.where(low == 0, 16, 32 - low)
    return low, high


def tile_bins():
    low, high = residues()
    k2 = np.arange(64)
    return np.concatenate([low[:, None] + 32 * k2, high[:, None] + 32 * k2], axis=1)


def second_stage_table():
    bins = tile_bins()
    b = np.arange(128)
    phase = 2 * np.pi * ((b[None, :, None] * bins[:, None, :]) % NT) / NT
    cos, sin = np.cos(phase), np.sin(phase)
    table = np.zeros((QT, 2, 128, 2, 128))
    conj = np.concatenate([np.ones(64), -np.ones(64)])
    table[:, 0, :, 0] = cos
    table[:, 1, :, 0] = sin * conj
    table[:, 0, :, 1] = -sin
    table[:, 1, :, 1] = cos * conj
    table[0] = 0.0
    table[0, 0, :, 0, :64] = cos[0, :, :64]
    table[0, 0, :, 1, :64] = -sin[0, :, :64]
    table[0, 1, :, 0, 64:] = cos[0, :, 64:]
    table[0, 1, :, 1, 64:] = -sin[0, :, 64:]
    return (table.reshape(QT, 256, 256) / math.sqrt(NT)).astype(ml_dtypes.bfloat16)


def real_fft(rows):
    count = len(rows)
    if count == 2:
        return [(rows[0] + rows[1], None), (rows[0] - rows[1], None)]
    even = real_fft(rows[0::2])
    odd = real_fft(rows[1::2])
    half, quarter = count // 2, count // 4
    out = [None] * (half + 1)
    out[0] = (even[0][0] + odd[0][0], None)
    out[half] = (even[0][0] - odd[0][0], None)
    out[quarter] = (even[quarter][0], -odd[quarter][0])
    for k in range(1, quarter):
        wr, wi = math.cos(2 * math.pi * k / count), -math.sin(2 * math.pi * k / count)
        o_re, o_im = odd[k]
        e_re, e_im = even[k]
        t_re = o_re * wr - o_im * wi
        t_im = o_re * wi + o_im * wr
        out[k] = (e_re + t_re, e_im + t_im)
        out[half - k] = (e_re - t_re, t_im - e_im)
    return out


def place():
    shard = lax.axis_index("shard")
    return lax.axis_index("group"), shard // 8, (shard // 2) % 4, shard % 2


def wrap(value, size):
    return lax.rem(value, size)


def signal_some(barrier, i, guard=True):
    x, z, y, core = place()
    there = (x + i // 4) % 4
    row = (z + i % 4) % 4 * 8
    for dy in range(4):
        for dc in range(2):
            shard = row + (y + dy) % 4 * 2 + (core + dc) % 2

            def signal():
                pl.semaphore_signal(barrier, inc=1, device_id=(there, shard), device_id_type=MESH)

            if guard and dy == 0 and dc == 0:
                pl.when(i > 0)(signal)
            else:
                signal()


def first_stage(rows, y_ref, at):
    freq = real_fft(rows)
    for q in range(QT):
        second = freq[16][0] if q == 0 else freq[q][1]
        y_ref[q, at, 0:128] = freq[q][0].astype(jnp.bfloat16)
        y_ref[q, at, 128:256] = second.astype(jnp.bfloat16)


def sort_taps(fan_ref, turned_ref, taps_ref):
    blank = jnp.zeros((128 - TAPS, 128), jnp.float32)

    @pl.loop(0, QT)
    def _(j):
        at = pl.ds(pl.multiple_of(j * 128, 128), 128)
        turned_ref[at, :] = jnp.concatenate([fan_ref[:, at], blank], axis=0).T

    @pl.loop(0, QT)
    def _(q):
        high = jnp.where(q == 0, 16, 32 - q)
        both = jnp.concatenate(
            [turned_ref[pl.ds(q, 64, stride=32), :], turned_ref[pl.ds(high, 64, stride=32), :]], axis=0
        )
        taps_ref[q] = both.T[:40]


def lag_tables(coarse_ref, fine_ref):
    lag = lax.broadcasted_iota(jnp.int32, (64, NLAG), 1) - NLAG // 2
    row = lax.broadcasted_iota(jnp.int32, (64, NLAG), 0)
    fine = ((32 * row * lag) & (NT - 1)).astype(jnp.float32) * (2.0 * math.pi / NT)
    coarse = ((row * lag) & (NT - 1)).astype(jnp.float32) * (2.0 * math.pi / NT)
    fine_ref[0] = jnp.cos(fine)
    fine_ref[1] = jnp.sin(fine)
    coarse_ref[0] = jnp.cos(coarse[:32])
    coarse_ref[1] = jnp.sin(coarse[:32])


def lag_rows(q, coarse_ref, fine_ref, lags_ref):
    cos_b, sin_b = fine_ref[0], fine_ref[1]
    for half, residue in ((0, q), (64, jnp.where(q == 0, 16, 32 - q))):
        cos_a, sin_a = coarse_ref[0, pl.ds(residue, 1), :], coarse_ref[1, pl.ds(residue, 1), :]
        lags_ref[q, half : half + 64] = (cos_a * cos_b - sin_a * sin_b).astype(jnp.bfloat16)
        lags_ref[q, 128 + half : 192 + half] = (-(sin_a * cos_b + cos_a * sin_b)).astype(jnp.bfloat16)


def pick_rows(planes, pairs_ref, pick_ref):
    block = lax.broadcasted_iota(jnp.int32, (128, 128), 0)
    for side in range(2):
        for n, plane in enumerate(planes):
            at = pl.ds(pl.multiple_of(plane * 128, 128), 128)
            chosen = block == pairs_ref[side : side + 1, at]
            pick_ref[side, n * 128 : n * 128 + 128, :] = jnp.where(chosen, 1.0, 0.0).T.astype(jnp.bfloat16)


def bin_rows(offset, rows_ref):
    lane = lax.broadcasted_iota(jnp.int32, (QT, 128), 1)
    tile = lax.broadcasted_iota(jnp.int32, (QT, 128), 0)
    residue = jnp.where(lane < 64, tile, jnp.where(tile == 0, 16, 32 - tile))
    bins = residue + 32 * (lane & 63)
    theta = ((bins * offset) & (NT - 1)).astype(jnp.float32) * (2.0 * math.pi / NT)
    rows_ref[0] = jnp.cos(theta)
    rows_ref[1] = jnp.sin(theta)
    count = jnp.minimum(bins + 64, NB - 1) - jnp.maximum(bins - 64, 0) + 1
    rows_ref[2] = 1.0 / count.astype(jnp.float32)


def copy_to(src, dst, send_sem, recv_sem, device):
    return pltpu.make_async_remote_copy(
        src_ref=src, dst_ref=dst, send_sem=send_sem, recv_sem=recv_sem, device_id=device, device_id_type=MESH
    )


def channel_of(x, z, y, core):
    return wrap(x + z + y, 2) * 32 + (x * 16 + z * 4 + y) // 2 + 64 * core


def kernel(
    pairs_hbm, offsets_hbm, valid_hbm, x_hbm, fan_hbm, table_hbm, out_ref,
    pairs_ref, offsets_ref, valid_ref, x_ref, fan_ref, table_ref,
    halo_ref, y_ref, y_halo_ref, spec_ref, turned_ref, taps_ref, filt_ref, upto_ref, run_ref, rows_ref,
    rows32_ref, white_ref, blocks_ref, own_ref, other_ref, pick_ref, cross_ref, sums_ref,
    parts_ref, recv_ref, lags_ref, coarse_ref, fine_ref,
    fetch_sem, halo_send, halo_recv, block_send, block_recv, swap_send, swap_recv, part_send, part_recv,
):
    x, z, y, core = place()
    me = lax.axis_index("group") * 32 + lax.axis_index("shard")
    barrier = pltpu.get_barrier_semaphore()
    moves = (
        (x_hbm, x_ref), (offsets_hbm, offsets_ref), (fan_hbm, fan_ref),
        (pairs_hbm, pairs_ref), (valid_hbm, valid_ref), (table_hbm, table_ref),
    )
    fetches = [pltpu.make_async_copy(src, dst, fetch_sem.at[n]) for n, (src, dst) in enumerate(moves)]
    for fetch in fetches:
        fetch.start()

    @pl.loop(0, 8)
    def _(column):
        signal_some(barrier, column)

    fetches[0].wait()

    @pl.loop(0, 8)
    def _(chunk):
        signal_some(barrier, chunk + 8, False)
        at = pl.ds(pl.multiple_of(chunk * 16, 16), 16)
        first_stage([x_ref[at, a * 128 : (a + 1) * 128].astype(jnp.float32) for a in range(32)], y_ref, at)

    for fetch in fetches[1:]:
        fetch.wait()
    sort_taps(fan_ref, turned_ref, taps_ref)
    bin_rows(offsets_ref[me], rows_ref)

    @pl.loop(0, QT // 4)
    def _(group):
        for n in range(4):
            q = group * 4 + n
            both = jnp.dot(y_ref[q], table_ref[q], preferred_element_type=jnp.float32)
            spec_ref[q, 0, HALF : HALF + BLK] = both[:, :128]
            spec_ref[q, 1, HALF : HALF + BLK] = both[:, 128:]

    pl.semaphore_wait(barrier, NDEV - 1)
    after, before = wrap(me + 1, NDEV), wrap(me + NDEV - 1, NDEV)
    to_after = copy_to(
        x_ref.at[pl.ds(BLK - HALF, HALF)], halo_ref.at[0], halo_send.at[0], halo_recv.at[0],
        (after // 32, wrap(after, 32)),
    )
    to_before = copy_to(
        x_ref.at[pl.ds(0, HALF)], halo_ref.at[1], halo_send.at[1], halo_recv.at[1],
        (before // 32, wrap(before, 32)),
    )
    to_after.start()
    to_before.start()

    def take_halo():
        to_after.wait()
        to_before.wait()

        @pl.loop(0, 2)
        def _(side):
            edge = jnp.where(side == 0, me > 0, me < NDEV - 1).astype(jnp.float32)
            to = pl.ds(pl.multiple_of(side * HALF, HALF), HALF)
            first_stage(
                [halo_ref[side, :, a * 128 : (a + 1) * 128].astype(jnp.float32) * edge for a in range(32)],
                y_halo_ref,
                to,
            )

        @pl.loop(0, QT // 4)
        def _(group):
            for n in range(4):
                q = group * 4 + n
                both = jnp.dot(y_halo_ref[q], table_ref[q], preferred_element_type=jnp.float32)
                for r in range(2):
                    spec_ref[q, r, 0:HALF] = both[:HALF, r * 128 : r * 128 + 128]
                    spec_ref[q, r, HALF + BLK : WIDE] = both[HALF:, r * 128 : r * 128 + 128]

    lanes = lax.broadcasted_iota(jnp.int32, (CHUNK, 128), 1)
    low = lanes < 64
    k2 = lanes & 63
    sign = 1 - 2 * core
    mine = channel_of(x, z, y, core)
    somewhere = (x, lax.axis_index("shard") + 1 - 2 * core)
    others = pl.ds(0, NDEV - 1)
    xs = [wrap(x + 4 + sign * n, 4) for n in range(4)]
    zs = [wrap(z + 4 + sign * n, 4) for n in range(4)]
    ys = [wrap(y // 2 + n, 2) for n in range(2)]

    @pl.loop(0, 4)
    def _(turn):
        pl.when(turn == 2)(take_halo)
        ahead = jnp.where(turn < 2, 1 + turn, 3 * turn - 6)
        chunk = jnp.where(core == 0, ahead, 3 - ahead)
        first = pl.multiple_of(chunk * CHUNK, CHUNK)

        def fan(q, run):
            re = jnp.zeros((CHUNK, 128), jnp.float32)
            im = re
            for t in range(TAPS):
                tap = taps_ref[q, t : t + 1, :]
                re = re + tap * spec_ref[q, 0, pl.ds(first + t, CHUNK), :]
                im = im + tap * spec_ref[q, 1, pl.ds(first + t, CHUNK), :]
            filt_ref[q, 0] = re
            filt_ref[q, 1] = im
            run = run + jnp.where(low | (q > 0), re * re + im * im, 0.0)
            upto_ref[q] = run
            return run

        run = lax.fori_loop(0, QT, fan, jnp.zeros((CHUNK, 128), jnp.float32))

        power = filt_ref[0, 0] * filt_ref[0, 0] + filt_ref[0, 1] * filt_ref[0, 1]
        sums = run + jnp.where(low, 0.0, power)
        swapped = pltpu.roll(sums, 64, 1)
        total = sums + swapped
        run_ref[1] = total
        run_ref[2] = (
            total
            + jnp.where(k2 >= 1, pltpu.roll(total, 1, 1), 0.0)
            + jnp.where(k2 <= 62, pltpu.roll(total, 127, 1), 0.0)
        )
        run_ref[3] = jnp.where(low, power, sums)
        run_ref[4] = jnp.where(low, total, swapped + power)

        @pl.loop(0, QT, unroll=2)
        def _(q):
            re, im = filt_ref[q, 0], filt_ref[q, 1]
            upto = jnp.where(q == 0, run_ref[3], upto_ref[q])
            rest = jnp.where(q == 0, run_ref[4], jnp.maximum(run_ref[1] - upto_ref[jnp.maximum(q - 1, 0)], 0.0))
            prefix = jnp.where(low, upto, rest)
            suffix = jnp.where(low, rest, upto)
            window = (
                run_ref[2]
                + jnp.where(k2 >= 2, pltpu.roll(suffix, 2, 1), 0.0)
                + jnp.where(k2 <= 61, pltpu.roll(prefix, 126, 1), 0.0)
            )
            scale = lax.rsqrt(window * rows_ref[2, pl.ds(q, 1), :] + EPSILON)
            cos = rows_ref[0, pl.ds(q, 1), :]
            sin = rows_ref[1, pl.ds(q, 1), :]
            rows32_ref[pl.ds(q, CHUNK, stride=33), :] = (re * cos + im * sin) * scale
            rows32_ref[pl.ds(16 + q, CHUNK, stride=33), :] = (im * cos - re * sin) * scale

        to_core, parity = chunk // 2, wrap(chunk, 2)
        for n in range(32):
            to_x, to_z, to_y2 = xs[n % 4], zs[(n // 4 + n) % 4], ys[n // 16]
            shard = to_z * 8 + to_y2 * 4 + 2 * wrap(parity + to_x + to_z, 2) + to_core
            row = to_x * 8 + to_z * 2 + to_y2
            white_ref[first + row] = rows32_ref[pl.ds(row * 33, 32), :].astype(jnp.bfloat16)
            push = copy_to(
                white_ref.at[first + row], blocks_ref.at[me], block_send, block_recv, (to_x, shard)
            ).start
            if n == 0:
                pl.when(first + row != mine)(push)
            else:
                push()

    blocks_ref[me] = white_ref[mine]

    lag_tables(coarse_ref, fine_ref)
    pick_rows(xs, pairs_ref, pick_ref)

    @pl.loop(0, QT)
    def _(q):
        lag_rows(q, coarse_ref, fine_ref, lags_ref)

    copy_to(white_ref.at[others], blocks_ref.at[others], block_send, block_recv, somewhere).wait()

    @pl.loop(0, NDEV // 8)
    def _(d):
        for n in range(8):
            rows32_ref[pl.ds((d * 8 + n) * 33, 32), :] = blocks_ref[d * 8 + n].astype(jnp.float32)

    def swap(part):
        some = pl.ds(part * 4, 4)
        return copy_to(own_ref.at[some], other_ref.at[some], swap_send.at[part], swap_recv.at[part], somewhere)

    @pl.loop(0, 4)
    def _(part):
        for n in range(4):
            q = part * 4 + n
            own_ref[q, :, 0:128] = rows32_ref[pl.ds(q, BLK, stride=33), :].astype(jnp.bfloat16)
            own_ref[q, :, 128:256] = rows32_ref[pl.ds(16 + q, BLK, stride=33), :].astype(jnp.bfloat16)
        swap(part).start()

    def add_part(part, half):
        rows = pl.ds(pl.multiple_of(half * 256, 256), 256)
        for n in range(4):
            q = part * 4 + n
            left = jnp.dot(pick_ref[0, rows, :], own_ref[q], preferred_element_type=jnp.float32)
            right = jnp.dot(pick_ref[1, rows, :], other_ref[q], preferred_element_type=jnp.float32)
            l_re, l_im, r_re, r_im = left[:, :128], left[:, 128:], right[:, :128], right[:, 128:]
            cross_ref[:, n * 256 : n * 256 + 128] = (l_re * r_re + l_im * r_im).astype(jnp.bfloat16)
            cross_ref[:, n * 256 + 128 : n * 256 + 256] = (l_im * r_re - l_re * r_im).astype(jnp.bfloat16)
        lags = lags_ref[pl.ds(part * 4, 4)].reshape(1024, NLAG)
        return jnp.dot(cross_ref[...], lags, preferred_element_type=jnp.float32)

    @pl.loop(0, 2)
    def _(turn):
        @pl.loop(0, 4)
        def _(part):
            pl.when(turn == 0)(lambda: swap(part).wait())
            added = add_part(part, turn)
            sums_ref[...] = jnp.where(part == 0, added, sums_ref[...] + added)

        for n in range(4):
            rows32_ref[pl.ds(n, 256, stride=4), :] = sums_ref[:, n * 128 : n * 128 + 128]

        planes = [wrap(x + 4 + sign * (2 * turn + n), 4) for n in range(2)]

        @pl.loop(0, 4)
        def _(i):
            for n in range(16):
                to_core = core if n < 8 else 1 - core
                shard = zs[n // 2 % 4] * 8 + wrap(y + i + n, 4) * 2 + to_core
                row = n % 2 * 32 + shard
                slot = turn * 64 + row
                parts_ref[slot] = rows32_ref[pl.ds(pl.multiple_of(row * 16, 16), 16), :].astype(jnp.bfloat16)
                push = copy_to(
                    parts_ref.at[slot], recv_ref.at[mine], part_send, part_recv, (planes[n % 2], shard)
                ).start
                if n == 0:
                    pl.when(turn + i > 0)(push)
                else:
                    push()

    recv_ref[mine] = parts_ref[lax.axis_index("shard")]
    copy_to(parts_ref.at[others], recv_ref.at[others], part_send, part_recv, somewhere).wait()

    @pl.loop(0, NDEV // 16)
    def _(d):
        for n in range(16):
            rows32_ref[pl.ds((d * 16 + n) * 17, 16), :] = recv_ref[d * 16 + n].astype(jnp.float32)

    for p in range(4):
        weight = valid_ref[p].astype(jnp.float32) * (1.0 / math.sqrt(NB))
        for n in range(4):
            out_ref[p, :, n * 128 : n * 128 + 128] = rows32_ref[pl.ds(p * 4 + n, BLK, stride=17), :] * weight


def correlate(*operands):
    f32, bf16, i32 = jnp.float32, jnp.bfloat16, jnp.int32
    return pl.pallas_call(
        kernel,
        out_shape=jax.ShapeDtypeStruct((4, BLK, NLAG), f32),
        in_specs=[pl.BlockSpec(memory_space=pltpu.HBM)] * 6,
        out_specs=pl.BlockSpec(memory_space=pltpu.VMEM),
        scratch_shapes=[
            pltpu.VMEM((2, PAIRS), i32),
            pltpu.SMEM((NDEV,), i32),
            pltpu.SMEM((4,), i32),
            pltpu.VMEM((BLK, NT), bf16),
            pltpu.VMEM((TAPS, NB), f32),
            pltpu.VMEM((QT, 256, 256), bf16),
            pltpu.VMEM((2, HALF, NT), bf16),
            pltpu.VMEM((QT, BLK, 256), bf16),
            pltpu.VMEM((QT, 2 * HALF, 256), bf16),
            pltpu.VMEM((QT, 2, WIDE, 128), f32),
            pltpu.VMEM((NB, 128), f32),
            pltpu.VMEM((QT, 40, 128), f32),
            pltpu.VMEM((QT, 2, CHUNK, 128), f32),
            pltpu.VMEM((QT, CHUNK, 128), f32),
            pltpu.VMEM((5, CHUNK, 128), f32),
            pltpu.VMEM((3, QT, 128), f32),
            pltpu.VMEM((33 * BLK, 128), f32),
            pltpu.VMEM((NDEV, 32, 128), bf16),
            pltpu.VMEM((NDEV, 32, 128), bf16),
            pltpu.VMEM((QT, NDEV, 256), bf16),
            pltpu.VMEM((QT, NDEV, 256), bf16),
            pltpu.VMEM((2, PAIRS, NDEV), bf16),
            pltpu.VMEM((256, 1024), bf16),
            pltpu.VMEM((PAIRS // 2, NLAG), f32),
            pltpu.VMEM((NDEV, 16, 128), bf16),
            pltpu.VMEM((NDEV, 16, 128), bf16),
            pltpu.VMEM((QT, 256, NLAG), bf16),
            pltpu.VMEM((2, 32, NLAG), f32),
            pltpu.VMEM((2, 64, NLAG), f32),
            pltpu.SemaphoreType.DMA((6,)),
            pltpu.SemaphoreType.DMA((2,)),
            pltpu.SemaphoreType.DMA((2,)),
            pltpu.SemaphoreType.DMA,
            pltpu.SemaphoreType.DMA,
            pltpu.SemaphoreType.DMA((4,)),
            pltpu.SemaphoreType.DMA((4,)),
            pltpu.SemaphoreType.DMA,
            pltpu.SemaphoreType.DMA,
        ],
        compiler_params=pltpu.CompilerParams(collective_id=0, has_side_effects=True, vmem_limit_bytes=48 << 20),
        name="correlate",
    )(*operands)


def body(samples, fan_taps, pair_blocks, pair_valid, coil_offsets):
    table = jnp.asarray(second_stage_table())
    operands = (pair_blocks.T, coil_offsets, pair_valid, samples.reshape(BLK, NT), fan_taps, table)
    return correlate(*(pltpu.with_memory_space_constraint(operand, pltpu.HBM) for operand in operands))


def solution(mesh):
    return jax.shard_map(
        body,
        mesh=mesh,
        in_specs=(P(AXES, None, None), P(), P(), P(AXES), P()),
        out_specs=P(AXES, None, None),
        check_vma=False,
    )
```

```python
import math

import jax
import jax.numpy as jnp
import ml_dtypes
import numpy as np
from jax import lax
from jax.experimental import pallas as pl
from jax.experimental.pallas import tpu as pltpu
from jax.sharding import PartitionSpec as P

HALF = 16
NLAG = 512
NT = 4096
NB = 2048
BLK = 128
WIDE = BLK + 2 * HALF
EPSILON = 1e-05
AXES = ("group", "shard")
NDEV = 128
PAIRS = 512
CHUNK = 32
MESH = pl.DeviceIdType.MESH
TAPS = 2 * HALF + 1
QT = 16


def residues():
    low = np.arange(QT)
    high = np.where(low == 0, 16, 32 - low)
    return low, high


def tile_bins():
    low, high = residues()
    k2 = np.arange(64)
    return np.concatenate([low[:, None] + 32 * k2, high[:, None] + 32 * k2], axis=1)


def second_stage_table():
    bins = tile_bins()
    b = np.arange(128)
    phase = 2 * np.pi * ((b[None, :, None] * bins[:, None, :]) % NT) / NT
    cos, sin = np.cos(phase), np.sin(phase)
    table = np.zeros((QT, 2, 128, 2, 128))
    conj = np.concatenate([np.ones(64), -np.ones(64)])
    table[:, 0, :, 0] = cos
    table[:, 1, :, 0] = sin * conj
    table[:, 0, :, 1] = -sin
    table[:, 1, :, 1] = cos * conj
    table[0] = 0.0
    table[0, 0, :, 0, :64] = cos[0, :, :64]
    table[0, 0, :, 1, :64] = -sin[0, :, :64]
    table[0, 1, :, 0, 64:] = cos[0, :, 64:]
    table[0, 1, :, 1, 64:] = -sin[0, :, 64:]
    return (table.reshape(QT, 256, 256) / math.sqrt(NT)).astype(ml_dtypes.bfloat16)


def real_fft(rows):
    count = len(rows)
    if count == 2:
        return [(rows[0] + rows[1], None), (rows[0] - rows[1], None)]
    even = real_fft(rows[0::2])
    odd = real_fft(rows[1::2])
    half, quarter = count // 2, count // 4
    out = [None] * (half + 1)
    out[0] = (even[0][0] + odd[0][0], None)
    out[half] = (even[0][0] - odd[0][0], None)
    out[quarter] = (even[quarter][0], -odd[quarter][0])
    for k in range(1, quarter):
        wr, wi = math.cos(2 * math.pi * k / count), -math.sin(2 * math.pi * k / count)
        o_re, o_im = odd[k]
        e_re, e_im = even[k]
        t_re = o_re * wr - o_im * wi
        t_im = o_re * wi + o_im * wr
        out[k] = (e_re + t_re, e_im + t_im)
        out[half - k] = (e_re - t_re, t_im - e_im)
    return out


def place():
    shard = lax.axis_index("shard")
    return lax.axis_index("group"), shard // 8, (shard // 2) % 4, shard % 2


def wrap(value, size):
    return lax.rem(value, size)


def signal_some(barrier, i, guard=True):
    x, z, y, core = place()
    there = (x + i // 4) % 4
    row = (z + i % 4) % 4 * 8
    for dy in range(4):
        for dc in range(2):
            shard = row + (y + dy) % 4 * 2 + (core + dc) % 2

            def signal():
                pl.semaphore_signal(barrier, inc=1, device_id=(there, shard), device_id_type=MESH)

            if guard and dy == 0 and dc == 0:
                pl.when(i > 0)(signal)
            else:
                signal()


def first_stage(rows, y_ref, at):
    freq = real_fft(rows)
    for q in range(QT):
        second = freq[16][0] if q == 0 else freq[q][1]
        y_ref[q, at, 0:128] = freq[q][0].astype(jnp.bfloat16)
        y_ref[q, at, 128:256] = second.astype(jnp.bfloat16)


def sort_taps(fan_ref, turned_ref, taps_ref):
    blank = jnp.zeros((128 - TAPS, 128), jnp.float32)

    @pl.loop(0, QT)
    def _(j):
        at = pl.ds(pl.multiple_of(j * 128, 128), 128)
        turned_ref[at, :] = jnp.concatenate([fan_ref[:, at], blank], axis=0).T

    @pl.loop(0, QT)
    def _(q):
        high = jnp.where(q == 0, 16, 32 - q)
        both = jnp.concatenate(
            [turned_ref[pl.ds(q, 64, stride=32), :], turned_ref[pl.ds(high, 64, stride=32), :]], axis=0
        )
        taps_ref[q] = both.T[:40]


def lag_tables(coarse_ref, fine_ref):
    lag = lax.broadcasted_iota(jnp.int32, (64, NLAG), 1) - NLAG // 2
    row = lax.broadcasted_iota(jnp.int32, (64, NLAG), 0)
    fine = ((32 * row * lag) & (NT - 1)).astype(jnp.float32) * (2.0 * math.pi / NT)
    coarse = ((row * lag) & (NT - 1)).astype(jnp.float32) * (2.0 * math.pi / NT)
    fine_ref[0] = jnp.cos(fine)
    fine_ref[1] = jnp.sin(fine)
    coarse_ref[0] = jnp.cos(coarse[:32])
    coarse_ref[1] = jnp.sin(coarse[:32])


def lag_rows(q, coarse_ref, fine_ref, lags_ref):
    cos_b, sin_b = fine_ref[0], fine_ref[1]
    for half, residue in ((0, q), (64, jnp.where(q == 0, 16, 32 - q))):
        cos_a, sin_a = coarse_ref[0, pl.ds(residue, 1), :], coarse_ref[1, pl.ds(residue, 1), :]
        lags_ref[q, half : half + 64] = (cos_a * cos_b - sin_a * sin_b).astype(jnp.bfloat16)
        lags_ref[q, 128 + half : 192 + half] = (-(sin_a * cos_b + cos_a * sin_b)).astype(jnp.bfloat16)


def pick_rows(planes, pairs_ref, pick_ref):
    block = lax.broadcasted_iota(jnp.int32, (128, 128), 0)
    for side in range(2):
        for n, plane in enumerate(planes):
            at = pl.ds(pl.multiple_of(plane * 128, 128), 128)
            chosen = block == pairs_ref[side : side + 1, at]
            pick_ref[side, n * 128 : n * 128 + 128, :] = jnp.where(chosen, 1.0, 0.0).T.astype(jnp.bfloat16)


def bin_rows(offset, rows_ref):
    lane = lax.broadcasted_iota(jnp.int32, (QT, 128), 1)
    tile = lax.broadcasted_iota(jnp.int32, (QT, 128), 0)
    residue = jnp.where(lane < 64, tile, jnp.where(tile == 0, 16, 32 - tile))
    bins = residue + 32 * (lane & 63)
    theta = ((bins * offset) & (NT - 1)).astype(jnp.float32) * (2.0 * math.pi / NT)
    rows_ref[0] = jnp.cos(theta)
    rows_ref[1] = jnp.sin(theta)
    count = jnp.minimum(bins + 64, NB - 1) - jnp.maximum(bins - 64, 0) + 1
    rows_ref[2] = 1.0 / count.astype(jnp.float32)


def copy_to(src, dst, send_sem, recv_sem, device):
    return pltpu.make_async_remote_copy(
        src_ref=src, dst_ref=dst, send_sem=send_sem, recv_sem=recv_sem, device_id=device, device_id_type=MESH
    )


def channel_of(x, z, y, core):
    return wrap(x + z + y, 2) * 32 + (x * 16 + z * 4 + y) // 2 + 64 * core


def kernel(
    pairs_hbm, offsets_hbm, valid_hbm, x_hbm, fan_hbm, table_hbm, out_ref,
    pairs_ref, offsets_ref, valid_ref, x_ref, fan_ref, table_ref,
    halo_ref, y_ref, y_halo_ref, spec_ref, turned_ref, taps_ref, filt_ref, upto_ref, run_ref, rows_ref,
    rows32_ref, white_ref, blocks_ref, own_ref, other_ref, pick_ref, cross_ref, sums_ref,
    parts_ref, recv_ref, lags_ref, coarse_ref, fine_ref,
    fetch_sem, halo_send, halo_recv, block_send, block_recv, swap_send, swap_recv, part_send, part_recv,
):
    x, z, y, core = place()
    me = lax.axis_index("group") * 32 + lax.axis_index("shard")
    barrier = pltpu.get_barrier_semaphore()
    moves = (
        (x_hbm, x_ref), (offsets_hbm, offsets_ref), (fan_hbm, fan_ref),
        (pairs_hbm, pairs_ref), (valid_hbm, valid_ref), (table_hbm, table_ref),
    )
    fetches = [pltpu.make_async_copy(src, dst, fetch_sem.at[n]) for n, (src, dst) in enumerate(moves)]
    for fetch in fetches:
        fetch.start()

    @pl.loop(0, 8)
    def _(column):
        signal_some(barrier, column)

    fetches[0].wait()

    @pl.loop(0, 8)
    def _(chunk):
        signal_some(barrier, chunk + 8, False)
        at = pl.ds(pl.multiple_of(chunk * 16, 16), 16)
        first_stage([x_ref[at, a * 128 : (a + 1) * 128].astype(jnp.float32) for a in range(32)], y_ref, at)

    for fetch in fetches[1:]:
        fetch.wait()
    sort_taps(fan_ref, turned_ref, taps_ref)
    bin_rows(offsets_ref[me], rows_ref)

    @pl.loop(0, QT // 4)
    def _(group):
        for n in range(4):
            q = group * 4 + n
            both = jnp.dot(y_ref[q], table_ref[q], preferred_element_type=jnp.float32)
            spec_ref[q, 0, HALF : HALF + BLK] = both[:, :128]
            spec_ref[q, 1, HALF : HALF + BLK] = both[:, 128:]

    pl.semaphore_wait(barrier, NDEV - 1)
    after, before = wrap(me + 1, NDEV), wrap(me + NDEV - 1, NDEV)
    to_after = copy_to(
        x_ref.at[pl.ds(BLK - HALF, HALF)], halo_ref.at[0], halo_send.at[0], halo_recv.at[0],
        (after // 32, wrap(after, 32)),
    )
    to_before = copy_to(
        x_ref.at[pl.ds(0, HALF)], halo_ref.at[1], halo_send.at[1], halo_recv.at[1],
        (before // 32, wrap(before, 32)),
    )
    to_after.start()
    to_before.start()

    def take_halo():
        to_after.wait()
        to_before.wait()

        @pl.loop(0, 2)
        def _(side):
            edge = jnp.where(side == 0, me > 0, me < NDEV - 1).astype(jnp.float32)
            to = pl.ds(pl.multiple_of(side * HALF, HALF), HALF)
            first_stage(
                [halo_ref[side, :, a * 128 : (a + 1) * 128].astype(jnp.float32) * edge for a in range(32)],
                y_halo_ref,
                to,
            )

        @pl.loop(0, QT // 4)
        def _(group):
            for n in range(4):
                q = group * 4 + n
                both = jnp.dot(y_halo_ref[q], table_ref[q], preferred_element_type=jnp.float32)
                for r in range(2):
                    spec_ref[q, r, 0:HALF] = both[:HALF, r * 128 : r * 128 + 128]
                    spec_ref[q, r, HALF + BLK : WIDE] = both[HALF:, r * 128 : r * 128 + 128]

    lanes = lax.broadcasted_iota(jnp.int32, (CHUNK, 128), 1)
    low = lanes < 64
    k2 = lanes & 63
    sign = 1 - 2 * core
    mine = channel_of(x, z, y, core)
    somewhere = (x, lax.axis_index("shard") + 1 - 2 * core)
    others = pl.ds(0, NDEV - 1)
    xs = [wrap(x + 4 + sign * n, 4) for n in range(4)]
    zs = [wrap(z + 4 + sign * n, 4) for n in range(4)]
    ys = [wrap(y // 2 + n, 2) for n in range(2)]

    @pl.loop(0, 4)
    def _(turn):
        pl.when(turn == 2)(take_halo)
        ahead = jnp.where(turn < 2, 1 + turn, 3 * turn - 6)
        chunk = jnp.where(core == 0, ahead, 3 - ahead)
        first = pl.multiple_of(chunk * CHUNK, CHUNK)

        def fan(q, run):
            re = jnp.zeros((CHUNK, 128), jnp.float32)
            im = re
            for t in range(TAPS):
                tap = taps_ref[q, t : t + 1, :]
                re = re + tap * spec_ref[q, 0, pl.ds(first + t, CHUNK), :]
                im = im + tap * spec_ref[q, 1, pl.ds(first + t, CHUNK), :]
            filt_ref[q, 0] = re
            filt_ref[q, 1] = im
            run = run + jnp.where(low | (q > 0), re * re + im * im, 0.0)
            upto_ref[q] = run
            return run

        run = lax.fori_loop(0, QT, fan, jnp.zeros((CHUNK, 128), jnp.float32), unroll=2)

        power = filt_ref[0, 0] * filt_ref[0, 0] + filt_ref[0, 1] * filt_ref[0, 1]
        sums = run + jnp.where(low, 0.0, power)
        swapped = pltpu.roll(sums, 64, 1)
        total = sums + swapped
        run_ref[1] = total
        run_ref[2] = (
            total
            + jnp.where(k2 >= 1, pltpu.roll(total, 1, 1), 0.0)
            + jnp.where(k2 <= 62, pltpu.roll(total, 127, 1), 0.0)
        )
        run_ref[3] = jnp.where(low, power, sums)
        run_ref[4] = jnp.where(low, total, swapped + power)

        @pl.loop(0, QT, unroll=8)
        def _(q):
            re, im = filt_ref[q, 0], filt_ref[q, 1]
            upto = jnp.where(q == 0, run_ref[3], upto_ref[q])
            rest = jnp.where(q == 0, run_ref[4], jnp.maximum(run_ref[1] - upto_ref[jnp.maximum(q - 1, 0)], 0.0))
            prefix = jnp.where(low, upto, rest)
            suffix = jnp.where(low, rest, upto)
            window = (
                run_ref[2]
                + jnp.where(k2 >= 2, pltpu.roll(suffix, 2, 1), 0.0)
                + jnp.where(k2 <= 61, pltpu.roll(prefix, 126, 1), 0.0)
            )
            scale = lax.rsqrt(window * rows_ref[2, pl.ds(q, 1), :] + EPSILON)
            cos = rows_ref[0, pl.ds(q, 1), :]
            sin = rows_ref[1, pl.ds(q, 1), :]
            rows32_ref[pl.ds(q, CHUNK, stride=33), :] = (re * cos + im * sin) * scale
            rows32_ref[pl.ds(16 + q, CHUNK, stride=33), :] = (im * cos - re * sin) * scale

        to_core, parity = chunk // 2, wrap(chunk, 2)
        for n in range(32):
            to_x, to_z, to_y2 = xs[n % 4], zs[(n // 4 + n) % 4], ys[n // 16]
            shard = to_z * 8 + to_y2 * 4 + 2 * wrap(parity + to_x + to_z, 2) + to_core
            row = to_x * 8 + to_z * 2 + to_y2
            white_ref[first + row] = rows32_ref[pl.ds(row * 33, 32), :].astype(jnp.bfloat16)
            push = copy_to(
                white_ref.at[first + row], blocks_ref.at[me], block_send, block_recv, (to_x, shard)
            ).start
            if n == 0:
                pl.when(first + row != mine)(push)
            else:
                push()

    blocks_ref[me] = white_ref[mine]

    lag_tables(coarse_ref, fine_ref)
    pick_rows(xs, pairs_ref, pick_ref)

    @pl.loop(0, QT)
    def _(q):
        lag_rows(q, coarse_ref, fine_ref, lags_ref)

    copy_to(white_ref.at[others], blocks_ref.at[others], block_send, block_recv, somewhere).wait()

    @pl.loop(0, NDEV // 8)
    def _(d):
        for n in range(8):
            rows32_ref[pl.ds((d * 8 + n) * 33, 32), :] = blocks_ref[d * 8 + n].astype(jnp.float32)

    def swap(part):
        some = pl.ds(part * 4, 4)
        return copy_to(own_ref.at[some], other_ref.at[some], swap_send.at[part], swap_recv.at[part], somewhere)

    @pl.loop(0, 4)
    def _(part):
        for n in range(4):
            q = part * 4 + n
            own_ref[q, :, 0:128] = rows32_ref[pl.ds(q, BLK, stride=33), :].astype(jnp.bfloat16)
            own_ref[q, :, 128:256] = rows32_ref[pl.ds(16 + q, BLK, stride=33), :].astype(jnp.bfloat16)
        swap(part).start()

    def add_part(part, half):
        rows = pl.ds(pl.multiple_of(half * 256, 256), 256)
        for n in range(4):
            q = part * 4 + n
            left = jnp.dot(pick_ref[0, rows, :], own_ref[q], preferred_element_type=jnp.float32)
            right = jnp.dot(pick_ref[1, rows, :], other_ref[q], preferred_element_type=jnp.float32)
            l_re, l_im, r_re, r_im = left[:, :128], left[:, 128:], right[:, :128], right[:, 128:]
            cross_ref[:, n * 256 : n * 256 + 128] = (l_re * r_re + l_im * r_im).astype(jnp.bfloat16)
            cross_ref[:, n * 256 + 128 : n * 256 + 256] = (l_im * r_re - l_re * r_im).astype(jnp.bfloat16)
        lags = lags_ref[pl.ds(part * 4, 4)].reshape(1024, NLAG)
        return jnp.dot(cross_ref[...], lags, preferred_element_type=jnp.float32)

    @pl.loop(0, 2)
    def _(turn):
        @pl.loop(0, 4)
        def _(part):
            pl.when(turn == 0)(lambda: swap(part).wait())
            added = add_part(part, turn)
            sums_ref[...] = jnp.where(part == 0, added, sums_ref[...] + added)

        for n in range(4):
            rows32_ref[pl.ds(n, 256, stride=4), :] = sums_ref[:, n * 128 : n * 128 + 128]

        planes = [wrap(x + 4 + sign * (2 * turn + n), 4) for n in range(2)]

        @pl.loop(0, 4)
        def _(i):
            for n in range(16):
                to_core = core if n < 8 else 1 - core
                shard = zs[n // 2 % 4] * 8 + wrap(y + i + n, 4) * 2 + to_core
                row = n % 2 * 32 + shard
                slot = turn * 64 + row
                parts_ref[slot] = rows32_ref[pl.ds(pl.multiple_of(row * 16, 16), 16), :].astype(jnp.bfloat16)
                push = copy_to(
                    parts_ref.at[slot], recv_ref.at[mine], part_send, part_recv, (planes[n % 2], shard)
                ).start
                if n == 0:
                    pl.when(turn + i > 0)(push)
                else:
                    push()

    recv_ref[mine] = parts_ref[lax.axis_index("shard")]
    copy_to(parts_ref.at[others], recv_ref.at[others], part_send, part_recv, somewhere).wait()

    @pl.loop(0, NDEV // 16)
    def _(d):
        for n in range(16):
            rows32_ref[pl.ds((d * 16 + n) * 17, 16), :] = recv_ref[d * 16 + n].astype(jnp.float32)

    for p in range(4):
        weight = valid_ref[p].astype(jnp.float32) * (1.0 / math.sqrt(NB))
        for n in range(4):
            out_ref[p, :, n * 128 : n * 128 + 128] = rows32_ref[pl.ds(p * 4 + n, BLK, stride=17), :] * weight


def correlate(*operands):
    f32, bf16, i32 = jnp.float32, jnp.bfloat16, jnp.int32
    return pl.pallas_call(
        kernel,
        out_shape=jax.ShapeDtypeStruct((4, BLK, NLAG), f32),
        in_specs=[pl.BlockSpec(memory_space=pltpu.HBM)] * 6,
        out_specs=pl.BlockSpec(memory_space=pltpu.VMEM),
        scratch_shapes=[
            pltpu.VMEM((2, PAIRS), i32),
            pltpu.SMEM((NDEV,), i32),
            pltpu.SMEM((4,), i32),
            pltpu.VMEM((BLK, NT), bf16),
            pltpu.VMEM((TAPS, NB), f32),
            pltpu.VMEM((QT, 256, 256), bf16),
            pltpu.VMEM((2, HALF, NT), bf16),
            pltpu.VMEM((QT, BLK, 256), bf16),
            pltpu.VMEM((QT, 2 * HALF, 256), bf16),
            pltpu.VMEM((QT, 2, WIDE, 128), f32),
            pltpu.VMEM((NB, 128), f32),
            pltpu.VMEM((QT, 40, 128), f32),
            pltpu.VMEM((QT, 2, CHUNK, 128), f32),
            pltpu.VMEM((QT, CHUNK, 128), f32),
            pltpu.VMEM((5, CHUNK, 128), f32),
            pltpu.VMEM((3, QT, 128), f32),
            pltpu.VMEM((33 * BLK, 128), f32),
            pltpu.VMEM((NDEV, 32, 128), bf16),
            pltpu.VMEM((NDEV, 32, 128), bf16),
            pltpu.VMEM((QT, NDEV, 256), bf16),
            pltpu.VMEM((QT, NDEV, 256), bf16),
            pltpu.VMEM((2, PAIRS, NDEV), bf16),
            pltpu.VMEM((256, 1024), bf16),
            pltpu.VMEM((PAIRS // 2, NLAG), f32),
            pltpu.VMEM((NDEV, 16, 128), bf16),
            pltpu.VMEM((NDEV, 16, 128), bf16),
            pltpu.VMEM((QT, 256, NLAG), bf16),
            pltpu.VMEM((2, 32, NLAG), f32),
            pltpu.VMEM((2, 64, NLAG), f32),
            pltpu.SemaphoreType.DMA((6,)),
            pltpu.SemaphoreType.DMA((2,)),
            pltpu.SemaphoreType.DMA((2,)),
            pltpu.SemaphoreType.DMA,
            pltpu.SemaphoreType.DMA,
            pltpu.SemaphoreType.DMA((4,)),
            pltpu.SemaphoreType.DMA((4,)),
            pltpu.SemaphoreType.DMA,
            pltpu.SemaphoreType.DMA,
        ],
        compiler_params=pltpu.CompilerParams(collective_id=0, has_side_effects=True, vmem_limit_bytes=48 << 20),
        name="correlate",
    )(*operands)


def body(samples, fan_taps, pair_blocks, pair_valid, coil_offsets):
    table = jnp.asarray(second_stage_table())
    operands = (pair_blocks.T, coil_offsets, pair_valid, samples.reshape(BLK, NT), fan_taps, table)
    return correlate(*(pltpu.with_memory_space_constraint(operand, pltpu.HBM) for operand in operands))


def solution(mesh):
    return jax.shard_map(
        body,
        mesh=mesh,
        in_specs=(P(AXES, None, None), P(), P(), P(AXES), P()),
        out_specs=P(AXES, None, None),
        check_vma=False,
    )
```

```python
import math

import jax
import jax.numpy as jnp
import ml_dtypes
import numpy as np
from jax import lax
from jax.experimental import pallas as pl
from jax.experimental.pallas import tpu as pltpu
from jax.sharding import PartitionSpec as P

HALF = 16
NLAG = 512
NT = 4096
NB = 2048
BLK = 128
WIDE = BLK + 2 * HALF
EPSILON = 1e-05
AXES = ("group", "shard")
NDEV = 128
PAIRS = 512
CHUNK = 32
MESH = pl.DeviceIdType.MESH
TAPS = 2 * HALF + 1
QT = 16


def residues():
    low = np.arange(QT)
    high = np.where(low == 0, 16, 32 - low)
    return low, high


def tile_bins():
    low, high = residues()
    k2 = np.arange(64)
    return np.concatenate([low[:, None] + 32 * k2, high[:, None] + 32 * k2], axis=1)


def second_stage_table():
    bins = tile_bins()
    b = np.arange(128)
    phase = 2 * np.pi * ((b[None, :, None] * bins[:, None, :]) % NT) / NT
    cos, sin = np.cos(phase), np.sin(phase)
    table = np.zeros((QT, 2, 128, 2, 128))
    conj = np.concatenate([np.ones(64), -np.ones(64)])
    table[:, 0, :, 0] = cos
    table[:, 1, :, 0] = sin * conj
    table[:, 0, :, 1] = -sin
    table[:, 1, :, 1] = cos * conj
    table[0] = 0.0
    table[0, 0, :, 0, :64] = cos[0, :, :64]
    table[0, 0, :, 1, :64] = -sin[0, :, :64]
    table[0, 1, :, 0, 64:] = cos[0, :, 64:]
    table[0, 1, :, 1, 64:] = -sin[0, :, 64:]
    return (table.reshape(QT, 256, 256) / math.sqrt(NT)).astype(ml_dtypes.bfloat16)


def real_fft(rows):
    count = len(rows)
    if count == 2:
        return [(rows[0] + rows[1], None), (rows[0] - rows[1], None)]
    even = real_fft(rows[0::2])
    odd = real_fft(rows[1::2])
    half, quarter = count // 2, count // 4
    out = [None] * (half + 1)
    out[0] = (even[0][0] + odd[0][0], None)
    out[half] = (even[0][0] - odd[0][0], None)
    out[quarter] = (even[quarter][0], -odd[quarter][0])
    for k in range(1, quarter):
        wr, wi = math.cos(2 * math.pi * k / count), -math.sin(2 * math.pi * k / count)
        o_re, o_im = odd[k]
        e_re, e_im = even[k]
        t_re = o_re * wr - o_im * wi
        t_im = o_re * wi + o_im * wr
        out[k] = (e_re + t_re, e_im + t_im)
        out[half - k] = (e_re - t_re, t_im - e_im)
    return out


def place():
    shard = lax.axis_index("shard")
    return lax.axis_index("group"), shard // 8, (shard // 2) % 4, shard % 2


def wrap(value, size):
    return lax.rem(value, size)


def signal_some(barrier, i, guard=True):
    x, z, y, core = place()
    there = (x + i // 4) % 4
    row = (z + i % 4) % 4 * 8
    for dy in range(4):
        for dc in range(2):
            shard = row + (y + dy) % 4 * 2 + (core + dc) % 2

            def signal():
                pl.semaphore_signal(barrier, inc=1, device_id=(there, shard), device_id_type=MESH)

            if guard and dy == 0 and dc == 0:
                pl.when(i > 0)(signal)
            else:
                signal()


def first_stage(rows, y_ref, at):
    freq = real_fft(rows)
    for q in range(QT):
        second = freq[16][0] if q == 0 else freq[q][1]
        y_ref[q, at, 0:128] = freq[q][0].astype(jnp.bfloat16)
        y_ref[q, at, 128:256] = second.astype(jnp.bfloat16)


def sort_taps(fan_ref, turned_ref, taps_ref):
    blank = jnp.zeros((128 - TAPS, 128), jnp.float32)

    @pl.loop(0, QT)
    def _(j):
        at = pl.ds(pl.multiple_of(j * 128, 128), 128)
        turned_ref[at, :] = jnp.concatenate([fan_ref[:, at], blank], axis=0).T

    @pl.loop(0, QT)
    def _(q):
        high = jnp.where(q == 0, 16, 32 - q)
        both = jnp.concatenate(
            [turned_ref[pl.ds(q, 64, stride=32), :], turned_ref[pl.ds(high, 64, stride=32), :]], axis=0
        )
        taps_ref[q] = both.T[:40]


def lag_tables(coarse_ref, fine_ref):
    lag = lax.broadcasted_iota(jnp.int32, (64, NLAG), 1) - NLAG // 2
    row = lax.broadcasted_iota(jnp.int32, (64, NLAG), 0)
    fine = ((32 * row * lag) & (NT - 1)).astype(jnp.float32) * (2.0 * math.pi / NT)
    coarse = ((row * lag) & (NT - 1)).astype(jnp.float32) * (2.0 * math.pi / NT)
    fine_ref[0] = jnp.cos(fine)
    fine_ref[1] = jnp.sin(fine)
    coarse_ref[0] = jnp.cos(coarse[:32])
    coarse_ref[1] = jnp.sin(coarse[:32])


def lag_rows(q, coarse_ref, fine_ref, lags_ref):
    cos_b, sin_b = fine_ref[0], fine_ref[1]
    for half, residue in ((0, q), (64, jnp.where(q == 0, 16, 32 - q))):
        cos_a, sin_a = coarse_ref[0, pl.ds(residue, 1), :], coarse_ref[1, pl.ds(residue, 1), :]
        lags_ref[q, half : half + 64] = (cos_a * cos_b - sin_a * sin_b).astype(jnp.bfloat16)
        lags_ref[q, 128 + half : 192 + half] = (-(sin_a * cos_b + cos_a * sin_b)).astype(jnp.bfloat16)


def pick_rows(planes, pairs_ref, pick_ref):
    block = lax.broadcasted_iota(jnp.int32, (128, 128), 0)
    for side in range(2):
        for n, plane in enumerate(planes):
            at = pl.ds(pl.multiple_of(plane * 128, 128), 128)
            chosen = block == pairs_ref[side : side + 1, at]
            pick_ref[side, n * 128 : n * 128 + 128, :] = jnp.where(chosen, 1.0, 0.0).T.astype(jnp.bfloat16)


def bin_rows(offset, rows_ref):
    lane = lax.broadcasted_iota(jnp.int32, (QT, 128), 1)
    tile = lax.broadcasted_iota(jnp.int32, (QT, 128), 0)
    residue = jnp.where(lane < 64, tile, jnp.where(tile == 0, 16, 32 - tile))
    bins = residue + 32 * (lane & 63)
    theta = ((bins * offset) & (NT - 1)).astype(jnp.float32) * (2.0 * math.pi / NT)
    rows_ref[0] = jnp.cos(theta)
    rows_ref[1] = jnp.sin(theta)
    count = jnp.minimum(bins + 64, NB - 1) - jnp.maximum(bins - 64, 0) + 1
    rows_ref[2] = 1.0 / count.astype(jnp.float32)


def copy_to(src, dst, send_sem, recv_sem, device):
    return pltpu.make_async_remote_copy(
        src_ref=src, dst_ref=dst, send_sem=send_sem, recv_sem=recv_sem, device_id=device, device_id_type=MESH
    )


def channel_of(x, z, y, core):
    return wrap(x + z + y, 2) * 32 + (x * 16 + z * 4 + y) // 2 + 64 * core


def kernel(
    pairs_hbm, offsets_hbm, valid_hbm, x_hbm, fan_hbm, table_hbm, out_ref,
    pairs_ref, offsets_ref, valid_ref, x_ref, fan_ref, table_ref,
    halo_ref, y_ref, y_halo_ref, spec_ref, turned_ref, taps_ref, filt_ref, upto_ref, run_ref, rows_ref,
    rows32_ref, white_ref, blocks_ref, own_ref, other_ref, pick_ref, cross_ref, sums_ref,
    parts_ref, recv_ref, lags_ref, coarse_ref, fine_ref,
    fetch_sem, halo_send, halo_recv, block_send, block_recv, swap_send, swap_recv, part_send, part_recv,
):
    x, z, y, core = place()
    me = lax.axis_index("group") * 32 + lax.axis_index("shard")
    barrier = pltpu.get_barrier_semaphore()
    moves = (
        (x_hbm, x_ref), (offsets_hbm, offsets_ref), (fan_hbm, fan_ref),
        (pairs_hbm, pairs_ref), (valid_hbm, valid_ref), (table_hbm, table_ref),
    )
    fetches = [pltpu.make_async_copy(src, dst, fetch_sem.at[n]) for n, (src, dst) in enumerate(moves)]
    for fetch in fetches:
        fetch.start()

    @pl.loop(0, 8)
    def _(column):
        signal_some(barrier, column)

    fetches[0].wait()

    @pl.loop(0, 8)
    def _(chunk):
        signal_some(barrier, chunk + 8, False)
        at = pl.ds(pl.multiple_of(chunk * 16, 16), 16)
        first_stage([x_ref[at, a * 128 : (a + 1) * 128].astype(jnp.float32) for a in range(32)], y_ref, at)

    for fetch in fetches[1:]:
        fetch.wait()
    sort_taps(fan_ref, turned_ref, taps_ref)
    bin_rows(offsets_ref[me], rows_ref)

    @pl.loop(0, QT // 4)
    def _(group):
        for n in range(4):
            q = group * 4 + n
            both = jnp.dot(y_ref[q], table_ref[q], preferred_element_type=jnp.float32)
            spec_ref[q, 0, HALF : HALF + BLK] = both[:, :128]
            spec_ref[q, 1, HALF : HALF + BLK] = both[:, 128:]

    pl.semaphore_wait(barrier, NDEV - 1)
    after, before = wrap(me + 1, NDEV), wrap(me + NDEV - 1, NDEV)
    to_after = copy_to(
        x_ref.at[pl.ds(BLK - HALF, HALF)], halo_ref.at[0], halo_send.at[0], halo_recv.at[0],
        (after // 32, wrap(after, 32)),
    )
    to_before = copy_to(
        x_ref.at[pl.ds(0, HALF)], halo_ref.at[1], halo_send.at[1], halo_recv.at[1],
        (before // 32, wrap(before, 32)),
    )
    to_after.start()
    to_before.start()

    def take_halo():
        to_after.wait()
        to_before.wait()

        @pl.loop(0, 2)
        def _(side):
            edge = jnp.where(side == 0, me > 0, me < NDEV - 1).astype(jnp.float32)
            to = pl.ds(pl.multiple_of(side * HALF, HALF), HALF)
            first_stage(
                [halo_ref[side, :, a * 128 : (a + 1) * 128].astype(jnp.float32) * edge for a in range(32)],
                y_halo_ref,
                to,
            )

        @pl.loop(0, QT // 4)
        def _(group):
            for n in range(4):
                q = group * 4 + n
                both = jnp.dot(y_halo_ref[q], table_ref[q], preferred_element_type=jnp.float32)
                for r in range(2):
                    spec_ref[q, r, 0:HALF] = both[:HALF, r * 128 : r * 128 + 128]
                    spec_ref[q, r, HALF + BLK : WIDE] = both[HALF:, r * 128 : r * 128 + 128]

    lanes = lax.broadcasted_iota(jnp.int32, (CHUNK, 128), 1)
    low = lanes < 64
    k2 = lanes & 63
    sign = 1 - 2 * core
    mine = channel_of(x, z, y, core)
    somewhere = (x, lax.axis_index("shard") + 1 - 2 * core)
    others = pl.ds(0, NDEV - 1)
    xs = [wrap(x + 4 + sign * n, 4) for n in range(4)]
    zs = [wrap(z + 4 + sign * n, 4) for n in range(4)]
    ys = [wrap(y // 2 + n, 2) for n in range(2)]

    @pl.loop(0, 4)
    def _(turn):
        pl.when(turn == 2)(take_halo)
        ahead = jnp.where(turn < 2, 1 + turn, 3 * turn - 6)
        chunk = jnp.where(core == 0, ahead, 3 - ahead)
        first = pl.multiple_of(chunk * CHUNK, CHUNK)

        def fan(q, run):
            re = jnp.zeros((CHUNK, 128), jnp.float32)
            im = re
            for t in range(TAPS):
                tap = taps_ref[q, t : t + 1, :]
                re = re + tap * spec_ref[q, 0, pl.ds(first + t, CHUNK), :]
                im = im + tap * spec_ref[q, 1, pl.ds(first + t, CHUNK), :]
            filt_ref[q, 0] = re
            filt_ref[q, 1] = im
            run = run + jnp.where(low | (q > 0), re * re + im * im, 0.0)
            upto_ref[q] = run
            return run

        run = lax.fori_loop(0, QT, fan, jnp.zeros((CHUNK, 128), jnp.float32), unroll=2)

        power = filt_ref[0, 0] * filt_ref[0, 0] + filt_ref[0, 1] * filt_ref[0, 1]
        sums = run + jnp.where(low, 0.0, power)
        swapped = pltpu.roll(sums, 64, 1)
        total = sums + swapped
        run_ref[1] = total
        run_ref[2] = (
            total
            + jnp.where(k2 >= 1, pltpu.roll(total, 1, 1), 0.0)
            + jnp.where(k2 <= 62, pltpu.roll(total, 127, 1), 0.0)
        )
        run_ref[3] = jnp.where(low, power, sums)
        run_ref[4] = jnp.where(low, total, swapped + power)

        @pl.loop(0, QT, unroll=8)
        def _(q):
            re, im = filt_ref[q, 0], filt_ref[q, 1]
            upto = jnp.where(q == 0, run_ref[3], upto_ref[q])
            rest = jnp.where(q == 0, run_ref[4], jnp.maximum(run_ref[1] - upto_ref[jnp.maximum(q - 1, 0)], 0.0))
            prefix = jnp.where(low, upto, rest)
            suffix = jnp.where(low, rest, upto)
            window = (
                run_ref[2]
                + jnp.where(k2 >= 2, pltpu.roll(suffix, 2, 1), 0.0)
                + jnp.where(k2 <= 61, pltpu.roll(prefix, 126, 1), 0.0)
            )
            scale = lax.rsqrt(window * rows_ref[2, pl.ds(q, 1), :] + EPSILON)
            cos = rows_ref[0, pl.ds(q, 1), :]
            sin = rows_ref[1, pl.ds(q, 1), :]
            rows32_ref[pl.ds(q, CHUNK, stride=33), :] = (re * cos + im * sin) * scale
            rows32_ref[pl.ds(16 + q, CHUNK, stride=33), :] = (im * cos - re * sin) * scale

        to_core, parity = chunk // 2, wrap(chunk, 2)
        for n in range(32):
            to_x, to_z, to_y2 = xs[n % 4], zs[(n // 4 + n) % 4], ys[n // 16]
            shard = to_z * 8 + to_y2 * 4 + 2 * wrap(parity + to_x + to_z, 2) + to_core
            row = to_x * 8 + to_z * 2 + to_y2
            white_ref[first + row] = rows32_ref[pl.ds(row * 33, 32), :].astype(jnp.bfloat16)
            push = copy_to(
                white_ref.at[first + row], blocks_ref.at[me], block_send, block_recv, (to_x, shard)
            ).start
            if n == 0:
                pl.when(first + row != mine)(push)
            else:
                push()

    blocks_ref[me] = white_ref[mine]

    lag_tables(coarse_ref, fine_ref)
    pick_rows(xs, pairs_ref, pick_ref)

    @pl.loop(0, QT)
    def _(q):
        lag_rows(q, coarse_ref, fine_ref, lags_ref)

    copy_to(white_ref.at[others], blocks_ref.at[others], block_send, block_recv, somewhere).wait()

    @pl.loop(0, NDEV // 8, unroll=2)
    def _(d):
        for n in range(8):
            rows32_ref[pl.ds((d * 8 + n) * 33, 32), :] = blocks_ref[d * 8 + n].astype(jnp.float32)

    def swap(part):
        some = pl.ds(part * 4, 4)
        return copy_to(own_ref.at[some], other_ref.at[some], swap_send.at[part], swap_recv.at[part], somewhere)

    @pl.loop(0, 4)
    def _(part):
        for n in range(4):
            q = part * 4 + n
            own_ref[q, :, 0:128] = rows32_ref[pl.ds(q, BLK, stride=33), :].astype(jnp.bfloat16)
            own_ref[q, :, 128:256] = rows32_ref[pl.ds(16 + q, BLK, stride=33), :].astype(jnp.bfloat16)
        swap(part).start()

    def add_part(part, half):
        rows = pl.ds(pl.multiple_of(half * 256, 256), 256)
        for n in range(4):
            q = part * 4 + n
            left = jnp.dot(pick_ref[0, rows, :], own_ref[q], preferred_element_type=jnp.float32)
            right = jnp.dot(pick_ref[1, rows, :], other_ref[q], preferred_element_type=jnp.float32)
            l_re, l_im, r_re, r_im = left[:, :128], left[:, 128:], right[:, :128], right[:, 128:]
            cross_ref[:, n * 256 : n * 256 + 128] = (l_re * r_re + l_im * r_im).astype(jnp.bfloat16)
            cross_ref[:, n * 256 + 128 : n * 256 + 256] = (l_im * r_re - l_re * r_im).astype(jnp.bfloat16)
        lags = lags_ref[pl.ds(part * 4, 4)].reshape(1024, NLAG)
        return jnp.dot(cross_ref[...], lags, preferred_element_type=jnp.float32)

    @pl.loop(0, 2)
    def _(turn):
        @pl.loop(0, 4)
        def _(part):
            pl.when(turn == 0)(lambda: swap(part).wait())
            added = add_part(part, turn)
            sums_ref[...] = jnp.where(part == 0, added, sums_ref[...] + added)

        for n in range(4):
            rows32_ref[pl.ds(n, 256, stride=4), :] = sums_ref[:, n * 128 : n * 128 + 128]

        planes = [wrap(x + 4 + sign * (2 * turn + n), 4) for n in range(2)]

        @pl.loop(0, 4, unroll=2)
        def _(i):
            for n in range(16):
                to_core = core if n < 8 else 1 - core
                shard = zs[n // 2 % 4] * 8 + wrap(y + i + n, 4) * 2 + to_core
                row = n % 2 * 32 + shard
                slot = turn * 64 + row
                parts_ref[slot] = rows32_ref[pl.ds(pl.multiple_of(row * 16, 16), 16), :].astype(jnp.bfloat16)
                push = copy_to(
                    parts_ref.at[slot], recv_ref.at[mine], part_send, part_recv, (planes[n % 2], shard)
                ).start
                if n == 0:
                    pl.when(turn + i > 0)(push)
                else:
                    push()

    recv_ref[mine] = parts_ref[lax.axis_index("shard")]
    copy_to(parts_ref.at[others], recv_ref.at[others], part_send, part_recv, somewhere).wait()

    @pl.loop(0, NDEV // 16)
    def _(d):
        for n in range(16):
            rows32_ref[pl.ds((d * 16 + n) * 17, 16), :] = recv_ref[d * 16 + n].astype(jnp.float32)

    for p in range(4):
        weight = valid_ref[p].astype(jnp.float32) * (1.0 / math.sqrt(NB))
        for n in range(4):
            out_ref[p, :, n * 128 : n * 128 + 128] = rows32_ref[pl.ds(p * 4 + n, BLK, stride=17), :] * weight


def correlate(*operands):
    f32, bf16, i32 = jnp.float32, jnp.bfloat16, jnp.int32
    return pl.pallas_call(
        kernel,
        out_shape=jax.ShapeDtypeStruct((4, BLK, NLAG), f32),
        in_specs=[pl.BlockSpec(memory_space=pltpu.HBM)] * 6,
        out_specs=pl.BlockSpec(memory_space=pltpu.VMEM),
        scratch_shapes=[
            pltpu.VMEM((2, PAIRS), i32),
            pltpu.SMEM((NDEV,), i32),
            pltpu.SMEM((4,), i32),
            pltpu.VMEM((BLK, NT), bf16),
            pltpu.VMEM((TAPS, NB), f32),
            pltpu.VMEM((QT, 256, 256), bf16),
            pltpu.VMEM((2, HALF, NT), bf16),
            pltpu.VMEM((QT, BLK, 256), bf16),
            pltpu.VMEM((QT, 2 * HALF, 256), bf16),
            pltpu.VMEM((QT, 2, WIDE, 128), f32),
            pltpu.VMEM((NB + 64, 128), f32),
            pltpu.VMEM((QT, 40, 128), f32),
            pltpu.VMEM((QT, 2, CHUNK, 128), f32),
            pltpu.VMEM((QT, CHUNK, 128), f32),
            pltpu.VMEM((5, CHUNK, 128), f32),
            pltpu.VMEM((3, QT, 128), f32),
            pltpu.VMEM((33 * BLK + 64, 128), f32),
            pltpu.VMEM((NDEV, 32, 128), bf16),
            pltpu.VMEM((NDEV, 32, 128), bf16),
            pltpu.VMEM((QT, NDEV, 256), bf16),
            pltpu.VMEM((QT, NDEV, 256), bf16),
            pltpu.VMEM((2, PAIRS, NDEV), bf16),
            pltpu.VMEM((256, 1024), bf16),
            pltpu.VMEM((PAIRS // 2, NLAG), f32),
            pltpu.VMEM((NDEV, 16, 128), bf16),
            pltpu.VMEM((NDEV, 16, 128), bf16),
            pltpu.VMEM((QT, 256, NLAG), bf16),
            pltpu.VMEM((2, 32, NLAG), f32),
            pltpu.VMEM((2, 64, NLAG), f32),
            pltpu.SemaphoreType.DMA((6,)),
            pltpu.SemaphoreType.DMA((2,)),
            pltpu.SemaphoreType.DMA((2,)),
            pltpu.SemaphoreType.DMA,
            pltpu.SemaphoreType.DMA,
            pltpu.SemaphoreType.DMA((4,)),
            pltpu.SemaphoreType.DMA((4,)),
            pltpu.SemaphoreType.DMA,
            pltpu.SemaphoreType.DMA,
        ],
        compiler_params=pltpu.CompilerParams(collective_id=0, has_side_effects=True, vmem_limit_bytes=48 << 20),
        name="correlate",
    )(*operands)


def body(samples, fan_taps, pair_blocks, pair_valid, coil_offsets):
    table = jnp.asarray(second_stage_table())
    operands = (pair_blocks.T, coil_offsets, pair_valid, samples.reshape(BLK, NT), fan_taps, table)
    return correlate(*(pltpu.with_memory_space_constraint(operand, pltpu.HBM) for operand in operands))


def solution(mesh):
    return jax.shard_map(
        body,
        mesh=mesh,
        in_specs=(P(AXES, None, None), P(), P(), P(AXES), P()),
        out_specs=P(AXES, None, None),
        check_vma=False,
    )
```

```python
import math

import jax
import jax.numpy as jnp
import ml_dtypes
import numpy as np
from jax import lax
from jax.experimental import pallas as pl
from jax.experimental.pallas import tpu as pltpu
from jax.sharding import PartitionSpec as P

HALF = 16
NLAG = 512
NT = 4096
NB = 2048
BLK = 128
WIDE = BLK + 2 * HALF
EPSILON = 1e-05
AXES = ("group", "shard")
NDEV = 128
PAIRS = 512
CHUNK = 32
MESH = pl.DeviceIdType.MESH
TAPS = 2 * HALF + 1
QT = 16


def residues():
    low = np.arange(QT)
    high = np.where(low == 0, 16, 32 - low)
    return low, high


def tile_bins():
    low, high = residues()
    k2 = np.arange(64)
    return np.concatenate([low[:, None] + 32 * k2, high[:, None] + 32 * k2], axis=1)


def second_stage_table():
    bins = tile_bins()
    b = np.arange(128)
    phase = 2 * np.pi * ((b[None, :, None] * bins[:, None, :]) % NT) / NT
    cos, sin = np.cos(phase), np.sin(phase)
    table = np.zeros((QT, 2, 128, 2, 128))
    conj = np.concatenate([np.ones(64), -np.ones(64)])
    table[:, 0, :, 0] = cos
    table[:, 1, :, 0] = sin * conj
    table[:, 0, :, 1] = -sin
    table[:, 1, :, 1] = cos * conj
    table[0] = 0.0
    table[0, 0, :, 0, :64] = cos[0, :, :64]
    table[0, 0, :, 1, :64] = -sin[0, :, :64]
    table[0, 1, :, 0, 64:] = cos[0, :, 64:]
    table[0, 1, :, 1, 64:] = -sin[0, :, 64:]
    return (table.reshape(QT, 256, 256) / math.sqrt(NT)).astype(ml_dtypes.bfloat16)


def real_fft(rows):
    count = len(rows)
    if count == 2:
        return [(rows[0] + rows[1], None), (rows[0] - rows[1], None)]
    even = real_fft(rows[0::2])
    odd = real_fft(rows[1::2])
    half, quarter = count // 2, count // 4
    out = [None] * (half + 1)
    out[0] = (even[0][0] + odd[0][0], None)
    out[half] = (even[0][0] - odd[0][0], None)
    out[quarter] = (even[quarter][0], -odd[quarter][0])
    for k in range(1, quarter):
        wr, wi = math.cos(2 * math.pi * k / count), -math.sin(2 * math.pi * k / count)
        o_re, o_im = odd[k]
        e_re, e_im = even[k]
        t_re = o_re * wr - o_im * wi
        t_im = o_re * wi + o_im * wr
        out[k] = (e_re + t_re, e_im + t_im)
        out[half - k] = (e_re - t_re, t_im - e_im)
    return out


def place():
    shard = lax.axis_index("shard")
    return lax.axis_index("group"), shard // 8, (shard // 2) % 4, shard % 2


def wrap(value, size):
    return lax.rem(value, size)


def signal_some(barrier, i, guard=True):
    x, z, y, core = place()
    there = (x + i // 4) % 4
    row = (z + i % 4) % 4 * 8
    for dy in range(4):
        for dc in range(2):
            shard = row + (y + dy) % 4 * 2 + (core + dc) % 2

            def signal():
                pl.semaphore_signal(barrier, inc=1, device_id=(there, shard), device_id_type=MESH)

            if guard and dy == 0 and dc == 0:
                pl.when(i > 0)(signal)
            else:
                signal()


def first_stage(rows, y_ref, at):
    freq = real_fft(rows)
    for q in range(QT):
        second = freq[16][0] if q == 0 else freq[q][1]
        y_ref[q, at, 0:128] = freq[q][0].astype(jnp.bfloat16)
        y_ref[q, at, 128:256] = second.astype(jnp.bfloat16)


def sort_taps(fan_ref, turned_ref, taps_ref):
    blank = jnp.zeros((128 - TAPS, 128), jnp.float32)

    @pl.loop(0, QT)
    def _(j):
        at = pl.ds(pl.multiple_of(j * 128, 128), 128)
        turned_ref[at, :] = jnp.concatenate([fan_ref[:, at], blank], axis=0).T

    @pl.loop(0, QT)
    def _(q):
        high = jnp.where(q == 0, 16, 32 - q)
        both = jnp.concatenate(
            [turned_ref[pl.ds(q, 64, stride=32), :], turned_ref[pl.ds(high, 64, stride=32), :]], axis=0
        )
        taps_ref[q] = both.T[:40]


def lag_tables(coarse_ref, fine_ref):
    lag = lax.broadcasted_iota(jnp.int32, (64, NLAG), 1) - NLAG // 2
    row = lax.broadcasted_iota(jnp.int32, (64, NLAG), 0)
    fine = ((32 * row * lag) & (NT - 1)).astype(jnp.float32) * (2.0 * math.pi / NT)
    coarse = ((row * lag) & (NT - 1)).astype(jnp.float32) * (2.0 * math.pi / NT)
    fine_ref[0] = jnp.cos(fine)
    fine_ref[1] = jnp.sin(fine)
    coarse_ref[0] = jnp.cos(coarse[:32])
    coarse_ref[1] = jnp.sin(coarse[:32])


def lag_rows(q, coarse_ref, fine_ref, lags_ref):
    cos_b, sin_b = fine_ref[0], fine_ref[1]
    for half, residue in ((0, q), (64, jnp.where(q == 0, 16, 32 - q))):
        cos_a, sin_a = coarse_ref[0, pl.ds(residue, 1), :], coarse_ref[1, pl.ds(residue, 1), :]
        lags_ref[q, half : half + 64] = (cos_a * cos_b - sin_a * sin_b).astype(jnp.bfloat16)
        lags_ref[q, 128 + half : 192 + half] = (-(sin_a * cos_b + cos_a * sin_b)).astype(jnp.bfloat16)


def pick_rows(planes, pairs_ref, pick_ref):
    block = lax.broadcasted_iota(jnp.int32, (128, 128), 0)
    for side in range(2):
        for n, plane in enumerate(planes):
            at = pl.ds(pl.multiple_of(plane * 128, 128), 128)
            chosen = block == pairs_ref[side : side + 1, at]
            pick_ref[side, n * 128 : n * 128 + 128, :] = jnp.where(chosen, 1.0, 0.0).T.astype(jnp.bfloat16)


def bin_rows(offset, rows_ref):
    lane = lax.broadcasted_iota(jnp.int32, (QT, 128), 1)
    tile = lax.broadcasted_iota(jnp.int32, (QT, 128), 0)
    residue = jnp.where(lane < 64, tile, jnp.where(tile == 0, 16, 32 - tile))
    bins = residue + 32 * (lane & 63)
    theta = ((bins * offset) & (NT - 1)).astype(jnp.float32) * (2.0 * math.pi / NT)
    rows_ref[0] = jnp.cos(theta)
    rows_ref[1] = jnp.sin(theta)
    count = jnp.minimum(bins + 64, NB - 1) - jnp.maximum(bins - 64, 0) + 1
    rows_ref[2] = 1.0 / count.astype(jnp.float32)


def copy_to(src, dst, send_sem, recv_sem, device):
    return pltpu.make_async_remote_copy(
        src_ref=src, dst_ref=dst, send_sem=send_sem, recv_sem=recv_sem, device_id=device, device_id_type=MESH
    )


def channel_of(x, z, y, core):
    return wrap(x + z + y, 2) * 32 + (x * 16 + z * 4 + y) // 2 + 64 * core


def kernel(
    pairs_hbm, offsets_hbm, valid_hbm, x_hbm, fan_hbm, table_hbm, out_ref,
    pairs_ref, offsets_ref, valid_ref, x_ref, fan_ref, table_ref,
    halo_ref, y_ref, y_halo_ref, spec_ref, turned_ref, taps_ref, filt_ref, upto_ref, run_ref, rows_ref,
    rows32_ref, white_ref, blocks_ref, own_ref, other_ref, pick_ref, cross_ref, sums_ref,
    parts_ref, recv_ref, lags_ref, coarse_ref, fine_ref,
    fetch_sem, halo_send, halo_recv, block_send, block_recv, swap_send, swap_recv, part_send, part_recv,
):
    x, z, y, core = place()
    me = lax.axis_index("group") * 32 + lax.axis_index("shard")
    barrier = pltpu.get_barrier_semaphore()
    moves = (
        (x_hbm, x_ref), (offsets_hbm, offsets_ref), (fan_hbm, fan_ref),
        (pairs_hbm, pairs_ref), (valid_hbm, valid_ref), (table_hbm, table_ref),
    )
    fetches = [pltpu.make_async_copy(src, dst, fetch_sem.at[n]) for n, (src, dst) in enumerate(moves)]
    for fetch in fetches:
        fetch.start()

    @pl.loop(0, 8)
    def _(column):
        signal_some(barrier, column)

    fetches[0].wait()

    @pl.loop(0, 8)
    def _(chunk):
        signal_some(barrier, chunk + 8, False)
        at = pl.ds(pl.multiple_of(chunk * 16, 16), 16)
        first_stage([x_ref[at, a * 128 : (a + 1) * 128].astype(jnp.float32) for a in range(32)], y_ref, at)

    for fetch in fetches[1:]:
        fetch.wait()
    sort_taps(fan_ref, turned_ref, taps_ref)
    bin_rows(offsets_ref[me], rows_ref)

    @pl.loop(0, QT // 4)
    def _(group):
        for n in range(4):
            q = group * 4 + n
            both = jnp.dot(y_ref[q], table_ref[q], preferred_element_type=jnp.float32)
            spec_ref[q, 0, HALF : HALF + BLK] = both[:, :128]
            spec_ref[q, 1, HALF : HALF + BLK] = both[:, 128:]

    pl.semaphore_wait(barrier, NDEV - 1)
    after, before = wrap(me + 1, NDEV), wrap(me + NDEV - 1, NDEV)
    to_after = copy_to(
        x_ref.at[pl.ds(BLK - HALF, HALF)], halo_ref.at[0], halo_send.at[0], halo_recv.at[0],
        (after // 32, wrap(after, 32)),
    )
    to_before = copy_to(
        x_ref.at[pl.ds(0, HALF)], halo_ref.at[1], halo_send.at[1], halo_recv.at[1],
        (before // 32, wrap(before, 32)),
    )
    to_after.start()
    to_before.start()

    def take_halo():
        to_after.wait()
        to_before.wait()

        @pl.loop(0, 2, unroll=2)
        def _(side):
            edge = jnp.where(side == 0, me > 0, me < NDEV - 1).astype(jnp.float32)
            to = pl.ds(pl.multiple_of(side * HALF, HALF), HALF)
            first_stage(
                [halo_ref[side, :, a * 128 : (a + 1) * 128].astype(jnp.float32) * edge for a in range(32)],
                y_halo_ref,
                to,
            )

        @pl.loop(0, QT // 4, unroll=2)
        def _(group):
            for n in range(4):
                q = group * 4 + n
                both = jnp.dot(y_halo_ref[q], table_ref[q], preferred_element_type=jnp.float32)
                for r in range(2):
                    spec_ref[q, r, 0:HALF] = both[:HALF, r * 128 : r * 128 + 128]
                    spec_ref[q, r, HALF + BLK : WIDE] = both[HALF:, r * 128 : r * 128 + 128]

    lanes = lax.broadcasted_iota(jnp.int32, (CHUNK, 128), 1)
    low = lanes < 64
    k2 = lanes & 63
    sign = 1 - 2 * core
    mine = channel_of(x, z, y, core)
    somewhere = (x, lax.axis_index("shard") + 1 - 2 * core)
    others = pl.ds(0, NDEV - 1)
    xs = [wrap(x + 4 + sign * n, 4) for n in range(4)]
    zs = [wrap(z + 4 + sign * n, 4) for n in range(4)]
    ys = [wrap(y // 2 + n, 2) for n in range(2)]

    @pl.loop(0, 4)
    def _(turn):
        pl.when(turn == 2)(take_halo)
        ahead = jnp.where(turn < 2, 1 + turn, 3 * turn - 6)
        chunk = jnp.where(core == 0, ahead, 3 - ahead)
        first = pl.multiple_of(chunk * CHUNK, CHUNK)

        def fan(q, run):
            re = jnp.zeros((CHUNK, 128), jnp.float32)
            im = re
            for t in range(TAPS):
                tap = taps_ref[q, t : t + 1, :]
                re = re + tap * spec_ref[q, 0, pl.ds(first + t, CHUNK), :]
                im = im + tap * spec_ref[q, 1, pl.ds(first + t, CHUNK), :]
            filt_ref[q, 0] = re
            filt_ref[q, 1] = im
            run = run + jnp.where(low | (q > 0), re * re + im * im, 0.0)
            upto_ref[q] = run
            return run

        run = lax.fori_loop(0, QT, fan, jnp.zeros((CHUNK, 128), jnp.float32), unroll=2)

        power = filt_ref[0, 0] * filt_ref[0, 0] + filt_ref[0, 1] * filt_ref[0, 1]
        sums = run + jnp.where(low, 0.0, power)
        swapped = pltpu.roll(sums, 64, 1)
        total = sums + swapped
        run_ref[1] = total
        run_ref[2] = (
            total
            + jnp.where(k2 >= 1, pltpu.roll(total, 1, 1), 0.0)
            + jnp.where(k2 <= 62, pltpu.roll(total, 127, 1), 0.0)
        )
        run_ref[3] = jnp.where(low, power, sums)
        run_ref[4] = jnp.where(low, total, swapped + power)

        @pl.loop(0, QT, unroll=8)
        def _(q):
            re, im = filt_ref[q, 0], filt_ref[q, 1]
            upto = jnp.where(q == 0, run_ref[3], upto_ref[q])
            rest = jnp.where(q == 0, run_ref[4], jnp.maximum(run_ref[1] - upto_ref[jnp.maximum(q - 1, 0)], 0.0))
            prefix = jnp.where(low, upto, rest)
            suffix = jnp.where(low, rest, upto)
            window = (
                run_ref[2]
                + jnp.where(k2 >= 2, pltpu.roll(suffix, 2, 1), 0.0)
                + jnp.where(k2 <= 61, pltpu.roll(prefix, 126, 1), 0.0)
            )
            scale = lax.rsqrt(window * rows_ref[2, pl.ds(q, 1), :] + EPSILON)
            cos = rows_ref[0, pl.ds(q, 1), :]
            sin = rows_ref[1, pl.ds(q, 1), :]
            rows32_ref[pl.ds(q, CHUNK, stride=33), :] = (re * cos + im * sin) * scale
            rows32_ref[pl.ds(16 + q, CHUNK, stride=33), :] = (im * cos - re * sin) * scale

        to_core, parity = chunk // 2, wrap(chunk, 2)
        for n in range(32):
            to_x, to_z, to_y2 = xs[n % 4], zs[(n // 4 + n) % 4], ys[n // 16]
            shard = to_z * 8 + to_y2 * 4 + 2 * wrap(parity + to_x + to_z, 2) + to_core
            row = to_x * 8 + to_z * 2 + to_y2
            white_ref[first + row] = rows32_ref[pl.ds(row * 33, 32), :].astype(jnp.bfloat16)
            push = copy_to(
                white_ref.at[first + row], blocks_ref.at[me], block_send, block_recv, (to_x, shard)
            ).start
            if n == 0:
                pl.when(first + row != mine)(push)
            else:
                push()

    blocks_ref[me] = white_ref[mine]

    lag_tables(coarse_ref, fine_ref)
    pick_rows(xs, pairs_ref, pick_ref)

    @pl.loop(0, QT)
    def _(q):
        lag_rows(q, coarse_ref, fine_ref, lags_ref)

    copy_to(white_ref.at[others], blocks_ref.at[others], block_send, block_recv, somewhere).wait()

    @pl.loop(0, NDEV // 8, unroll=2)
    def _(d):
        for n in range(8):
            rows32_ref[pl.ds((d * 8 + n) * 33, 32), :] = blocks_ref[d * 8 + n].astype(jnp.float32)

    def swap(part):
        some = pl.ds(part * 4, 4)
        return copy_to(own_ref.at[some], other_ref.at[some], swap_send.at[part], swap_recv.at[part], somewhere)

    @pl.loop(0, 4)
    def _(part):
        for n in range(4):
            q = part * 4 + n
            own_ref[q, :, 0:128] = rows32_ref[pl.ds(q, BLK, stride=33), :].astype(jnp.bfloat16)
            own_ref[q, :, 128:256] = rows32_ref[pl.ds(16 + q, BLK, stride=33), :].astype(jnp.bfloat16)
        swap(part).start()

    def add_part(part, half):
        rows = pl.ds(pl.multiple_of(half * 256, 256), 256)
        for n in range(4):
            q = part * 4 + n
            left = jnp.dot(pick_ref[0, rows, :], own_ref[q], preferred_element_type=jnp.float32)
            right = jnp.dot(pick_ref[1, rows, :], other_ref[q], preferred_element_type=jnp.float32)
            l_re, l_im, r_re, r_im = left[:, :128], left[:, 128:], right[:, :128], right[:, 128:]
            cross_ref[:, n * 256 : n * 256 + 128] = (l_re * r_re + l_im * r_im).astype(jnp.bfloat16)
            cross_ref[:, n * 256 + 128 : n * 256 + 256] = (l_im * r_re - l_re * r_im).astype(jnp.bfloat16)
        lags = lags_ref[pl.ds(part * 4, 4)].reshape(1024, NLAG)
        return jnp.dot(cross_ref[...], lags, preferred_element_type=jnp.float32)

    @pl.loop(0, 2)
    def _(turn):
        @pl.loop(0, 4)
        def _(part):
            pl.when(turn == 0)(lambda: swap(part).wait())
            added = add_part(part, turn)
            sums_ref[...] = jnp.where(part == 0, added, sums_ref[...] + added)

        for n in range(4):
            rows32_ref[pl.ds(n, 256, stride=4), :] = sums_ref[:, n * 128 : n * 128 + 128]

        planes = [wrap(x + 4 + sign * (2 * turn + n), 4) for n in range(2)]

        @pl.loop(0, 4, unroll=2)
        def _(i):
            for n in range(16):
                to_core = core if n < 8 else 1 - core
                shard = zs[n // 2 % 4] * 8 + wrap(y + i + n, 4) * 2 + to_core
                row = n % 2 * 32 + shard
                slot = turn * 64 + row
                parts_ref[slot] = rows32_ref[pl.ds(pl.multiple_of(row * 16, 16), 16), :].astype(jnp.bfloat16)
                push = copy_to(
                    parts_ref.at[slot], recv_ref.at[mine], part_send, part_recv, (planes[n % 2], shard)
                ).start
                if n == 0:
                    pl.when(turn + i > 0)(push)
                else:
                    push()

    recv_ref[mine] = parts_ref[lax.axis_index("shard")]
    copy_to(parts_ref.at[others], recv_ref.at[others], part_send, part_recv, somewhere).wait()

    @pl.loop(0, NDEV // 16)
    def _(d):
        for n in range(16):
            rows32_ref[pl.ds((d * 16 + n) * 17, 16), :] = recv_ref[d * 16 + n].astype(jnp.float32)

    for p in range(4):
        weight = valid_ref[p].astype(jnp.float32) * (1.0 / math.sqrt(NB))
        for n in range(4):
            out_ref[p, :, n * 128 : n * 128 + 128] = rows32_ref[pl.ds(p * 4 + n, BLK, stride=17), :] * weight


def correlate(*operands):
    f32, bf16, i32 = jnp.float32, jnp.bfloat16, jnp.int32
    return pl.pallas_call(
        kernel,
        out_shape=jax.ShapeDtypeStruct((4, BLK, NLAG), f32),
        in_specs=[pl.BlockSpec(memory_space=pltpu.HBM)] * 6,
        out_specs=pl.BlockSpec(memory_space=pltpu.VMEM),
        scratch_shapes=[
            pltpu.VMEM((2, PAIRS), i32),
            pltpu.SMEM((NDEV,), i32),
            pltpu.SMEM((4,), i32),
            pltpu.VMEM((BLK, NT), bf16),
            pltpu.VMEM((TAPS, NB), f32),
            pltpu.VMEM((QT, 256, 256), bf16),
            pltpu.VMEM((2, HALF, NT), bf16),
            pltpu.VMEM((QT, BLK, 256), bf16),
            pltpu.VMEM((QT, 2 * HALF, 256), bf16),
            pltpu.VMEM((QT, 2, WIDE, 128), f32),
            pltpu.VMEM((NB + 64, 128), f32),
            pltpu.VMEM((QT, 40, 128), f32),
            pltpu.VMEM((QT, 2, CHUNK, 128), f32),
            pltpu.VMEM((QT, CHUNK, 128), f32),
            pltpu.VMEM((5, CHUNK, 128), f32),
            pltpu.VMEM((3, QT, 128), f32),
            pltpu.VMEM((33 * BLK + 64, 128), f32),
            pltpu.VMEM((NDEV, 32, 128), bf16),
            pltpu.VMEM((NDEV, 32, 128), bf16),
            pltpu.VMEM((QT, NDEV, 256), bf16),
            pltpu.VMEM((QT, NDEV, 256), bf16),
            pltpu.VMEM((2, PAIRS, NDEV), bf16),
            pltpu.VMEM((256, 1024), bf16),
            pltpu.VMEM((PAIRS // 2, NLAG), f32),
            pltpu.VMEM((NDEV, 16, 128), bf16),
            pltpu.VMEM((NDEV, 16, 128), bf16),
            pltpu.VMEM((QT, 256, NLAG), bf16),
            pltpu.VMEM((2, 32, NLAG), f32),
            pltpu.VMEM((2, 64, NLAG), f32),
            pltpu.SemaphoreType.DMA((6,)),
            pltpu.SemaphoreType.DMA((2,)),
            pltpu.SemaphoreType.DMA((2,)),
            pltpu.SemaphoreType.DMA,
            pltpu.SemaphoreType.DMA,
            pltpu.SemaphoreType.DMA((4,)),
            pltpu.SemaphoreType.DMA((4,)),
            pltpu.SemaphoreType.DMA,
            pltpu.SemaphoreType.DMA,
        ],
        compiler_params=pltpu.CompilerParams(collective_id=0, has_side_effects=True, vmem_limit_bytes=48 << 20),
        name="correlate",
    )(*operands)


def body(samples, fan_taps, pair_blocks, pair_valid, coil_offsets):
    table = jnp.asarray(second_stage_table())
    operands = (pair_blocks.T, coil_offsets, pair_valid, samples.reshape(BLK, NT), fan_taps, table)
    return correlate(*(pltpu.with_memory_space_constraint(operand, pltpu.HBM) for operand in operands))


def solution(mesh):
    return jax.shard_map(
        body,
        mesh=mesh,
        in_specs=(P(AXES, None, None), P(), P(), P(AXES), P()),
        out_specs=P(AXES, None, None),
        check_vma=False,
    )
```

```python
import math

import jax
import jax.numpy as jnp
import ml_dtypes
import numpy as np
from jax import lax
from jax.experimental import pallas as pl
from jax.experimental.pallas import tpu as pltpu
from jax.sharding import PartitionSpec as P

HALF = 16
NLAG = 512
NT = 4096
NB = 2048
BLK = 128
WIDE = BLK + 2 * HALF
EPSILON = 1e-05
AXES = ("group", "shard")
NDEV = 128
PAIRS = 512
CHUNK = 32
MESH = pl.DeviceIdType.MESH
TAPS = 2 * HALF + 1
QT = 16


def residues():
    low = np.arange(QT)
    high = np.where(low == 0, 16, 32 - low)
    return low, high


def tile_bins():
    low, high = residues()
    k2 = np.arange(64)
    return np.concatenate([low[:, None] + 32 * k2, high[:, None] + 32 * k2], axis=1)


def second_stage_table():
    bins = tile_bins()
    b = np.arange(128)
    phase = 2 * np.pi * ((b[None, :, None] * bins[:, None, :]) % NT) / NT
    cos, sin = np.cos(phase), np.sin(phase)
    table = np.zeros((QT, 2, 128, 2, 128))
    conj = np.concatenate([np.ones(64), -np.ones(64)])
    table[:, 0, :, 0] = cos
    table[:, 1, :, 0] = sin * conj
    table[:, 0, :, 1] = -sin
    table[:, 1, :, 1] = cos * conj
    table[0] = 0.0
    table[0, 0, :, 0, :64] = cos[0, :, :64]
    table[0, 0, :, 1, :64] = -sin[0, :, :64]
    table[0, 1, :, 0, 64:] = cos[0, :, 64:]
    table[0, 1, :, 1, 64:] = -sin[0, :, 64:]
    return (table.reshape(QT, 256, 256) / math.sqrt(NT)).astype(ml_dtypes.bfloat16)


def real_fft(rows):
    count = len(rows)
    if count == 2:
        return [(rows[0] + rows[1], None), (rows[0] - rows[1], None)]
    even = real_fft(rows[0::2])
    odd = real_fft(rows[1::2])
    half, quarter = count // 2, count // 4
    out = [None] * (half + 1)
    out[0] = (even[0][0] + odd[0][0], None)
    out[half] = (even[0][0] - odd[0][0], None)
    out[quarter] = (even[quarter][0], -odd[quarter][0])
    for k in range(1, quarter):
        wr, wi = math.cos(2 * math.pi * k / count), -math.sin(2 * math.pi * k / count)
        o_re, o_im = odd[k]
        e_re, e_im = even[k]
        t_re = o_re * wr - o_im * wi
        t_im = o_re * wi + o_im * wr
        out[k] = (e_re + t_re, e_im + t_im)
        out[half - k] = (e_re - t_re, t_im - e_im)
    return out


def place():
    shard = lax.axis_index("shard")
    return lax.axis_index("group"), shard // 8, (shard // 2) % 4, shard % 2


def wrap(value, size):
    return lax.rem(value, size)


def signal_some(barrier, i, guard=True):
    x, z, y, core = place()
    there = (x + i // 4) % 4
    row = (z + i % 4) % 4 * 8
    for dy in range(4):
        for dc in range(2):
            shard = row + (y + dy) % 4 * 2 + (core + dc) % 2

            def signal():
                pl.semaphore_signal(barrier, inc=1, device_id=(there, shard), device_id_type=MESH)

            if guard and dy == 0 and dc == 0:
                pl.when(i > 0)(signal)
            else:
                signal()


def first_stage(rows, y_ref, at):
    freq = real_fft(rows)
    for q in range(QT):
        second = freq[16][0] if q == 0 else freq[q][1]
        y_ref[q, at, 0:128] = freq[q][0].astype(jnp.bfloat16)
        y_ref[q, at, 128:256] = second.astype(jnp.bfloat16)


def sort_taps(fan_ref, turned_ref, taps_ref):
    blank = jnp.zeros((128 - TAPS, 128), jnp.float32)

    @pl.loop(0, QT)
    def _(j):
        at = pl.ds(pl.multiple_of(j * 128, 128), 128)
        turned_ref[at, :] = jnp.concatenate([fan_ref[:, at], blank], axis=0).T

    @pl.loop(0, QT)
    def _(q):
        high = jnp.where(q == 0, 16, 32 - q)
        both = jnp.concatenate(
            [turned_ref[pl.ds(q, 64, stride=32), :], turned_ref[pl.ds(high, 64, stride=32), :]], axis=0
        )
        taps_ref[q] = both.T[:40]


def lag_tables(coarse_ref, fine_ref):
    lag = lax.broadcasted_iota(jnp.int32, (64, NLAG), 1) - NLAG // 2
    row = lax.broadcasted_iota(jnp.int32, (64, NLAG), 0)
    fine = ((32 * row * lag) & (NT - 1)).astype(jnp.float32) * (2.0 * math.pi / NT)
    coarse = ((row * lag) & (NT - 1)).astype(jnp.float32) * (2.0 * math.pi / NT)
    fine_ref[0] = jnp.cos(fine)
    fine_ref[1] = jnp.sin(fine)
    coarse_ref[0] = jnp.cos(coarse[:32])
    coarse_ref[1] = jnp.sin(coarse[:32])


def lag_rows(q, coarse_ref, fine_ref, lags_ref):
    cos_b, sin_b = fine_ref[0], fine_ref[1]
    for half, residue in ((0, q), (64, jnp.where(q == 0, 16, 32 - q))):
        cos_a, sin_a = coarse_ref[0, pl.ds(residue, 1), :], coarse_ref[1, pl.ds(residue, 1), :]
        lags_ref[q, half : half + 64] = (cos_a * cos_b - sin_a * sin_b).astype(jnp.bfloat16)
        lags_ref[q, 128 + half : 192 + half] = (-(sin_a * cos_b + cos_a * sin_b)).astype(jnp.bfloat16)


def pick_rows(planes, pairs_ref, pick_ref):
    block = lax.broadcasted_iota(jnp.int32, (128, 128), 0)
    for side in range(2):
        for n, plane in enumerate(planes):
            at = pl.ds(pl.multiple_of(plane * 128, 128), 128)
            chosen = block == pairs_ref[side : side + 1, at]
            pick_ref[side, n * 128 : n * 128 + 128, :] = jnp.where(chosen, 1.0, 0.0).T.astype(jnp.bfloat16)


def bin_rows(offset, rows_ref):
    lane = lax.broadcasted_iota(jnp.int32, (QT, 128), 1)
    tile = lax.broadcasted_iota(jnp.int32, (QT, 128), 0)
    residue = jnp.where(lane < 64, tile, jnp.where(tile == 0, 16, 32 - tile))
    bins = residue + 32 * (lane & 63)
    theta = ((bins * offset) & (NT - 1)).astype(jnp.float32) * (2.0 * math.pi / NT)
    rows_ref[0] = jnp.cos(theta)
    rows_ref[1] = jnp.sin(theta)
    count = jnp.minimum(bins + 64, NB - 1) - jnp.maximum(bins - 64, 0) + 1
    rows_ref[2] = 1.0 / count.astype(jnp.float32)


def copy_to(src, dst, send_sem, recv_sem, device):
    return pltpu.make_async_remote_copy(
        src_ref=src, dst_ref=dst, send_sem=send_sem, recv_sem=recv_sem, device_id=device, device_id_type=MESH
    )


def channel_of(x, z, y, core):
    return wrap(x + z + y, 2) * 32 + (x * 16 + z * 4 + y) // 2 + 64 * core


def kernel(
    pairs_hbm, offsets_hbm, valid_hbm, x_hbm, fan_hbm, table_hbm, out_ref,
    pairs_ref, offsets_ref, valid_ref, x_ref, fan_ref, table_ref,
    halo_ref, y_ref, y_halo_ref, spec_ref, turned_ref, taps_ref, filt_ref, upto_ref, run_ref, rows_ref,
    rows32_ref, white_ref, blocks_ref, own_ref, other_ref, pick_ref, cross_ref, sums_ref,
    parts_ref, recv_ref, lags_ref, coarse_ref, fine_ref,
    fetch_sem, halo_send, halo_recv, block_send, block_recv, swap_send, swap_recv, part_send, part_recv,
):
    x, z, y, core = place()
    me = lax.axis_index("group") * 32 + lax.axis_index("shard")
    barrier = pltpu.get_barrier_semaphore()
    moves = (
        (x_hbm, x_ref), (offsets_hbm, offsets_ref), (fan_hbm, fan_ref),
        (pairs_hbm, pairs_ref), (valid_hbm, valid_ref), (table_hbm, table_ref),
    )
    fetches = [pltpu.make_async_copy(src, dst, fetch_sem.at[n]) for n, (src, dst) in enumerate(moves)]
    for fetch in fetches:
        fetch.start()

    @pl.loop(0, 8)
    def _(column):
        signal_some(barrier, column)

    fetches[0].wait()

    @pl.loop(0, 8)
    def _(chunk):
        signal_some(barrier, chunk + 8, False)
        at = pl.ds(pl.multiple_of(chunk * 16, 16), 16)
        first_stage([x_ref[at, a * 128 : (a + 1) * 128].astype(jnp.float32) for a in range(32)], y_ref, at)

    for fetch in fetches[1:]:
        fetch.wait()
    sort_taps(fan_ref, turned_ref, taps_ref)
    bin_rows(offsets_ref[me], rows_ref)

    @pl.loop(0, QT // 4)
    def _(group):
        for n in range(4):
            q = group * 4 + n
            both = jnp.dot(y_ref[q], table_ref[q], preferred_element_type=jnp.float32)
            spec_ref[q, 0, HALF : HALF + BLK] = both[:, :128]
            spec_ref[q, 1, HALF : HALF + BLK] = both[:, 128:]

    pl.semaphore_wait(barrier, NDEV - 1)
    after, before = wrap(me + 1, NDEV), wrap(me + NDEV - 1, NDEV)
    to_after = copy_to(
        x_ref.at[pl.ds(BLK - HALF, HALF)], halo_ref.at[0], halo_send.at[0], halo_recv.at[0],
        (after // 32, wrap(after, 32)),
    )
    to_before = copy_to(
        x_ref.at[pl.ds(0, HALF)], halo_ref.at[1], halo_send.at[1], halo_recv.at[1],
        (before // 32, wrap(before, 32)),
    )
    to_after.start()
    to_before.start()

    def take_halo():
        to_after.wait()
        to_before.wait()

        @pl.loop(0, 2)
        def _(side):
            edge = jnp.where(side == 0, me > 0, me < NDEV - 1).astype(jnp.float32)
            to = pl.ds(pl.multiple_of(side * HALF, HALF), HALF)
            first_stage(
                [halo_ref[side, :, a * 128 : (a + 1) * 128].astype(jnp.float32) * edge for a in range(32)],
                y_halo_ref,
                to,
            )

        @pl.loop(0, QT // 4)
        def _(group):
            for n in range(4):
                q = group * 4 + n
                both = jnp.dot(y_halo_ref[q], table_ref[q], preferred_element_type=jnp.float32)
                for r in range(2):
                    spec_ref[q, r, 0:HALF] = both[:HALF, r * 128 : r * 128 + 128]
                    spec_ref[q, r, HALF + BLK : WIDE] = both[HALF:, r * 128 : r * 128 + 128]

    lanes = lax.broadcasted_iota(jnp.int32, (CHUNK, 128), 1)
    low = lanes < 64
    k2 = lanes & 63
    sign = 1 - 2 * core
    mine = channel_of(x, z, y, core)
    somewhere = (x, lax.axis_index("shard") + 1 - 2 * core)
    others = pl.ds(0, NDEV - 1)
    xs = [wrap(x + 4 + sign * n, 4) for n in range(4)]
    zs = [wrap(z + 4 + sign * n, 4) for n in range(4)]
    ys = [wrap(y // 2 + n, 2) for n in range(2)]

    @pl.loop(0, 4)
    def _(turn):
        pl.when(turn == 2)(take_halo)
        ahead = jnp.where(turn < 2, 1 + turn, 3 * turn - 6)
        chunk = jnp.where(core == 0, ahead, 3 - ahead)
        first = pl.multiple_of(chunk * CHUNK, CHUNK)

        def fan(q, run):
            re = jnp.zeros((CHUNK, 128), jnp.float32)
            im = re
            for t in range(TAPS):
                tap = taps_ref[q, t : t + 1, :]
                re = re + tap * spec_ref[q, 0, pl.ds(first + t, CHUNK), :]
                im = im + tap * spec_ref[q, 1, pl.ds(first + t, CHUNK), :]
            filt_ref[q, 0] = re
            filt_ref[q, 1] = im
            run = run + jnp.where(low | (q > 0), re * re + im * im, 0.0)
            upto_ref[q] = run
            return run

        run = lax.fori_loop(0, QT, fan, jnp.zeros((CHUNK, 128), jnp.float32), unroll=2)

        power = filt_ref[0, 0] * filt_ref[0, 0] + filt_ref[0, 1] * filt_ref[0, 1]
        sums = run + jnp.where(low, 0.0, power)
        swapped = pltpu.roll(sums, 64, 1)
        total = sums + swapped
        run_ref[1] = total
        run_ref[2] = (
            total
            + jnp.where(k2 >= 1, pltpu.roll(total, 1, 1), 0.0)
            + jnp.where(k2 <= 62, pltpu.roll(total, 127, 1), 0.0)
        )
        run_ref[3] = jnp.where(low, power, sums)
        run_ref[4] = jnp.where(low, total, swapped + power)

        @pl.loop(0, QT, unroll=8)
        def _(q):
            re, im = filt_ref[q, 0], filt_ref[q, 1]
            upto = jnp.where(q == 0, run_ref[3], upto_ref[q])
            rest = jnp.where(q == 0, run_ref[4], jnp.maximum(run_ref[1] - upto_ref[jnp.maximum(q - 1, 0)], 0.0))
            prefix = jnp.where(low, upto, rest)
            suffix = jnp.where(low, rest, upto)
            window = (
                run_ref[2]
                + jnp.where(k2 >= 2, pltpu.roll(suffix, 2, 1), 0.0)
                + jnp.where(k2 <= 61, pltpu.roll(prefix, 126, 1), 0.0)
            )
            scale = lax.rsqrt(window * rows_ref[2, pl.ds(q, 1), :] + EPSILON)
            cos = rows_ref[0, pl.ds(q, 1), :]
            sin = rows_ref[1, pl.ds(q, 1), :]
            rows32_ref[pl.ds(q, CHUNK, stride=33), :] = (re * cos + im * sin) * scale
            rows32_ref[pl.ds(16 + q, CHUNK, stride=33), :] = (im * cos - re * sin) * scale

        to_core, parity = chunk // 2, wrap(chunk, 2)
        for n in range(32):
            to_x, to_z, to_y2 = xs[n % 4], zs[(n // 4 + n) % 4], ys[n // 16]
            shard = to_z * 8 + to_y2 * 4 + 2 * wrap(parity + to_x + to_z, 2) + to_core
            row = to_x * 8 + to_z * 2 + to_y2
            white_ref[first + row] = rows32_ref[pl.ds(row * 33, 32), :].astype(jnp.bfloat16)
            push = copy_to(
                white_ref.at[first + row], blocks_ref.at[me], block_send, block_recv, (to_x, shard)
            ).start
            if n == 0:
                pl.when(first + row != mine)(push)
            else:
                push()

    blocks_ref[me] = white_ref[mine]

    lag_tables(coarse_ref, fine_ref)
    pick_rows(xs, pairs_ref, pick_ref)

    @pl.loop(0, QT)
    def _(q):
        lag_rows(q, coarse_ref, fine_ref, lags_ref)

    copy_to(white_ref.at[others], blocks_ref.at[others], block_send, block_recv, somewhere).wait()

    @pl.loop(0, NDEV // 8, unroll=2)
    def _(d):
        for n in range(8):
            rows32_ref[pl.ds((d * 8 + n) * 33, 32), :] = blocks_ref[d * 8 + n].astype(jnp.float32)

    def swap(part):
        some = pl.ds(part * 4, 4)
        return copy_to(own_ref.at[some], other_ref.at[some], swap_send.at[part], swap_recv.at[part], somewhere)

    @pl.loop(0, 4, unroll=2)
    def _(part):
        for n in range(4):
            q = part * 4 + n
            own_ref[q, :, 0:128] = rows32_ref[pl.ds(q, BLK, stride=33), :].astype(jnp.bfloat16)
            own_ref[q, :, 128:256] = rows32_ref[pl.ds(16 + q, BLK, stride=33), :].astype(jnp.bfloat16)
        swap(part).start()

    def add_part(part, half):
        rows = pl.ds(pl.multiple_of(half * 256, 256), 256)
        for n in range(4):
            q = part * 4 + n
            left = jnp.dot(pick_ref[0, rows, :], own_ref[q], preferred_element_type=jnp.float32)
            right = jnp.dot(pick_ref[1, rows, :], other_ref[q], preferred_element_type=jnp.float32)
            l_re, l_im, r_re, r_im = left[:, :128], left[:, 128:], right[:, :128], right[:, 128:]
            cross_ref[:, n * 256 : n * 256 + 128] = (l_re * r_re + l_im * r_im).astype(jnp.bfloat16)
            cross_ref[:, n * 256 + 128 : n * 256 + 256] = (l_im * r_re - l_re * r_im).astype(jnp.bfloat16)
        lags = lags_ref[pl.ds(part * 4, 4)].reshape(1024, NLAG)
        return jnp.dot(cross_ref[...], lags, preferred_element_type=jnp.float32)

    @pl.loop(0, 2)
    def _(turn):
        @pl.loop(0, 4)
        def _(part):
            pl.when(turn == 0)(lambda: swap(part).wait())
            added = add_part(part, turn)
            sums_ref[...] = jnp.where(part == 0, added, sums_ref[...] + added)

        for n in range(4):
            rows32_ref[pl.ds(n, 256, stride=4), :] = sums_ref[:, n * 128 : n * 128 + 128]

        planes = [wrap(x + 4 + sign * (2 * turn + n), 4) for n in range(2)]

        @pl.loop(0, 4, unroll=2)
        def _(i):
            for n in range(16):
                to_core = core if n < 8 else 1 - core
                shard = zs[n // 2 % 4] * 8 + wrap(y + i + n, 4) * 2 + to_core
                row = n % 2 * 32 + shard
                slot = turn * 64 + row
                parts_ref[slot] = rows32_ref[pl.ds(pl.multiple_of(row * 16, 16), 16), :].astype(jnp.bfloat16)
                push = copy_to(
                    parts_ref.at[slot], recv_ref.at[mine], part_send, part_recv, (planes[n % 2], shard)
                ).start
                if n == 0:
                    pl.when(turn + i > 0)(push)
                else:
                    push()

    recv_ref[mine] = parts_ref[lax.axis_index("shard")]
    copy_to(parts_ref.at[others], recv_ref.at[others], part_send, part_recv, somewhere).wait()

    @pl.loop(0, NDEV // 16)
    def _(d):
        for n in range(16):
            rows32_ref[pl.ds((d * 16 + n) * 17, 16), :] = recv_ref[d * 16 + n].astype(jnp.float32)

    for p in range(4):
        weight = valid_ref[p].astype(jnp.float32) * (1.0 / math.sqrt(NB))
        for n in range(4):
            out_ref[p, :, n * 128 : n * 128 + 128] = rows32_ref[pl.ds(p * 4 + n, BLK, stride=17), :] * weight


def correlate(*operands):
    f32, bf16, i32 = jnp.float32, jnp.bfloat16, jnp.int32
    return pl.pallas_call(
        kernel,
        out_shape=jax.ShapeDtypeStruct((4, BLK, NLAG), f32),
        in_specs=[pl.BlockSpec(memory_space=pltpu.HBM)] * 6,
        out_specs=pl.BlockSpec(memory_space=pltpu.VMEM),
        scratch_shapes=[
            pltpu.VMEM((2, PAIRS), i32),
            pltpu.SMEM((NDEV,), i32),
            pltpu.SMEM((4,), i32),
            pltpu.VMEM((BLK, NT), bf16),
            pltpu.VMEM((TAPS, NB), f32),
            pltpu.VMEM((QT, 256, 256), bf16),
            pltpu.VMEM((2, HALF, NT), bf16),
            pltpu.VMEM((QT, BLK, 256), bf16),
            pltpu.VMEM((QT, 2 * HALF, 256), bf16),
            pltpu.VMEM((QT, 2, WIDE, 128), f32),
            pltpu.VMEM((NB + 64, 128), f32),
            pltpu.VMEM((QT, 40, 128), f32),
            pltpu.VMEM((QT, 2, CHUNK, 128), f32),
            pltpu.VMEM((QT, CHUNK, 128), f32),
            pltpu.VMEM((5, CHUNK, 128), f32),
            pltpu.VMEM((3, QT, 128), f32),
            pltpu.VMEM((33 * BLK + 64, 128), f32),
            pltpu.VMEM((NDEV, 32, 128), bf16),
            pltpu.VMEM((NDEV, 32, 128), bf16),
            pltpu.VMEM((QT, NDEV, 256), bf16),
            pltpu.VMEM((QT, NDEV, 256), bf16),
            pltpu.VMEM((2, PAIRS, NDEV), bf16),
            pltpu.VMEM((256, 1024), bf16),
            pltpu.VMEM((PAIRS // 2, NLAG), f32),
            pltpu.VMEM((NDEV, 16, 128), bf16),
            pltpu.VMEM((NDEV, 16, 128), bf16),
            pltpu.VMEM((QT, 256, NLAG), bf16),
            pltpu.VMEM((2, 32, NLAG), f32),
            pltpu.VMEM((2, 64, NLAG), f32),
            pltpu.SemaphoreType.DMA((6,)),
            pltpu.SemaphoreType.DMA((2,)),
            pltpu.SemaphoreType.DMA((2,)),
            pltpu.SemaphoreType.DMA,
            pltpu.SemaphoreType.DMA,
            pltpu.SemaphoreType.DMA((4,)),
            pltpu.SemaphoreType.DMA((4,)),
            pltpu.SemaphoreType.DMA,
            pltpu.SemaphoreType.DMA,
        ],
        compiler_params=pltpu.CompilerParams(collective_id=0, has_side_effects=True, vmem_limit_bytes=48 << 20),
        name="correlate",
    )(*operands)


def body(samples, fan_taps, pair_blocks, pair_valid, coil_offsets):
    table = jnp.asarray(second_stage_table())
    operands = (pair_blocks.T, coil_offsets, pair_valid, samples.reshape(BLK, NT), fan_taps, table)
    return correlate(*(pltpu.with_memory_space_constraint(operand, pltpu.HBM) for operand in operands))


def solution(mesh):
    return jax.shard_map(
        body,
        mesh=mesh,
        in_specs=(P(AXES, None, None), P(), P(), P(AXES), P()),
        out_specs=P(AXES, None, None),
        check_vma=False,
    )
```
